32 devices in a mesh: groups: 2 (over y), req: 4 (over z), head: 2 (over x), sub: 2 (over core).
Axes of the slice: x: 2, y: 2, z: 4, core: 2. Of those that a mesh axis runs over, the one named last changes fastest.
Arguments:
- q_nope: bfloat16 [2048, 8192], P(('groups', 'req', 'sub'), 'head'), parts along dimension 0, may hold values from -12 to 12
- q_rope: bfloat16 [2048, 4096], P(('groups', 'req', 'sub'), 'head'), parts along dimension 0, may hold values from -16 to 16
- new_latent: bfloat16 [2048, 512], P(('groups', 'req', 'sub')), parts along dimension 0, may hold values from -6 to 6
- new_rope: bfloat16 [2048, 64], P(('groups', 'req', 'sub')), parts along dimension 0, may hold values from -8 to 8
- pool_latent: bfloat16 [128, 128, 512], P(('groups', 'req'), None, 'sub'), parts along dimension 0, may hold values from -6 to 6
- pool_rope: bfloat16 [128, 128, 64], P(('groups', 'req')), parts along dimension 0, may hold values from -6 to 6
- w_uk: bfloat16 [512, 8192], P(None, 'head'), may hold values from -0.25 to 0.25
- w_uv: bfloat16 [512, 8192], P(None, 'head'), may hold values from -0.25 to 0.25
- block_list: int32 [8, 6], P(('groups', 'req')), parts along dimension 0, may hold values from 0 to 63, as said below
- prefix_len: int32 [8], P(('groups', 'req')), parts along dimension 0, may hold values from 192 to 768, as said below
- block_slot: int32 [128], P('groups'), parts along dimension 0, may hold values from 0 to 63, as said below
Outputs:
- attended: bfloat16 [2048, 8192], P(('groups', 'req', 'sub'), 'head'), parts along dimension 0
The draws below stay inside these ranges and needn't reach their ends.
There are 2 independent parts, one for each index of `groups`. The reference program is written for one: setup_inputs(seed, part) draws one part's arguments, and reference() takes and returns one part's arrays. A program takes and returns all parts, laid end to end along the dimension named above; an argument that names none is the same for every part. Nothing has to cross between parts.
Inputs may be any that keep to these rules, and one draw needn't show every extreme that they name: `block_list`: each row lists 6 different block ids; no row lists more than 2 blocks stored with one owner (storage positions o * 16 to o * 16 + 15), and in every draw some owner stores 2 blocks of every row. `prefix_len`: some row has the full 6 * 128 prefix tokens. `block_slot`: each storage position once.
All inputs are finite; a program needn't handle non-finite values.
Results may differ from the reference program's by a relative error of at most 0.0072.
Values may be sent and summed in bfloat16 or wider, within the bound.
No kernel may reach another device: no remote copies, remote signals or barrier semaphores. Data moves between devices by JAX's collectives and lax.ppermute only.
A program may use at most 128 MiB of HBM per device.

```python
import math
import jax
import jax.numpy as jnp
from jax import lax

HEADS = 64
NOPE = 128
ROPE = 64
VDIM = 128
LATENT = 512
BLOCK = 128
CAP = 2
POOL_DEV = 16
QUERIES = 256
PB = 6
ROWS = 4
POOL = 64


def draw_q_rope(key, part):
    kbase = jax.random.fold_in(key, 3)
    base = jnp.clip(2.0 * jax.random.normal(kbase, (ROWS * QUERIES, HEADS * ROPE), jnp.float32), -16.0, 16.0)
    return base.astype(jnp.bfloat16)


def draw_new_rope(key, part):
    kbase = jax.random.fold_in(key, 5)
    base = jnp.clip(jax.random.normal(kbase, (ROWS * QUERIES, ROPE), jnp.float32), -8.0, 8.0)
    return base.astype(jnp.bfloat16)


def draw_prefix_len(key, part):
    klen, kpick = jax.random.split(jax.random.fold_in(key, 11))
    full = PB * BLOCK
    lengths = jax.random.randint(klen, (ROWS,), full // 4, full + 1)
    pick = jax.random.randint(kpick, (), 0, ROWS)
    return lengths.at[pick].set(full).astype(jnp.int32)


def block_tables(key):
    kperm, khot, krows = jax.random.split(jax.random.fold_in(key, 23), 3)
    slots = jax.random.permutation(kperm, POOL)
    inverse = jnp.argsort(slots)
    hot = jax.random.randint(khot, (), 0, ROWS)
    rest = jnp.arange((ROWS - 1) * CAP)
    other_owner = rest // CAP
    other_owner = other_owner + (other_owner >= hot).astype(other_owner.dtype)
    other_copy = rest % CAP

    def one_row(rowkey):
        kpick, kshuf, kbase = jax.random.split(rowkey, 3)
        chosen = jax.random.permutation(kpick, (ROWS - 1) * CAP)[:PB - CAP]
        owner = jnp.concatenate([jnp.full((CAP,), hot, other_owner.dtype), other_owner[chosen]])
        copies = jnp.concatenate([jnp.arange(CAP, dtype=other_copy.dtype), other_copy[chosen]])
        shuffle = jax.random.permutation(kshuf, PB)
        owner = owner[shuffle]
        copies = copies[shuffle]
        base = jax.random.randint(kbase, (ROWS,), 0, POOL_DEV)
        local = (base[owner] + copies) % POOL_DEV
        return inverse[owner * POOL_DEV + local]
    lists = jax.vmap(one_row)(jax.random.split(krows, ROWS))
    return (lists.astype(jnp.int32), slots.astype(jnp.int32))


def draw_block_list(key, part):
    return block_tables(key)[0]


def draw_block_slot(key, part):
    return block_tables(key)[1]


def block_levels(stream_key, shape, shards, low, top_value):
    def one(dim, parts):
        heights = jax.random.uniform(jax.random.fold_in(jax.random.fold_in(stream_key, 6), dim), (parts,), jnp.float32, low / len(shards), top_value / len(shards))
        return jnp.repeat(jnp.exp(heights), shape[dim] // parts).reshape((-1,) + (1,) * (len(shape) - dim - 1))

    level = one(*shards[0])
    for cut in shards[1:]:
        level = level * one(*cut)
    return level


def normal_values(rng, extent, width, most, cuts=(), kind=jnp.bfloat16):
    result = width * jax.random.normal(rng, extent, jnp.float32)
    if cuts:
        result = result * block_levels(rng, extent, cuts, -0.22, 0.18)
    return jnp.clip(result, -most, most).astype(kind)


def setup_inputs(seed: int = 0, part: int = 0) -> dict:
    keys = jax.random.split(jax.random.key(seed), 12)
    part_splits = jax.random.split(jax.random.fold_in(keys[11], part), 12)
    q_nope = normal_values(part_splits[0], (ROWS * QUERIES, HEADS * NOPE), 2.0, 12.0, ((0, 8), (1, 2)))
    q_rope = draw_q_rope(jax.random.fold_in(jax.random.fold_in(keys[11], part), 71), part)
    new_latent = normal_values(part_splits[2], (ROWS * QUERIES, LATENT), 1.0, 6.0, ((0, 8),))
    new_rope = draw_new_rope(jax.random.fold_in(jax.random.fold_in(keys[11], part), 71), part)
    pool_latent = normal_values(part_splits[4], (POOL, BLOCK, LATENT), 1.0, 6.0, ((0, 4), (2, 2)))
    pool_rope = normal_values(part_splits[5], (POOL, BLOCK, ROPE), 1.0, 6.0, ((0, 4),))
    w_uk = normal_values(keys[6], (LATENT, HEADS * NOPE), LATENT ** -0.5, 0.25, ((1, 2),))
    w_uv = normal_values(keys[7], (LATENT, HEADS * VDIM), LATENT ** -0.5, 0.25, ((1, 2),))
    block_list = draw_block_list(jax.random.fold_in(jax.random.fold_in(keys[11], part), 71), part)
    prefix_len = draw_prefix_len(jax.random.fold_in(jax.random.fold_in(keys[11], part), 71), part)
    block_slot = draw_block_slot(jax.random.fold_in(jax.random.fold_in(keys[11], part), 71), part)
    return dict(q_nope=q_nope, q_rope=q_rope, new_latent=new_latent, new_rope=new_rope, pool_latent=pool_latent, pool_rope=pool_rope, w_uk=w_uk, w_uv=w_uv, block_list=block_list, prefix_len=prefix_len, block_slot=block_slot)


def reference(q_nope, q_rope, new_latent, new_rope, pool_latent, pool_rope, w_uk, w_uv, block_list, prefix_len, block_slot):
    scale = 1.0 / math.sqrt(NOPE + ROPE)
    prefix = PB * BLOCK
    total = prefix + QUERIES

    def one_row(row):
        physical = block_slot[block_list[row]]
        lat = pool_latent[physical].reshape(prefix, LATENT)
        rope = pool_rope[physical].reshape(prefix, ROPE)
        start = (row * QUERIES).astype(jnp.int32)
        fresh_lat = lax.dynamic_slice_in_dim(new_latent, start, QUERIES, 0)
        fresh_rope = lax.dynamic_slice_in_dim(new_rope, start, QUERIES, 0)
        key_latent = jnp.concatenate([lat, fresh_lat], axis=0)
        key_rope = jnp.concatenate([rope, fresh_rope], axis=0)
        key_nope = jnp.dot(key_latent, w_uk, preferred_element_type=jnp.float32).astype(jnp.bfloat16).reshape(total, HEADS, NOPE)
        values = jnp.dot(key_latent, w_uv, preferred_element_type=jnp.float32).astype(jnp.bfloat16).reshape(total, HEADS, VDIM)
        query_nope = lax.dynamic_slice_in_dim(q_nope, start, QUERIES, 0).reshape(QUERIES, HEADS, NOPE)
        query_rope = lax.dynamic_slice_in_dim(q_rope, start, QUERIES, 0).reshape(QUERIES, HEADS, ROPE)
        scores = jnp.einsum('qhd,khd->hqk', query_nope.astype(jnp.float32), key_nope.astype(jnp.float32))
        scores = scores + jnp.einsum('qhd,kd->hqk', query_rope.astype(jnp.float32), key_rope.astype(jnp.float32))
        scores = scores * scale
        key_pos = jnp.arange(total, dtype=jnp.int32)
        query_pos = jnp.arange(QUERIES, dtype=jnp.int32)
        visible = jnp.where(key_pos[None, :] < prefix, key_pos[None, :] < prefix_len[row], key_pos[None, :] - prefix <= query_pos[:, None])
        scores = jnp.where(visible[None], scores, jnp.float32(-1e+30))
        peak = lax.optimization_barrier(jnp.max(scores, axis=2, keepdims=True))
        expo = jnp.where(visible[None], jnp.exp(scores - peak), jnp.float32(0.0))
        weights = (expo / lax.optimization_barrier(jnp.sum(expo, axis=2, keepdims=True))).astype(jnp.bfloat16)
        out = jnp.einsum('hqk,khd->qhd', weights.astype(jnp.float32), values.astype(jnp.float32))
        return out.astype(jnp.bfloat16).reshape(QUERIES, HEADS * VDIM)
    outs = lax.map(one_row, jnp.arange(ROWS, dtype=jnp.int32))
    return outs.reshape(ROWS * QUERIES, HEADS * VDIM)
```

```python
import functools
import math

import jax
import jax.numpy as jnp
from jax import lax
from jax.experimental import pallas as pl
from jax.experimental.pallas import tpu as pltpu
from jax.sharding import PartitionSpec as P

NOPE = 128
ROPE = 64
VDIM = 128
CAP = 2
LANES = 128
HIDE = -1e30


def pack_kernel(n, blocks, pool_local, lists, slots_ref, pool_ref, rope_ref, outs, where_ref,
                index_ref, count_ref, rope_buf, lat_sem, rope_sem):
    me = lax.axis_index("req")
    sub = lax.axis_index("sub")
    block = pool_ref.shape[1]
    width = pool_ref.shape[2]
    for i in range(n * CAP):
        index_ref[i] = 0
        where_ref[i] = -1
    for i in range(n):
        count_ref[i] = 0
    for k in range(n):
        found = jnp.int32(0)
        for p in range(blocks):
            physical = slots_ref[lists[k][0, p]]
            owner = physical // pool_local
            mine = owner == me

            @pl.when(mine)
            def _():
                index_ref[k * CAP + found] = physical - owner * pool_local

            found = found + mine.astype(jnp.int32)
            if k == 0:
                shift = lax.rem(me - owner + n, n)
                earlier = count_ref[shift]
                where_ref[shift * CAP + earlier] = p
                count_ref[shift] = earlier + 1
    lat_copies = []
    rope_copies = []
    for k in range(n):
        copy = pltpu.make_async_copy(
            rope_ref.at[index_ref[k * CAP + sub]], rope_buf.at[k], rope_sem.at[k]
        )
        copy.start()
        rope_copies.append(copy)
        for c in range(CAP):
            copy = pltpu.make_async_copy(
                pool_ref.at[index_ref[k * CAP + c]],
                outs[k].at[pl.ds(c * block, block)],
                lat_sem.at[k * CAP + c],
            )
            copy.start()
            lat_copies.append(copy)
    parts = width // ROPE
    rows = block // parts
    for k in range(n):
        rope_copies[k].wait()
        piece = rope_buf[k]
        outs[k][CAP * block :, :] = jnp.concatenate(
            [piece[i * rows : (i + 1) * rows] for i in range(parts)], axis=1
        )
    for copy in lat_copies:
        copy.wait()


def pack(n, lists, block_slot, pool_latent, pool_rope):
    pool_local, block, width = pool_latent.shape
    blocks = lists[0].shape[1]
    rows = CAP * block + block * ROPE // width
    vmem = pl.BlockSpec(memory_space=pltpu.VMEM)
    smem = pl.BlockSpec(memory_space=pltpu.SMEM)

    def body(*refs):
        pack_kernel(
            n, blocks, pool_local, refs[:n], refs[n], refs[n + 1], refs[n + 2],
            refs[n + 3 : 2 * n + 3], refs[2 * n + 3], *refs[2 * n + 4 :],
        )

    out = pl.pallas_call(
        body,
        out_shape=[jax.ShapeDtypeStruct((rows, width), jnp.bfloat16)] * n
        + [jax.ShapeDtypeStruct((n * CAP,), jnp.int32)],
        in_specs=[smem] * (n + 1) + [pl.BlockSpec(memory_space=pl.ANY)] * 2,
        out_specs=[vmem] * n + [smem],
        scratch_shapes=[
            pltpu.SMEM((n * CAP,), jnp.int32),
            pltpu.SMEM((n,), jnp.int32),
            pltpu.VMEM((n, block, ROPE), jnp.bfloat16),
            pltpu.SemaphoreType.DMA((n * CAP,)),
            pltpu.SemaphoreType.DMA((n,)),
        ],
        cost_estimate=pl.CostEstimate(flops=0, bytes_accessed=4 * n * rows * width, transcendentals=0),
        name="pack",
    )(*lists, block_slot, pool_latent, pool_rope)
    return out[:n], out[n]


def attend_kernel(n, blocks, sub_ref, len_ref, where_ref, *refs):
    mine = refs[:n]
    theirs = refs[n : 2 * n]
    (lat_a, rope_a, lat_b, rope_b, qn_a, qr_a, qn_b, qr_b, wk_ref, wv_ref,
     out_ref, send_ref, lat, tails, bias) = refs[2 * n :]
    sub = sub_ref[0]
    block = lat_a.shape[0]
    width = mine[0].shape[1]
    prefix = blocks * block
    queries = 2 * block

    @pl.when(pl.program_id(0) == 0)
    def _():
        parts = width // ROPE
        rows = block // parts
        lane = lax.broadcasted_iota(jnp.int32, (block, ROPE), 1)
        row = lax.broadcasted_iota(jnp.int32, (block, ROPE), 0)
        plain = jnp.zeros((block, ROPE), jnp.bfloat16)

        def put_tails(base, rope, mask):
            tails[0, pl.ds(base, block), :] = jnp.concatenate([rope, mask], axis=1)
            tails[1, pl.ds(base, block), :] = jnp.concatenate([mask, rope], axis=1)

        for k in range(n):
            for c in range(CAP):
                p = where_ref[k * CAP + c]

                @pl.when(p >= 0)
                def _():
                    base = pl.multiple_of(p * block, block)
                    here = pl.multiple_of(sub * width, width)
                    there = pl.multiple_of((1 - sub) * width, width)
                    lat[pl.ds(base, block), pl.ds(here, width)] = mine[k][pl.ds(c * block, block), :]
                    lat[pl.ds(base, block), pl.ds(there, width)] = theirs[k][pl.ds(c * block, block), :]
                    packed = jnp.where(
                        sub == c, mine[k][CAP * block :, :], theirs[k][CAP * block :, :]
                    )
                    rope = jnp.concatenate(
                        [packed[:, i * ROPE : (i + 1) * ROPE] for i in range(parts)], axis=0
                    )
                    hidden = (lane == 0) & (base + row >= len_ref[0])
                    put_tails(base, rope, jnp.where(hidden, HIDE, 0.0).astype(jnp.bfloat16))

        lat[prefix : prefix + block, :] = lat_a[...]
        lat[prefix + block :, :] = lat_b[...]
        put_tails(prefix, rope_a[...], plain)
        put_tails(prefix + block, rope_b[:, :ROPE], plain)
        i = lax.broadcasted_iota(jnp.int32, (queries, queries), 0)
        j = lax.broadcasted_iota(jnp.int32, (queries, queries), 1)
        flip = sub * block
        query_pos = jnp.bitwise_xor(i, flip)
        key_pos = jnp.bitwise_xor(j, flip)
        bias[...] = jnp.where(key_pos <= query_pos, 0.0, HIDE)

    keys = lat[...]
    k2 = jnp.dot(keys, wk_ref[...], preferred_element_type=jnp.float32).astype(jnp.bfloat16)
    v2 = jnp.dot(keys, wv_ref[...], preferred_element_type=jnp.float32).astype(jnp.bfloat16)
    qn = jnp.concatenate([qn_a[...], qn_b[...]], axis=0)
    qr = jnp.concatenate([qr_a[...], qr_b[...]], axis=0)
    lane = lax.broadcasted_iota(jnp.int32, (queries, LANES), 1)
    ones = jnp.ones((keys.shape[0], LANES), jnp.bfloat16)
    rate = math.log2(math.e) / math.sqrt(NOPE + ROPE)
    for j in range(2):
        fill = jnp.where(lane == (1 - j) * ROPE, 1.0, 0.0).astype(jnp.bfloat16)
        own = (lane >= ROPE) if j else (lane < ROPE)
        qc = jnp.concatenate([qn[:, j * NOPE : (j + 1) * NOPE], jnp.where(own, qr, fill)], axis=1)
        kc = jnp.concatenate([k2[:, j * NOPE : (j + 1) * NOPE], tails[j]], axis=1)
        s = lax.dot_general(qc, kc, (((1,), (1,)), ((), ())), preferred_element_type=jnp.float32)
        s = jnp.concatenate([s[:, :prefix], s[:, prefix:] + bias[...]], axis=1)
        peak = jnp.max(s, axis=1, keepdims=True)
        e = jnp.exp2((s - peak) * rate).astype(jnp.bfloat16)
        vc = jnp.concatenate([v2[:, j * VDIM : (j + 1) * VDIM], ones], axis=1)
        o = jnp.dot(e, vc, preferred_element_type=jnp.float32)
        o = (o[:, :VDIM] / o[:, VDIM : VDIM + 1]).astype(jnp.bfloat16)
        out_ref[:, j * VDIM : (j + 1) * VDIM] = o[:block]
        send_ref[:, j * VDIM : (j + 1) * VDIM] = o[block:]


def attend(n, blocks, sub, prefix_len, where, mine, theirs, new_latent, new_rope, q_nope, q_rope,
           other, w_uk, w_uv):
    block, latent = new_latent.shape
    heads = w_uk.shape[1] // NOPE // 2
    pairs = heads // 2
    keys = (blocks + 2) * block
    whole = lambda a: pl.BlockSpec(a.shape, lambda g, *_: (0,) * a.ndim)
    half = heads * NOPE
    nope_at = latent
    rope_at = nope_at + half
    tail_at = rope_at + heads * ROPE

    def at(width, first, follow):
        if follow:
            return pl.BlockSpec((block, width), lambda g, *_: (0, first // width + g))
        return pl.BlockSpec((block, width), lambda g, *_: (0, first // width))

    def ours(rows, width):
        return pl.BlockSpec((rows, width), lambda g, s, *_: (0, s[0] * pairs + g))

    spec = pltpu.PrefetchScalarGridSpec(
        num_scalar_prefetch=3,
        grid=(pairs,),
        in_specs=[whole(a) for a in mine]
        + [whole(a) for a in theirs]
        + [
            whole(new_latent),
            whole(new_rope),
            at(latent, 0, False),
            at(LANES, tail_at, False),
            ours(block, 2 * NOPE),
            ours(block, 2 * ROPE),
            at(2 * NOPE, nope_at, True),
            at(2 * ROPE, rope_at, True),
            ours(latent, 2 * NOPE),
            ours(latent, 2 * VDIM),
        ],
        out_specs=[
            ours(block, 2 * VDIM),
            pl.BlockSpec((block, 2 * VDIM), lambda g, *_: (0, g)),
        ],
        scratch_shapes=[
            pltpu.VMEM((keys, latent), jnp.bfloat16),
            pltpu.VMEM((2, keys, LANES), jnp.bfloat16),
            pltpu.VMEM((2 * block, 2 * block), jnp.float32),
        ],
    )
    return pl.pallas_call(
        functools.partial(attend_kernel, n, blocks),
        grid_spec=spec,
        out_shape=[
            jax.ShapeDtypeStruct((block, 2 * heads * VDIM), jnp.bfloat16),
            jax.ShapeDtypeStruct((block, heads * VDIM), jnp.bfloat16),
        ],
        cost_estimate=pl.CostEstimate(
            flops=4 * keys * latent * heads * NOPE + 8 * block * keys * heads * 256,
            bytes_accessed=8 * 1024 * 1024,
            transcendentals=2 * block * keys * heads,
        ),
        name="attend",
    )(sub, prefix_len, where, *mine, *theirs, new_latent, new_rope, other, other, q_nope, q_rope,
      other, other, w_uk, w_uv)


def shards(
    q_nope,
    q_rope,
    new_latent,
    new_rope,
    pool_latent,
    pool_rope,
    w_uk,
    w_uv,
    block_list,
    prefix_len,
    block_slot,
):
    n = lax.axis_size("req")
    blocks = block_list.shape[1]
    sub = lax.axis_index("sub")
    swap = lambda a: lax.ppermute(a, "sub", [(0, 1), (1, 0)])
    lists = [block_list] + [
        lax.ppermute(block_list, "req", [(i, (i - k) % n) for i in range(n)]) for k in range(1, n)
    ]
    half = q_nope.shape[1] // 2
    rope_half = q_rope.shape[1] // 2
    other = jnp.concatenate(
        [
            new_latent,
            lax.dynamic_slice_in_dim(q_nope, (1 - sub) * half, half, 1),
            lax.dynamic_slice_in_dim(q_rope, (1 - sub) * rope_half, rope_half, 1),
            new_rope,
            jnp.zeros((new_rope.shape[0], LANES - ROPE), jnp.bfloat16),
        ],
        axis=1,
    )
    other = swap(other)
    sent, where = pack(n, lists, block_slot, pool_latent, pool_rope)
    mine = [sent[0]] + [
        lax.ppermute(sent[k], "req", [(i, (i + k) % n) for i in range(n)]) for k in range(1, n)
    ]
    theirs = [swap(a) for a in mine]
    kept, gone = attend(
        n, blocks, sub.reshape(1), prefix_len, where, mine, theirs, new_latent, new_rope, q_nope,
        q_rope, other, w_uk, w_uv,
    )
    back = swap(gone)
    return lax.dynamic_update_slice_in_dim(kept, back, (1 - sub) * half, 1)


def solution(mesh):
    placed = (
        P(("groups", "req", "sub"), "head"),
        P(("groups", "req", "sub"), "head"),
        P(("groups", "req", "sub"), None),
        P(("groups", "req", "sub"), None),
        P(("groups", "req"), None, "sub"),
        P(("groups", "req"), None, None),
        P(None, "head"),
        P(None, "head"),
        P(("groups", "req"), None),
        P(("groups", "req")),
        P("groups"),
    )
    return jax.shard_map(
        shards,
        mesh=mesh,
        in_specs=placed,
        out_specs=P(("groups", "req", "sub"), "head"),
        check_vma=False,
    )
```

```python
import functools
import math

import jax
import jax.numpy as jnp
from jax import lax
from jax.experimental import pallas as pl
from jax.experimental.pallas import tpu as pltpu
from jax.sharding import PartitionSpec as P


NOPE = 128
ROPE = 64
VDIM = 128
CAP = 2
LANES = 128
HIDE = -1e30


def pack_kernel(n, blocks, pool_local, lists, slots_ref, pool_ref, rope_ref, outs, where_ref,
                index_ref, count_ref, lat_sem, rope_sem):
    me = lax.axis_index("req")
    sub = lax.axis_index("sub")
    block = pool_ref.shape[1]
    width = pool_ref.shape[2]
    for i in range(n * CAP):
        index_ref[i] = 0
        where_ref[i] = -1
    for i in range(n):
        count_ref[i] = 0
    for k in range(n):
        found = jnp.int32(0)
        for p in range(blocks):
            physical = slots_ref[lists[k][0, p]]
            owner = physical // pool_local
            mine = owner == me

            @pl.when(mine)
            def _():
                index_ref[k * CAP + found] = physical - owner * pool_local

            found = found + mine.astype(jnp.int32)
            if k == 0:
                step = jnp.bitwise_xor(me, owner)
                earlier = count_ref[step]
                where_ref[step * CAP + earlier] = p
                count_ref[step] = earlier + 1
    parts = width // block
    rows = ROPE // parts
    copies = []
    for k in range(n):
        for c in range(CAP):
            copies.append(pltpu.make_async_copy(
                pool_ref.at[index_ref[k * CAP + c]],
                outs[k].at[pl.ds(c * block, block)],
                lat_sem.at[k * CAP + c],
            ))
        for i in range(parts):
            copies.append(pltpu.make_async_copy(
                rope_ref.at[index_ref[k * CAP + sub], pl.ds(i * rows, rows)],
                outs[k].at[pl.ds(CAP * block, rows), pl.ds(i * block, block)],
                rope_sem.at[k * parts + i],
            ))
    for copy in copies:
        copy.start()
    for copy in copies:
        copy.wait()


def pack(n, lists, block_slot, pool_latent, rope_turned):
    pool_local, block, width = pool_latent.shape
    blocks = lists[0].shape[1]
    rows = CAP * block + block * ROPE // width
    vmem = pl.BlockSpec(memory_space=pltpu.VMEM)
    smem = pl.BlockSpec(memory_space=pltpu.SMEM)

    def body(*refs):
        pack_kernel(
            n, blocks, pool_local, refs[:n], refs[n], refs[n + 1], refs[n + 2],
            refs[n + 3 : 2 * n + 3], refs[2 * n + 3], *refs[2 * n + 4 :],
        )

    out = pl.pallas_call(
        body,
        out_shape=[jax.ShapeDtypeStruct((rows, width), jnp.bfloat16)] * n
        + [jax.ShapeDtypeStruct((n * CAP,), jnp.int32)],
        in_specs=[smem] * (n + 1) + [pl.BlockSpec(memory_space=pl.ANY)] * 2,
        out_specs=[vmem] * n + [smem],
        scratch_shapes=[
            pltpu.SMEM((n * CAP,), jnp.int32),
            pltpu.SMEM((n,), jnp.int32),
            pltpu.SemaphoreType.DMA((n * CAP,)),
            pltpu.SemaphoreType.DMA((n * width // block,)),
        ],
        compiler_params=pltpu.CompilerParams(vmem_limit_bytes=16 << 20),
        cost_estimate=pl.CostEstimate(flops=0, bytes_accessed=4 * n * rows * width, transcendentals=0),
        name="pack",
    )(*lists, block_slot, pool_latent, rope_turned)
    return out[:n], out[n]


def prepare_kernel(lat_ref, qn_ref, qr_ref, rope_ref, out_ref, sem):
    there = 1 - lax.axis_index("sub")
    latent = lat_ref.shape[1]
    half = qn_ref.shape[1] // 2
    rope_half = qr_ref.shape[1] // 2
    tail = latent + half + rope_half
    copies = [
        pltpu.make_async_copy(lat_ref, out_ref.at[:, pl.ds(0, latent)], sem.at[0]),
        pltpu.make_async_copy(
            qn_ref.at[:, pl.ds(pl.multiple_of(there * half, LANES), half)],
            out_ref.at[:, pl.ds(latent, half)],
            sem.at[1],
        ),
        pltpu.make_async_copy(
            qr_ref.at[:, pl.ds(pl.multiple_of(there * rope_half, LANES), rope_half)],
            out_ref.at[:, pl.ds(latent + half, rope_half)],
            sem.at[2],
        ),
        pltpu.make_async_copy(
            rope_ref, out_ref.at[pl.ds(0, ROPE), pl.ds(tail, rope_ref.shape[1])], sem.at[3]
        ),
    ]
    for copy in copies:
        copy.start()
    for copy in copies:
        copy.wait()


def prepare(new_latent, q_nope, q_rope, rope_turned):
    rows, latent = new_latent.shape
    width = latent + q_nope.shape[1] // 2 + q_rope.shape[1] // 2 + rows
    return pl.pallas_call(
        prepare_kernel,
        out_shape=jax.ShapeDtypeStruct((rows, width), jnp.bfloat16),
        in_specs=[pl.BlockSpec(memory_space=pl.ANY)] * 4,
        out_specs=pl.BlockSpec(memory_space=pltpu.VMEM),
        scratch_shapes=[pltpu.SemaphoreType.DMA((4,))],
        compiler_params=pltpu.CompilerParams(vmem_limit_bytes=16 << 20),
        cost_estimate=pl.CostEstimate(flops=0, bytes_accessed=4 * rows * width, transcendentals=0),
        name="prepare",
    )(new_latent, q_nope, q_rope, rope_turned)


RATE = math.log2(math.e) / math.sqrt(NOPE + ROPE)


def attend_kernel(steps, fresh, sub_ref, len_ref, where_ref, *refs):
    count = len(steps)
    mine = refs[:count]
    theirs = refs[count : 2 * count]
    refs = refs[2 * count :]
    if fresh:
        lat_a, rope_a, lat_b, rope_b, *refs = refs
        qn_a, qr_a, qn_b, qr_b, wk_ref, wv_ref, acc_ref, stat_ref, lat, tails, bias = refs
    else:
        (qn_a, qr_a, qn_b, qr_b, wk_ref, wv_ref, acc_ref, stat_ref, out_ref, send_ref, lat,
         tails) = refs
    sub = sub_ref[0]
    block = qn_a.shape[0]
    chunk = CAP * block
    first = chunk if fresh else 0
    queries = 2 * block

    @pl.when(pl.program_id(0) == 0)
    def _():
        def put_tails(base, rope, mask):
            tails[0, base : base + block, :] = jnp.concatenate([rope, mask], axis=1)
            tails[1, base : base + block, :] = jnp.concatenate([mask, rope], axis=1)

        lane = lax.broadcasted_iota(jnp.int32, (block, ROPE), 1)
        row = lax.broadcasted_iota(jnp.int32, (block, ROPE), 0)
        for i, k in enumerate(steps):
            width = mine[i].shape[1]
            here = pl.multiple_of(sub * width, width)
            there = pl.multiple_of((1 - sub) * width, width)
            base = first + i * chunk
            lat[base : base + chunk, pl.ds(here, width)] = mine[i][:chunk, :]
            lat[base : base + chunk, pl.ds(there, width)] = theirs[i][:chunk, :]
            for c in range(CAP):
                packed = jnp.where(sub == c, mine[i][chunk:, :], theirs[i][chunk:, :])
                rope = jnp.concatenate(
                    [packed[:, j * block : (j + 1) * block] for j in range(width // block)], axis=0
                )
                p = where_ref[k * CAP + c]
                hidden = (lane == 0) & ((p < 0) | (p * block + row >= len_ref[0]))
                put_tails(
                    base + c * block, rope.T, jnp.where(hidden, HIDE, 0.0).astype(jnp.bfloat16)
                )
        if fresh:
            plain = jnp.zeros((block, ROPE), jnp.bfloat16)
            lat[:block, :] = lat_a[...]
            lat[block:chunk, :] = lat_b[...]
            put_tails(0, rope_a[...].T, plain)
            put_tails(block, rope_b[:ROPE, :].T, plain)
            i = lax.broadcasted_iota(jnp.int32, (queries, queries), 0)
            j = lax.broadcasted_iota(jnp.int32, (queries, queries), 1)
            flip = sub * block
            seen = jnp.bitwise_xor(j, flip) <= jnp.bitwise_xor(i, flip)
            bias[...] = jnp.where(seen, 0.0, HIDE)

    chunks = count + (1 if fresh else 0)
    qn = jnp.concatenate([qn_a[...], qn_b[...]], axis=0)
    qr = jnp.concatenate([qr_a[...], qr_b[...]], axis=0)
    lane = lax.broadcasted_iota(jnp.int32, (queries, LANES), 1)
    ones = jnp.ones((chunk, LANES), jnp.bfloat16)
    qc = []
    for j in range(2):
        fill = jnp.where(lane == (1 - j) * ROPE, 1.0, 0.0).astype(jnp.bfloat16)
        own = (lane >= ROPE) if j else (lane < ROPE)
        qc.append(
            jnp.concatenate([qn[:, j * NOPE : (j + 1) * NOPE], jnp.where(own, qr, fill)], axis=1)
        )
    scores = [[], []]
    values = []
    for i in range(chunks):
        keys = lat[i * chunk : (i + 1) * chunk, :]
        k2 = jnp.dot(keys, wk_ref[...], preferred_element_type=jnp.float32).astype(jnp.bfloat16)
        v2 = jnp.dot(keys, wv_ref[...], preferred_element_type=jnp.float32).astype(jnp.bfloat16)
        values.append(v2)
        for j in range(2):
            kc = jnp.concatenate(
                [k2[:, j * NOPE : (j + 1) * NOPE], tails[j, i * chunk : (i + 1) * chunk, :]], axis=1
            )
            s = lax.dot_general(
                qc[j], kc, (((1,), (1,)), ((), ())), preferred_element_type=jnp.float32
            )
            if fresh and i == 0:
                s = s + bias[...]
            scores[j].append(s)
    peaks = []
    sums = []
    for j in range(2):
        peak = functools.reduce(jnp.maximum, scores[j])
        peak = jnp.max(peak, axis=1, keepdims=True)
        if not fresh:
            before = stat_ref[:, j : j + 1]
            peak = jnp.maximum(peak, before)
        o = None
        for i in range(chunks):
            e = jnp.exp2((scores[j][i] - peak) * RATE).astype(jnp.bfloat16)
            vc = jnp.concatenate([values[i][:, j * VDIM : (j + 1) * VDIM], ones], axis=1)
            part = jnp.dot(e, vc, preferred_element_type=jnp.float32)
            o = part if o is None else o + part
        total = o[:, VDIM:]
        o = o[:, :VDIM]
        if fresh:
            acc_ref[:, j * VDIM : (j + 1) * VDIM] = o
            peaks.append(peak)
            sums.append(total)
        else:
            keep = jnp.exp2((before - peak) * RATE)
            total = total[:, :1] + keep * stat_ref[:, 2 + j : 3 + j]
            o = o + keep * acc_ref[:, j * VDIM : (j + 1) * VDIM]
            o = (o / total).astype(jnp.bfloat16)
            out_ref[:, j * VDIM : (j + 1) * VDIM] = o[:block]
            send_ref[:, j * VDIM : (j + 1) * VDIM] = o[block:]
    if fresh:
        stat_ref[...] = jnp.where(
            lane == 0, peaks[0],
            jnp.where(lane == 1, peaks[1], jnp.where(lane == 2, sums[0], sums[1])),
        )


def attend(steps, sub, prefix_len, where, mine, theirs, new_latent, rope_turned, q_nope, q_rope,
           other, w_uk, w_uv, state):
    fresh = state is None
    block, latent = new_latent.shape
    heads = w_uk.shape[1] // NOPE // 2
    pairs = heads // 2
    keys = (len(steps) + (1 if fresh else 0)) * CAP * block
    whole = lambda a: pl.BlockSpec(a.shape, lambda g, *_: (0,) * a.ndim)
    nope_at = latent
    rope_at = nope_at + heads * NOPE
    tail_at = rope_at + heads * ROPE

    def at(width, first, follow):
        if follow:
            return pl.BlockSpec((block, width), lambda g, *_: (0, first // width + g))
        return pl.BlockSpec((block, width), lambda g, *_: (0, first // width))

    def ours(rows, width):
        return pl.BlockSpec((rows, width), lambda g, s, *_: (0, s[0] * pairs + g))

    def step(rows, width):
        return pl.BlockSpec((rows, width), lambda g, *_: (0, g))

    specs = [whole(a) for a in mine] + [whole(a) for a in theirs]
    args = [*mine, *theirs]
    if fresh:
        specs += [whole(new_latent), whole(rope_turned), at(latent, 0, False), at(LANES, tail_at, False)]
        args += [new_latent, rope_turned, other, other]
    specs += [
        ours(block, 2 * NOPE),
        ours(block, 2 * ROPE),
        at(2 * NOPE, nope_at, True),
        at(2 * ROPE, rope_at, True),
        ours(latent, 2 * NOPE),
        ours(latent, 2 * VDIM),
    ]
    args += [q_nope, q_rope, other, other, w_uk, w_uv]
    state_specs = [step(2 * block, 2 * VDIM), step(2 * block, LANES)]
    scratch = [
        pltpu.VMEM((keys, latent), jnp.bfloat16),
        pltpu.VMEM((2, keys, LANES), jnp.bfloat16),
    ]
    if fresh:
        out_specs = state_specs
        out_shape = [
            jax.ShapeDtypeStruct((2 * block, heads * VDIM), jnp.float32),
            jax.ShapeDtypeStruct((2 * block, pairs * LANES), jnp.float32),
        ]
        scratch.append(pltpu.VMEM((2 * block, 2 * block), jnp.float32))
    else:
        specs += state_specs
        args += state
        out_specs = [ours(block, 2 * VDIM), step(block, 2 * VDIM)]
        out_shape = [
            jax.ShapeDtypeStruct((block, 2 * heads * VDIM), jnp.bfloat16),
            jax.ShapeDtypeStruct((block, heads * VDIM), jnp.bfloat16),
        ]
    return pl.pallas_call(
        functools.partial(attend_kernel, steps, fresh),
        grid_spec=pltpu.PrefetchScalarGridSpec(
            num_scalar_prefetch=3,
            grid=(pairs,),
            in_specs=specs,
            out_specs=out_specs,
            scratch_shapes=scratch,
        ),
        out_shape=out_shape,
        compiler_params=pltpu.CompilerParams(vmem_limit_bytes=40 << 20),
        cost_estimate=pl.CostEstimate(
            flops=4 * keys * latent * heads * NOPE + 8 * block * keys * heads * 256,
            bytes_accessed=8 * 1024 * 1024,
            transcendentals=2 * block * keys * heads,
        ),
        name="attend_new" if fresh else "attend_prefix",
    )(sub, prefix_len, where, *args)


def shards(
    q_nope,
    q_rope,
    new_latent,
    new_rope,
    pool_latent,
    pool_rope,
    w_uk,
    w_uv,
    block_list,
    prefix_len,
    block_slot,
):
    n = lax.axis_size("req")
    sub = lax.axis_index("sub")
    half = q_nope.shape[1] // 2
    swap = lambda a: lax.ppermute(a, "sub", [(0, 1), (1, 0)])
    cross = lambda a, k: lax.ppermute(a, "req", [(i, i ^ k) for i in range(n)])
    far = list(range(n - 1, 0, -1))
    keep = lambda a: pltpu.with_memory_space_constraint(a, pltpu.HBM)
    q_nope, q_rope, new_latent, w_uk, w_uv = map(keep, (q_nope, q_rope, new_latent, w_uk, w_uv))
    pool_latent = keep(pool_latent)
    pool_turned = keep(pool_rope.swapaxes(1, 2))
    rope_turned = keep(new_rope.T)
    got = {k: cross(block_list, k) for k in far}
    lists = [block_list] + [got[k] for k in range(1, n)]
    other = prepare(new_latent, q_nope, q_rope, rope_turned)
    other = swap(other)
    sent, where = pack(n, lists, block_slot, pool_latent, pool_turned)
    local = swap(sent[0])
    mine = [cross(sent[k], k) for k in far]
    theirs = [swap(a) for a in mine]
    common = (new_latent, rope_turned, q_nope, q_rope, other, w_uk, w_uv)
    state = attend([0], sub.reshape(1), prefix_len, where, [sent[0]], [local], *common, None)
    kept, gone = attend(far, sub.reshape(1), prefix_len, where, mine, theirs, *common, state)
    back = swap(gone)
    return lax.dynamic_update_slice_in_dim(kept, back, (1 - sub) * half, 1)


def solution(mesh):
    placed = (
        P(("groups", "req", "sub"), "head"),
        P(("groups", "req", "sub"), "head"),
        P(("groups", "req", "sub"), None),
        P(("groups", "req", "sub"), None),
        P(("groups", "req"), None, "sub"),
        P(("groups", "req"), None, None),
        P(None, "head"),
        P(None, "head"),
        P(("groups", "req"), None),
        P(("groups", "req")),
        P("groups"),
    )
    return jax.shard_map(
        shards,
        mesh=mesh,
        in_specs=placed,
        out_specs=P(("groups", "req", "sub"), "head"),
        check_vma=False,
    )
```

```python
import functools
import math

import jax
import jax.numpy as jnp
from jax import lax
from jax.experimental import pallas as pl
from jax.experimental.pallas import tpu as pltpu
from jax.sharding import PartitionSpec as P


NOPE = 128
ROPE = 64
VDIM = 128
CAP = 2
LANES = 128
HIDE = -1e30


def pack_kernel(n, blocks, pool_local, lists, slots_ref, pool_ref, rope_ref, outs, where_ref,
                index_ref, count_ref, lat_sem, rope_sem):
    me = lax.axis_index("req")
    sub = lax.axis_index("sub")
    block = pool_ref.shape[1]
    width = pool_ref.shape[2]
    for i in range(n * CAP):
        index_ref[i] = 0
        where_ref[i] = -1
    for i in range(n):
        count_ref[i] = 0
    for k in range(n):
        found = jnp.int32(0)
        for p in range(blocks):
            physical = slots_ref[lists[k][0, p]]
            owner = physical // pool_local
            mine = owner == me

            @pl.when(mine)
            def _():
                index_ref[k * CAP + found] = physical - owner * pool_local

            found = found + mine.astype(jnp.int32)
            if k == 0:
                step = jnp.bitwise_xor(me, owner)
                earlier = count_ref[step]
                where_ref[step * CAP + earlier] = p
                count_ref[step] = earlier + 1
    parts = width // block
    rows = ROPE // parts
    copies = []
    for k in range(n):
        for c in range(CAP):
            copies.append(pltpu.make_async_copy(
                pool_ref.at[index_ref[k * CAP + c]],
                outs[k].at[pl.ds(c * block, block)],
                lat_sem.at[k * CAP + c],
            ))
        for i in range(parts):
            copies.append(pltpu.make_async_copy(
                rope_ref.at[index_ref[k * CAP + sub], pl.ds(i * rows, rows)],
                outs[k].at[pl.ds(CAP * block, rows), pl.ds(i * block, block)],
                rope_sem.at[k * parts + i],
            ))
    for copy in copies:
        copy.start()
    for copy in copies:
        copy.wait()


def pack(n, lists, block_slot, pool_latent, rope_turned):
    pool_local, block, width = pool_latent.shape
    blocks = lists[0].shape[1]
    rows = CAP * block + block * ROPE // width
    vmem = pl.BlockSpec(memory_space=pltpu.VMEM)
    smem = pl.BlockSpec(memory_space=pltpu.SMEM)

    def body(*refs):
        pack_kernel(
            n, blocks, pool_local, refs[:n], refs[n], refs[n + 1], refs[n + 2],
            refs[n + 3 : 2 * n + 3], refs[2 * n + 3], *refs[2 * n + 4 :],
        )

    out = pl.pallas_call(
        body,
        out_shape=[jax.ShapeDtypeStruct((rows, width), jnp.bfloat16)] * n
        + [jax.ShapeDtypeStruct((n * CAP,), jnp.int32)],
        in_specs=[smem] * (n + 1) + [pl.BlockSpec(memory_space=pl.ANY)] * 2,
        out_specs=[vmem] * n + [smem],
        scratch_shapes=[
            pltpu.SMEM((n * CAP,), jnp.int32),
            pltpu.SMEM((n,), jnp.int32),
            pltpu.SemaphoreType.DMA((n * CAP,)),
            pltpu.SemaphoreType.DMA((n * width // block,)),
        ],
        compiler_params=pltpu.CompilerParams(vmem_limit_bytes=16 << 20),
        cost_estimate=pl.CostEstimate(flops=0, bytes_accessed=4 * n * rows * width, transcendentals=0),
        name="pack",
    )(*lists, block_slot, pool_latent, rope_turned)
    return out[:n], out[n]


def prepare_kernel(lat_ref, qn_ref, qr_ref, rope_ref, out_ref, sem):
    there = 1 - lax.axis_index("sub")
    latent = lat_ref.shape[1]
    half = qn_ref.shape[1] // 2
    rope_half = qr_ref.shape[1] // 2
    tail = latent + half + rope_half
    copies = [
        pltpu.make_async_copy(lat_ref, out_ref.at[:, pl.ds(0, latent)], sem.at[0]),
        pltpu.make_async_copy(
            qn_ref.at[:, pl.ds(pl.multiple_of(there * half, LANES), half)],
            out_ref.at[:, pl.ds(latent, half)],
            sem.at[1],
        ),
        pltpu.make_async_copy(
            qr_ref.at[:, pl.ds(pl.multiple_of(there * rope_half, LANES), rope_half)],
            out_ref.at[:, pl.ds(latent + half, rope_half)],
            sem.at[2],
        ),
        pltpu.make_async_copy(
            rope_ref, out_ref.at[pl.ds(0, ROPE), pl.ds(tail, rope_ref.shape[1])], sem.at[3]
        ),
    ]
    for copy in copies:
        copy.start()
    for copy in copies:
        copy.wait()


def prepare(new_latent, q_nope, q_rope, rope_turned):
    rows, latent = new_latent.shape
    width = latent + q_nope.shape[1] // 2 + q_rope.shape[1] // 2 + rows
    return pl.pallas_call(
        prepare_kernel,
        out_shape=jax.ShapeDtypeStruct((rows, width), jnp.bfloat16),
        in_specs=[pl.BlockSpec(memory_space=pl.ANY)] * 4,
        out_specs=pl.BlockSpec(memory_space=pltpu.VMEM),
        scratch_shapes=[pltpu.SemaphoreType.DMA((4,))],
        compiler_params=pltpu.CompilerParams(vmem_limit_bytes=16 << 20),
        cost_estimate=pl.CostEstimate(flops=0, bytes_accessed=4 * rows * width, transcendentals=0),
        name="prepare",
    )(new_latent, q_nope, q_rope, rope_turned)


RATE = math.log2(math.e) / math.sqrt(NOPE + ROPE)


def attend_kernel(steps, fresh, pairs, sub_ref, len_ref, where_ref, *refs):
    count = len(steps)
    mine = refs[:count]
    theirs = refs[count : 2 * count]
    refs = refs[2 * count :]
    if fresh:
        lat_a, rope_a, lat_b, rope_b, *refs = refs
        (qn_a, qr_a, qn_b, qr_b, wk_ref, wv_ref, acc_ref, stat_ref,
         lat, kc, vc, score, weight, peak, bias) = refs
    else:
        (qn_a, qr_a, qn_b, qr_b, wk_ref, wv_ref, acc_ref, stat_ref, out_ref, send_ref,
         lat, kc, vc, score, weight, peak) = refs
    sub = sub_ref[0]
    block = qn_a.shape[0]
    chunk = CAP * block
    first = chunk if fresh else 0
    queries = 2 * block
    keys = lat.shape[0]
    g = pl.program_id(0)
    head = lambda j: slice(j * LANES, (j + 1) * LANES)

    @pl.when(g == 0)
    def _():
        def put_tails(base, rope, mask):
            kc[0, base : base + block, NOPE:] = jnp.concatenate([rope, mask], axis=1)
            kc[1, base : base + block, NOPE:] = jnp.concatenate([mask, rope], axis=1)

        lane = lax.broadcasted_iota(jnp.int32, (block, ROPE), 1)
        row = lax.broadcasted_iota(jnp.int32, (block, ROPE), 0)
        vc[:, :, VDIM:] = jnp.ones((2, keys, LANES), jnp.bfloat16)
        for i, k in enumerate(steps):
            width = mine[i].shape[1]
            here = pl.multiple_of(sub * width, width)
            there = pl.multiple_of((1 - sub) * width, width)
            base = first + i * chunk
            lat[base : base + chunk, pl.ds(here, width)] = mine[i][:chunk, :]
            lat[base : base + chunk, pl.ds(there, width)] = theirs[i][:chunk, :]
            for c in range(CAP):
                packed = jnp.where(sub == c, mine[i][chunk:, :], theirs[i][chunk:, :])
                rope = jnp.concatenate(
                    [packed[:, j * block : (j + 1) * block] for j in range(width // block)], axis=0
                )
                p = where_ref[k * CAP + c]
                hidden = (lane == 0) & ((p < 0) | (p * block + row >= len_ref[0]))
                put_tails(
                    base + c * block, rope.T, jnp.where(hidden, HIDE, 0.0).astype(jnp.bfloat16)
                )
        if fresh:
            plain = jnp.zeros((block, ROPE), jnp.bfloat16)
            lat[:block, :] = lat_a[...]
            lat[block:chunk, :] = lat_b[...]
            put_tails(0, rope_a[...].T, plain)
            put_tails(block, rope_b[:ROPE, :].T, plain)
            i = lax.broadcasted_iota(jnp.int32, (queries, queries), 0)
            j = lax.broadcasted_iota(jnp.int32, (queries, queries), 1)
            flip = sub * block
            seen = jnp.bitwise_xor(j, flip) <= jnp.bitwise_xor(i, flip)
            bias[...] = jnp.where(seen, 0.0, HIDE)

    def step(produce, consume):
        lane = lax.broadcasted_iota(jnp.int32, (queries, LANES), 1)
        if consume:
            top, keep, total = [], [], []
            for j in range(2):
                most = peak[j]
                if not fresh:
                    stat = stat_ref[:, head(j)]
                    turned = pltpu.roll(stat, LANES // 2, 1)
                    before = jnp.where(lane < LANES // 2, stat, turned)
                    total.append(jnp.where(lane < LANES // 2, turned, stat))
                    most = jnp.maximum(most, before)
                    keep.append(jnp.exp2((before - most) * RATE))
                top.append(most)
                for i in range(keys // LANES):
                    s = score[j, :, i * LANES : (i + 1) * LANES]
                    weight[j, :, i * LANES : (i + 1) * LANES] = jnp.exp2((s - most) * RATE).astype(
                        jnp.bfloat16
                    )
        for i in range(keys // chunk):
            rows = slice(i * chunk, (i + 1) * chunk)
            if produce:
                k2 = jnp.dot(lat[rows, :], wk_ref[...], preferred_element_type=jnp.float32)
                for j in range(2):
                    kc[j, rows, :NOPE] = k2[:, head(j)].astype(jnp.bfloat16)
            if consume:
                v2 = jnp.dot(lat[rows, :], wv_ref[...], preferred_element_type=jnp.float32)
                for j in range(2):
                    vc[j, rows, :VDIM] = v2[:, head(j)].astype(jnp.bfloat16)
        for j in range(2):
            if consume:
                o = jnp.dot(weight[j], vc[j], preferred_element_type=jnp.float32)
                o, norm = o[:, :VDIM], o[:, VDIM:]
                if fresh:
                    acc_ref[:, head(j)] = o
                    stat_ref[:, head(j)] = jnp.where(lane < LANES // 2, top[j], norm)
                else:
                    norm = norm + keep[j] * total[j]
                    o = o + keep[j] * acc_ref[:, head(j)]
                    o = (o / norm).astype(jnp.bfloat16)
                    out_ref[:, head(j)] = o[:block]
                    send_ref[:, head(j)] = o[block:]
            if produce:
                qn = jnp.concatenate([qn_a[:, head(j)], qn_b[:, head(j)]], axis=0)
                qr = jnp.concatenate([qr_a[...], qr_b[...]], axis=0)
                fill = jnp.where(lane == (1 - j) * ROPE, 1.0, 0.0).astype(jnp.bfloat16)
                own = (lane >= ROPE) if j else (lane < ROPE)
                qc = jnp.concatenate([qn, jnp.where(own, qr, fill)], axis=1)
                most = None
                for i in range(keys // chunk):
                    s = lax.dot_general(
                        qc, kc[j, i * chunk : (i + 1) * chunk, :], (((1,), (1,)), ((), ())),
                        preferred_element_type=jnp.float32,
                    )
                    if fresh and i == 0:
                        s = s + bias[...]
                    score[j, :, i * chunk : (i + 1) * chunk] = s
                    for part in range(chunk // LANES):
                        piece = s[:, head(part)]
                        most = piece if most is None else jnp.maximum(most, piece)
                peak[j] = jnp.broadcast_to(jnp.max(most, axis=1, keepdims=True), (queries, LANES))

    pl.when(g == 0)(lambda: step(True, False))
    pl.when((g > 0) & (g < pairs))(lambda: step(True, True))
    pl.when(g == pairs)(lambda: step(False, True))


def attend(steps, sub, prefix_len, where, mine, theirs, new_latent, rope_turned, q_nope, q_rope,
           other, w_uk, w_uv, state):
    fresh = state is None
    block, latent = new_latent.shape
    heads = w_uk.shape[1] // NOPE // 2
    pairs = heads // 2
    keys = (len(steps) + (1 if fresh else 0)) * CAP * block
    whole = lambda a: pl.BlockSpec(a.shape, lambda g, *_: (0,) * a.ndim)
    nope_at = latent
    rope_at = nope_at + heads * NOPE
    tail_at = rope_at + heads * ROPE

    now = lambda g: jnp.minimum(g, pairs - 1)
    past = lambda g: jnp.maximum(g - 1, 0)

    def at(width, first, follow):
        if follow:
            return pl.BlockSpec((block, width), lambda g, *_: (0, first // width + now(g)))
        return pl.BlockSpec((block, width), lambda g, *_: (0, first // width))

    def ours(rows, width, when):
        return pl.BlockSpec((rows, width), lambda g, s, *_: (0, s[0] * pairs + when(g)))

    def step(rows, width):
        return pl.BlockSpec((rows, width), lambda g, *_: (0, past(g)))

    specs = [whole(a) for a in mine] + [whole(a) for a in theirs]
    args = [*mine, *theirs]
    if fresh:
        specs += [whole(new_latent), whole(rope_turned), at(latent, 0, False), at(LANES, tail_at, False)]
        args += [new_latent, rope_turned, other, other]
    specs += [
        ours(block, 2 * NOPE, now),
        ours(block, 2 * ROPE, now),
        at(2 * NOPE, nope_at, True),
        at(2 * ROPE, rope_at, True),
        ours(latent, 2 * NOPE, now),
        ours(latent, 2 * VDIM, past),
    ]
    args += [q_nope, q_rope, other, other, w_uk, w_uv]
    state_specs = [step(2 * block, 2 * VDIM), step(2 * block, 2 * LANES)]
    scratch = [
        pltpu.VMEM((keys, latent), jnp.bfloat16),
        pltpu.VMEM((2, keys, NOPE + LANES), jnp.bfloat16),
        pltpu.VMEM((2, keys, VDIM + LANES), jnp.bfloat16),
        pltpu.VMEM((2, 2 * block, keys), jnp.float32),
        pltpu.VMEM((2, 2 * block, keys), jnp.bfloat16),
        pltpu.VMEM((2, 2 * block, LANES), jnp.float32),
    ]
    if fresh:
        out_specs = state_specs
        out_shape = [
            jax.ShapeDtypeStruct((2 * block, heads * VDIM), jnp.float32),
            jax.ShapeDtypeStruct((2 * block, heads * LANES), jnp.float32),
        ]
        scratch.append(pltpu.VMEM((2 * block, 2 * block), jnp.float32))
    else:
        specs += state_specs
        args += state
        out_specs = [ours(block, 2 * VDIM, past), step(block, 2 * VDIM)]
        out_shape = [
            jax.ShapeDtypeStruct((block, 2 * heads * VDIM), jnp.bfloat16),
            jax.ShapeDtypeStruct((block, heads * VDIM), jnp.bfloat16),
        ]
    return pl.pallas_call(
        functools.partial(attend_kernel, steps, fresh, pairs),
        grid_spec=pltpu.PrefetchScalarGridSpec(
            num_scalar_prefetch=3,
            grid=(pairs + 1,),
            in_specs=specs,
            out_specs=out_specs,
            scratch_shapes=scratch,
        ),
        out_shape=out_shape,
        compiler_params=pltpu.CompilerParams(vmem_limit_bytes=40 << 20),
        cost_estimate=pl.CostEstimate(
            flops=4 * keys * latent * heads * NOPE + 8 * block * keys * heads * 256,
            bytes_accessed=8 * 1024 * 1024,
            transcendentals=2 * block * keys * heads,
        ),
        name="attend_new" if fresh else "attend_prefix",
    )(sub, prefix_len, where, *args)


def shards(
    q_nope,
    q_rope,
    new_latent,
    new_rope,
    pool_latent,
    pool_rope,
    w_uk,
    w_uv,
    block_list,
    prefix_len,
    block_slot,
):
    n = lax.axis_size("req")
    sub = lax.axis_index("sub")
    half = q_nope.shape[1] // 2
    swap = lambda a: lax.ppermute(a, "sub", [(0, 1), (1, 0)])
    cross = lambda a, k: lax.ppermute(a, "req", [(i, i ^ k) for i in range(n)])
    far = list(range(n - 1, 0, -1))
    keep = lambda a: pltpu.with_memory_space_constraint(a, pltpu.HBM)
    q_nope, q_rope, new_latent, w_uk, w_uv = map(keep, (q_nope, q_rope, new_latent, w_uk, w_uv))
    pool_latent = keep(pool_latent)
    pool_turned = keep(pool_rope.swapaxes(1, 2))
    rope_turned = keep(new_rope.T)
    got = {k: cross(block_list, k) for k in far}
    lists = [block_list] + [got[k] for k in range(1, n)]
    other = prepare(new_latent, q_nope, q_rope, rope_turned)
    other = swap(other)
    sent, where = pack(n, lists, block_slot, pool_latent, pool_turned)
    local = swap(sent[0])
    mine = [cross(sent[k], k) for k in far]
    theirs = [swap(a) for a in mine]
    common = (new_latent, rope_turned, q_nope, q_rope, other, w_uk, w_uv)
    state = attend([0], sub.reshape(1), prefix_len, where, [sent[0]], [local], *common, None)
    kept, gone = attend(far, sub.reshape(1), prefix_len, where, mine, theirs, *common, state)
    back = swap(gone)
    return lax.dynamic_update_slice_in_dim(kept, back, (1 - sub) * half, 1)


def solution(mesh):
    placed = (
        P(("groups", "req", "sub"), "head"),
        P(("groups", "req", "sub"), "head"),
        P(("groups", "req", "sub"), None),
        P(("groups", "req", "sub"), None),
        P(("groups", "req"), None, "sub"),
        P(("groups", "req"), None, None),
        P(None, "head"),
        P(None, "head"),
        P(("groups", "req"), None),
        P(("groups", "req")),
        P("groups"),
    )
    return jax.shard_map(
        shards,
        mesh=mesh,
        in_specs=placed,
        out_specs=P(("groups", "req", "sub"), "head"),
        check_vma=False,
    )
```

```python
import functools
import math

import jax
import jax.numpy as jnp
from jax import lax
from jax.experimental import pallas as pl
from jax.experimental.pallas import tpu as pltpu
from jax.sharding import PartitionSpec as P


NOPE = 128
ROPE = 64
VDIM = 128
CAP = 2
LANES = 128
HIDE = -1e30


def pack_kernel(n, blocks, pool_local, lists, slots_ref, len_ref, pool_ref, rope_ref, outs, where_ref,
                index_ref, count_ref, lat_sem, rope_sem):
    me = lax.axis_index("req")
    sub = lax.axis_index("sub")
    block = pool_ref.shape[1]
    width = pool_ref.shape[2]
    for i in range(n * CAP):
        index_ref[i] = 0
        where_ref[i] = -1
    where_ref[n * CAP] = len_ref[0]
    for i in range(n):
        count_ref[i] = 0
    for k in range(n):
        found = jnp.int32(0)
        for p in range(blocks):
            physical = slots_ref[lists[k][0, p]]
            owner = physical // pool_local
            mine = owner == me

            @pl.when(mine)
            def _():
                index_ref[k * CAP + found] = physical - owner * pool_local

            found = found + mine.astype(jnp.int32)
            if k == 0:
                step = jnp.bitwise_xor(me, owner)
                earlier = count_ref[step]
                where_ref[step * CAP + earlier] = p
                count_ref[step] = earlier + 1
    parts = width // block
    rows = ROPE // parts
    copies = []
    for k in range(n):
        for c in range(CAP):
            copies.append(pltpu.make_async_copy(
                pool_ref.at[index_ref[k * CAP + c]],
                outs[k].at[pl.ds(c * block, block)],
                lat_sem.at[k * CAP + c],
            ))
        for i in range(parts):
            copies.append(pltpu.make_async_copy(
                rope_ref.at[index_ref[k * CAP + sub], pl.ds(i * rows, rows)],
                outs[k].at[pl.ds(CAP * block, rows), pl.ds(i * block, block)],
                rope_sem.at[k * parts + i],
            ))
    for copy in copies:
        copy.start()
    for copy in copies:
        copy.wait()


def pack(n, lists, block_slot, prefix_len, pool_latent, rope_turned):
    pool_local, block, width = pool_latent.shape
    blocks = lists[0].shape[1]
    rows = CAP * block + block * ROPE // width
    vmem = pl.BlockSpec(memory_space=pltpu.VMEM)
    smem = pl.BlockSpec(memory_space=pltpu.SMEM)

    def body(*refs):
        pack_kernel(
            n, blocks, pool_local, refs[:n], *refs[n : n + 4],
            refs[n + 4 : 2 * n + 4], *refs[2 * n + 4 :],
        )

    out = pl.pallas_call(
        body,
        out_shape=[jax.ShapeDtypeStruct((rows, width), jnp.bfloat16)] * n
        + [jax.ShapeDtypeStruct((n * CAP + 1,), jnp.int32)],
        in_specs=[smem] * (n + 2) + [pl.BlockSpec(memory_space=pl.ANY)] * 2,
        out_specs=[vmem] * n + [smem],
        scratch_shapes=[
            pltpu.SMEM((n * CAP,), jnp.int32),
            pltpu.SMEM((n,), jnp.int32),
            pltpu.SemaphoreType.DMA((n * CAP,)),
            pltpu.SemaphoreType.DMA((n * width // block,)),
        ],
        compiler_params=pltpu.CompilerParams(vmem_limit_bytes=16 << 20),
        cost_estimate=pl.CostEstimate(flops=0, bytes_accessed=4 * n * rows * width, transcendentals=0),
        name="pack",
    )(*lists, block_slot, prefix_len, pool_latent, rope_turned)
    return out[:n], out[n]


def prepare_kernel(lat_ref, qn_ref, qr_ref, rope_ref, out_ref, sem):
    there = 1 - lax.axis_index("sub")
    latent = lat_ref.shape[1]
    half = qn_ref.shape[1] // 2
    rope_half = qr_ref.shape[1] // 2
    tail = latent + half + rope_half
    copies = [
        pltpu.make_async_copy(lat_ref, out_ref.at[:, pl.ds(0, latent)], sem.at[0]),
        pltpu.make_async_copy(
            qn_ref.at[:, pl.ds(pl.multiple_of(there * half, LANES), half)],
            out_ref.at[:, pl.ds(latent, half)],
            sem.at[1],
        ),
        pltpu.make_async_copy(
            qr_ref.at[:, pl.ds(pl.multiple_of(there * rope_half, LANES), rope_half)],
            out_ref.at[:, pl.ds(latent + half, rope_half)],
            sem.at[2],
        ),
        pltpu.make_async_copy(
            rope_ref, out_ref.at[pl.ds(0, ROPE), pl.ds(tail, rope_ref.shape[1])], sem.at[3]
        ),
    ]
    for copy in copies:
        copy.start()
    for copy in copies:
        copy.wait()


def prepare(new_latent, q_nope, q_rope, rope_turned):
    rows, latent = new_latent.shape
    width = latent + q_nope.shape[1] // 2 + q_rope.shape[1] // 2 + rows
    return pl.pallas_call(
        prepare_kernel,
        out_shape=jax.ShapeDtypeStruct((rows, width), jnp.bfloat16),
        in_specs=[pl.BlockSpec(memory_space=pl.ANY)] * 4,
        out_specs=pl.BlockSpec(memory_space=pltpu.VMEM),
        scratch_shapes=[pltpu.SemaphoreType.DMA((4,))],
        compiler_params=pltpu.CompilerParams(vmem_limit_bytes=16 << 20),
        cost_estimate=pl.CostEstimate(flops=0, bytes_accessed=4 * rows * width, transcendentals=0),
        name="prepare",
    )(new_latent, q_nope, q_rope, rope_turned)


RATE = math.log2(math.e) / math.sqrt(NOPE + ROPE)


def attend_kernel(steps, fresh, halves, sub_ref, where_ref, *refs):
    count = len(steps)
    mine = refs[:count]
    theirs = refs[count : 2 * count]
    refs = refs[2 * count :]
    if fresh:
        lat_a, rope_a, lat_b, rope_b, *refs = refs
    lead, odd, even = refs[:6], refs[6:12], refs[12:18]
    if fresh:
        acc_ref, stat_ref, lat, kc, vt, score, weight, peak, bias = refs[18:]
    else:
        acc_ref, stat_ref, out_ref, send_ref, lat, kc, vt, score, weight, peak = refs[18:]
    sub = sub_ref[0]
    block = lead[0].shape[0]
    chunk = CAP * block
    first = chunk if fresh else 0
    queries = 2 * block
    keys = lat.shape[0]
    t = pl.program_id(0)
    head = lambda j: slice(j * LANES, (j + 1) * LANES)

    def build():
        def put_tails(base, rope, mask):
            kc[0, base : base + block, NOPE:] = jnp.concatenate([rope, mask], axis=1)
            kc[1, base : base + block, NOPE:] = jnp.concatenate([mask, rope], axis=1)

        lane = lax.broadcasted_iota(jnp.int32, (block, ROPE), 1)
        row = lax.broadcasted_iota(jnp.int32, (block, ROPE), 0)
        length = where_ref[where_ref.shape[0] - 1]
        vt[:, :, VDIM:, :] = jnp.ones((2, 2, 16, keys), jnp.bfloat16)
        for i, k in enumerate(steps):
            width = mine[i].shape[1]
            here = pl.multiple_of(sub * width, width)
            there = pl.multiple_of((1 - sub) * width, width)
            base = first + i * chunk
            lat[base : base + chunk, pl.ds(here, width)] = mine[i][:chunk, :]
            lat[base : base + chunk, pl.ds(there, width)] = theirs[i][:chunk, :]
            for c in range(CAP):
                packed = jnp.where(sub == c, mine[i][chunk:, :], theirs[i][chunk:, :])
                rope = jnp.concatenate(
                    [packed[:, j * block : (j + 1) * block] for j in range(width // block)], axis=0
                )
                p = where_ref[k * CAP + c]
                hidden = (lane == 0) & ((p < 0) | (p * block + row >= length))
                put_tails(
                    base + c * block, rope.T, jnp.where(hidden, HIDE, 0.0).astype(jnp.bfloat16)
                )
        if fresh:
            plain = jnp.zeros((block, ROPE), jnp.bfloat16)
            lat[:block, :] = lat_a[...]
            lat[block:chunk, :] = lat_b[...]
            put_tails(0, rope_a[...].T, plain)
            put_tails(block, rope_b[:ROPE, :].T, plain)
            i = lax.broadcasted_iota(jnp.int32, (queries, queries), 0)
            j = lax.broadcasted_iota(jnp.int32, (queries, queries), 1)
            flip = sub * block
            seen = jnp.bitwise_xor(i, flip) <= jnp.bitwise_xor(j, flip)
            bias[...] = jnp.where(seen, 0.0, HIDE)

    def form_keys(role):
        k2 = jnp.dot(lat[...], role[4][...], preferred_element_type=jnp.float32)
        for j in range(2):
            kc[j, :, :NOPE] = k2[:, head(j)].astype(jnp.bfloat16)

    def form_values(role, slot):
        v2 = lax.dot_general(
            role[5][...], lat[...], (((0,), (1,)), ((), ())), preferred_element_type=jnp.float32
        )
        for j in range(2):
            vt[slot, j, :VDIM, :] = v2[j * VDIM : (j + 1) * VDIM].astype(jnp.bfloat16)

    def form_scores(role, slot, j):
        qn_a, qr_a, qn_b, qr_b = role[:4]
        lane = lax.broadcasted_iota(jnp.int32, (queries, LANES), 1)
        qn = jnp.concatenate([qn_a[:, head(j)], qn_b[:, head(j)]], axis=0)
        qr = jnp.concatenate([qr_a[...], qr_b[...]], axis=0)
        fill = jnp.where(lane == (1 - j) * ROPE, 1.0, 0.0).astype(jnp.bfloat16)
        own = (lane >= ROPE) if j else (lane < ROPE)
        qc = jnp.concatenate([qn, jnp.where(own, qr, fill)], axis=1)
        s = lax.dot_general(
            kc[j], qc, (((1,), (1,)), ((), ())), preferred_element_type=jnp.float32
        )
        if fresh:
            s = jnp.concatenate([s[:queries] + bias[...], s[queries:]], axis=0)
        score[slot, j] = s
        most = jnp.max(s, axis=0, keepdims=True)
        peak[slot, j] = jnp.broadcast_to(most, (8, queries))

    def before(slot, j):
        rows = slice((slot * 2 + j) * 8, (slot * 2 + j) * 8 + 1)
        return stat_ref[rows, :]

    def form_weights(slot, j):
        most = peak[slot, j, :1, :]
        if not fresh:
            most = jnp.maximum(most, before(slot, j))
        weight[slot, j] = jnp.exp2((score[slot, j] - most) * RATE).astype(jnp.bfloat16)

    def form_output(slot, j):
        o = jnp.dot(vt[slot, j], weight[slot, j], preferred_element_type=jnp.float32)
        o, norm = o[:VDIM], o[VDIM : VDIM + 1]
        index = slot * 2 + j
        if fresh:
            acc_ref[index * VDIM : (index + 1) * VDIM, :] = o
            row = lax.broadcasted_iota(jnp.int32, (8, queries), 0)
            stat_ref[index * 8 : (index + 1) * 8, :] = jnp.where(row == 0, peak[slot, j], norm)
        else:
            old = before(slot, j)
            most = jnp.maximum(peak[slot, j, :1, :], old)
            keep = jnp.exp2((old - most) * RATE)
            norm = norm + keep * stat_ref[index * 8 + 1 : index * 8 + 2, :]
            o = (o + keep * acc_ref[index * VDIM : (index + 1) * VDIM, :]) / norm
            o = o.T.astype(jnp.bfloat16)
            out_ref[:, head(index)] = o[:block]
            send_ref[:, head(index)] = o[block:]

    def both(slot, role):
        form_weights(slot, 0)
        form_weights(slot, 1)
        if role is not None:
            form_keys(role)
            form_values(role, 1 - slot)
        for j in range(2):
            form_output(slot, j)
            if role is not None:
                form_scores(role, 1 - slot, j)

    @pl.when(t == 0)
    def _():
        build()
        form_keys(lead)
        form_values(lead, 0)
        for j in range(2):
            form_scores(lead, 0, j)

    @pl.when(t < halves - 1)
    def _():
        both(0, odd)
        both(1, even)

    @pl.when(t == halves - 1)
    def _():
        both(0, odd)
        both(1, None)


def attend(steps, sub, where, mine, theirs, new_latent, rope_turned, q_nope, q_rope,
           other, w_uk, w_uv, state):
    fresh = state is None
    block, latent = new_latent.shape
    heads = w_uk.shape[1] // NOPE // 2
    pairs = heads // 2
    halves = pairs // 2
    keys = (len(steps) + (1 if fresh else 0)) * CAP * block
    whole = lambda a: pl.BlockSpec(a.shape, lambda t, *_: (0,) * a.ndim)
    nope_at = latent
    rope_at = nope_at + heads * NOPE
    tail_at = rope_at + heads * ROPE

    def at(width, first):
        return pl.BlockSpec((block, width), lambda t, *_: (0, first // width))

    def follow(width, first, pair):
        return pl.BlockSpec((block, width), lambda t, *_: (0, first // width + pair(t)))

    def ours(rows, width, pair):
        return pl.BlockSpec((rows, width), lambda t, s, *_: (0, s[0] * pairs + pair(t)))

    specs = [whole(a) for a in mine] + [whole(a) for a in theirs]
    args = [*mine, *theirs]
    if fresh:
        specs += [whole(new_latent), whole(rope_turned), at(latent, 0), at(LANES, tail_at)]
        args += [new_latent, rope_turned, other, other]
    for pair in (
        lambda t: 0 * t,
        lambda t: 2 * t + 1,
        lambda t: jnp.minimum(2 * t + 2, pairs - 1),
    ):
        specs += [
            ours(block, 2 * NOPE, pair),
            ours(block, 2 * ROPE, pair),
            follow(2 * NOPE, nope_at, pair),
            follow(2 * ROPE, rope_at, pair),
            ours(latent, 2 * NOPE, pair),
            ours(latent, 2 * VDIM, pair),
        ]
        args += [q_nope, q_rope, other, other, w_uk, w_uv]
    tall = lambda rows: pl.BlockSpec((rows, 2 * block), lambda t, *_: (t, 0))
    state_specs = [tall(4 * VDIM), tall(32)]
    scratch = [
        pltpu.VMEM((keys, latent), jnp.bfloat16),
        pltpu.VMEM((2, keys, NOPE + LANES), jnp.bfloat16),
        pltpu.VMEM((2, 2, VDIM + 16, keys), jnp.bfloat16),
        pltpu.VMEM((2, 2, keys, 2 * block), jnp.float32),
        pltpu.VMEM((2, 2, keys, 2 * block), jnp.bfloat16),
        pltpu.VMEM((2, 2, 8, 2 * block), jnp.float32),
    ]
    if fresh:
        out_specs = state_specs
        out_shape = [
            jax.ShapeDtypeStruct((heads * VDIM, 2 * block), jnp.float32),
            jax.ShapeDtypeStruct((heads * 8, 2 * block), jnp.float32),
        ]
        scratch.append(pltpu.VMEM((2 * block, 2 * block), jnp.float32))
    else:
        specs += state_specs
        args += state
        out_specs = [
            pl.BlockSpec((block, 4 * VDIM), lambda t, s, *_: (0, s[0] * halves + t)),
            pl.BlockSpec((block, 4 * VDIM), lambda t, *_: (0, t)),
        ]
        out_shape = [
            jax.ShapeDtypeStruct((block, 2 * heads * VDIM), jnp.bfloat16),
            jax.ShapeDtypeStruct((block, heads * VDIM), jnp.bfloat16),
        ]
    return pl.pallas_call(
        functools.partial(attend_kernel, steps, fresh, halves),
        grid_spec=pltpu.PrefetchScalarGridSpec(
            num_scalar_prefetch=2,
            grid=(halves,),
            in_specs=specs,
            out_specs=out_specs,
            scratch_shapes=scratch,
        ),
        out_shape=out_shape,
        compiler_params=pltpu.CompilerParams(vmem_limit_bytes=(40 if len(steps) < 8 else 60) << 20),
        cost_estimate=pl.CostEstimate(
            flops=4 * keys * latent * heads * NOPE + 8 * block * keys * heads * 256,
            bytes_accessed=8 * 1024 * 1024,
            transcendentals=2 * block * keys * heads,
        ),
        name="attend_new" if fresh else "attend_prefix",
    )(sub, where, *args)


def shards(
    q_nope,
    q_rope,
    new_latent,
    new_rope,
    pool_latent,
    pool_rope,
    w_uk,
    w_uv,
    block_list,
    prefix_len,
    block_slot,
):
    n = lax.axis_size("req")
    sub = lax.axis_index("sub")
    half = q_nope.shape[1] // 2
    swap = lambda a: lax.ppermute(a, "sub", [(0, 1), (1, 0)])
    cross = lambda a, k: lax.ppermute(a, "req", [(i, i ^ k) for i in range(n)])
    far = list(range(n - 1, 0, -1))
    keep = lambda a: pltpu.with_memory_space_constraint(a, pltpu.HBM)
    q_nope, q_rope, new_latent, w_uk, w_uv = map(keep, (q_nope, q_rope, new_latent, w_uk, w_uv))
    pool_latent = keep(pool_latent)
    slots = keep(block_slot)
    pool_turned = keep(pool_rope.swapaxes(1, 2))
    rope_turned = keep(new_rope.T)
    got = {k: cross(block_list, k) for k in far}
    lists = [keep(block_list)] + [got[k] for k in range(1, n)]
    other = prepare(new_latent, q_nope, q_rope, rope_turned)
    other = swap(other)
    sent, where = pack(n, lists, slots, prefix_len, pool_latent, pool_turned)
    local = swap(sent[0])
    mine = [cross(sent[k], k) for k in far]
    theirs = [swap(a) for a in mine]
    common = (new_latent, rope_turned, q_nope, q_rope, other, w_uk, w_uv)
    state = attend([0], sub.reshape(1), where, [sent[0]], [local], *common, None)
    kept, gone = attend(far, sub.reshape(1), where, mine, theirs, *common, state)
    back = swap(gone)
    return lax.dynamic_update_slice_in_dim(kept, back, (1 - sub) * half, 1)


def solution(mesh):
    placed = (
        P(("groups", "req", "sub"), "head"),
        P(("groups", "req", "sub"), "head"),
        P(("groups", "req", "sub"), None),
        P(("groups", "req", "sub"), None),
        P(("groups", "req"), None, "sub"),
        P(("groups", "req"), None, None),
        P(None, "head"),
        P(None, "head"),
        P(("groups", "req"), None),
        P(("groups", "req")),
        P("groups"),
    )
    return jax.shard_map(
        shards,
        mesh=mesh,
        in_specs=placed,
        out_specs=P(("groups", "req", "sub"), "head"),
        check_vma=False,
    )
```

```python
import functools
import math

import jax
import jax.numpy as jnp
from jax import lax
from jax.experimental import pallas as pl
from jax.experimental.pallas import tpu as pltpu
from jax.sharding import PartitionSpec as P


NOPE = 128
ROPE = 64
VDIM = 128
CAP = 2
LANES = 128
HIDE = -1e30


def pack_kernel(n, blocks, pool_local, lists, slots_ref, len_ref, pool_ref, rope_ref, outs, where_ref,
                index_ref, count_ref, lat_sem, rope_sem):
    me = lax.axis_index("req")
    sub = lax.axis_index("sub")
    block = pool_ref.shape[1]
    width = pool_ref.shape[2]
    for i in range(n * CAP):
        index_ref[i] = 0
        where_ref[i] = -1
    where_ref[n * CAP] = len_ref[0]
    for i in range(n):
        count_ref[i] = 0
    parts = width // block
    rows = ROPE // parts
    copies = []
    for k in [*range(1, n), 0]:
        found = jnp.int32(0)
        for p in range(blocks):
            physical = slots_ref[lists[k][0, p]]
            owner = physical // pool_local
            mine = owner == me

            @pl.when(mine)
            def _():
                index_ref[k * CAP + found] = physical - owner * pool_local

            found = found + mine.astype(jnp.int32)
            if k == 0:
                step = jnp.bitwise_xor(me, owner)
                earlier = count_ref[step]
                where_ref[step * CAP + earlier] = p
                count_ref[step] = earlier + 1
        batch = [
            pltpu.make_async_copy(
                pool_ref.at[index_ref[k * CAP + c]],
                outs[k].at[pl.ds(c * block, block)],
                lat_sem.at[k * CAP + c],
            )
            for c in range(CAP)
        ] + [
            pltpu.make_async_copy(
                rope_ref.at[index_ref[k * CAP + sub], pl.ds(i * rows, rows)],
                outs[k].at[pl.ds(CAP * block, rows), pl.ds(i * block, block)],
                rope_sem.at[k * parts + i],
            )
            for i in range(parts)
        ]
        for copy in batch:
            copy.start()
        copies += batch
    for copy in copies:
        copy.wait()


def pack(n, lists, block_slot, prefix_len, pool_latent, rope_turned):
    pool_local, block, width = pool_latent.shape
    blocks = lists[0].shape[1]
    rows = CAP * block + block * ROPE // width
    vmem = pl.BlockSpec(memory_space=pltpu.VMEM)
    smem = pl.BlockSpec(memory_space=pltpu.SMEM)

    def body(*refs):
        pack_kernel(
            n, blocks, pool_local, refs[:n], *refs[n : n + 4],
            refs[n + 4 : 2 * n + 4], *refs[2 * n + 4 :],
        )

    out = pl.pallas_call(
        body,
        out_shape=[jax.ShapeDtypeStruct((rows, width), jnp.bfloat16)] * n
        + [jax.ShapeDtypeStruct((n * CAP + 1,), jnp.int32)],
        in_specs=[smem] * (n + 2) + [pl.BlockSpec(memory_space=pl.ANY)] * 2,
        out_specs=[vmem] * n + [smem],
        scratch_shapes=[
            pltpu.SMEM((n * CAP,), jnp.int32),
            pltpu.SMEM((n,), jnp.int32),
            pltpu.SemaphoreType.DMA((n * CAP,)),
            pltpu.SemaphoreType.DMA((n * width // block,)),
        ],
        compiler_params=pltpu.CompilerParams(vmem_limit_bytes=16 << 20),
        cost_estimate=pl.CostEstimate(flops=0, bytes_accessed=4 * n * rows * width, transcendentals=0),
        name="pack",
    )(*lists, block_slot, prefix_len, pool_latent, rope_turned)
    return out[:n], out[n]


def prepare_kernel(len_ref, lat_ref, qn_ref, qr_ref, rope_ref, out_ref, kept_ref, sem):
    kept_ref[0] = len_ref[0]
    there = 1 - lax.axis_index("sub")
    latent = lat_ref.shape[1]
    half = qn_ref.shape[1] // 2
    rope_half = qr_ref.shape[1] // 2
    tail = latent + half + rope_half
    copies = [
        pltpu.make_async_copy(lat_ref, out_ref.at[:, pl.ds(0, latent)], sem.at[0]),
        pltpu.make_async_copy(
            qn_ref.at[:, pl.ds(pl.multiple_of(there * half, LANES), half)],
            out_ref.at[:, pl.ds(latent, half)],
            sem.at[1],
        ),
        pltpu.make_async_copy(
            qr_ref.at[:, pl.ds(pl.multiple_of(there * rope_half, LANES), rope_half)],
            out_ref.at[:, pl.ds(latent + half, rope_half)],
            sem.at[2],
        ),
        pltpu.make_async_copy(
            rope_ref, out_ref.at[pl.ds(0, ROPE), pl.ds(tail, rope_ref.shape[1])], sem.at[3]
        ),
    ]
    for copy in copies:
        copy.start()
    for copy in copies:
        copy.wait()


def prepare(prefix_len, new_latent, q_nope, q_rope, rope_turned):
    rows, latent = new_latent.shape
    width = latent + q_nope.shape[1] // 2 + q_rope.shape[1] // 2 + rows
    return pl.pallas_call(
        prepare_kernel,
        out_shape=[
            jax.ShapeDtypeStruct((rows, width), jnp.bfloat16),
            jax.ShapeDtypeStruct((1,), jnp.int32),
        ],
        in_specs=[pl.BlockSpec(memory_space=pltpu.SMEM)] + [pl.BlockSpec(memory_space=pl.ANY)] * 4,
        out_specs=[pl.BlockSpec(memory_space=pltpu.VMEM), pl.BlockSpec(memory_space=pltpu.SMEM)],
        scratch_shapes=[pltpu.SemaphoreType.DMA((4,))],
        compiler_params=pltpu.CompilerParams(vmem_limit_bytes=16 << 20),
        cost_estimate=pl.CostEstimate(flops=0, bytes_accessed=4 * rows * width, transcendentals=0),
        name="prepare",
    )(prefix_len, new_latent, q_nope, q_rope, rope_turned)


RATE = math.log2(math.e) / math.sqrt(NOPE + ROPE)


def attend_kernel(steps, fresh, halves, sub_ref, where_ref, *refs):
    count = len(steps)
    mine = refs[:count]
    theirs = refs[count : 2 * count]
    refs = refs[2 * count :]
    if fresh:
        lat_a, rope_a, lat_b, rope_b, *refs = refs
    lead, odd, even = refs[:6], refs[6:12], refs[12:18]
    if fresh:
        acc_ref, stat_ref, lat, kc, vt, score, weight, peak, bias = refs[18:]
    else:
        acc_ref, stat_ref, out_ref, send_ref, lat, kc, vt, score, weight, peak = refs[18:]
    sub = sub_ref[0]
    block = lead[0].shape[0]
    chunk = CAP * block
    first = chunk if fresh else 0
    queries = 2 * block
    keys = lat.shape[0]
    t = pl.program_id(0)
    head = lambda j: slice(j * LANES, (j + 1) * LANES)

    def build():
        def put_tails(base, rope, mask):
            kc[0, base : base + block, NOPE:] = jnp.concatenate([rope, mask], axis=1)
            kc[1, base : base + block, NOPE:] = jnp.concatenate([mask, rope], axis=1)

        lane = lax.broadcasted_iota(jnp.int32, (block, ROPE), 1)
        row = lax.broadcasted_iota(jnp.int32, (block, ROPE), 0)
        length = where_ref[where_ref.shape[0] - 1]
        vt[:, :, VDIM:, :] = jnp.ones((2, 2, 16, keys), jnp.bfloat16)
        for i, k in enumerate(steps):
            width = mine[i].shape[1]
            here = pl.multiple_of(sub * width, width)
            there = pl.multiple_of((1 - sub) * width, width)
            base = first + i * chunk
            lat[base : base + chunk, pl.ds(here, width)] = mine[i][:chunk, :]
            lat[base : base + chunk, pl.ds(there, width)] = theirs[i][:chunk, :]
            for c in range(CAP):
                packed = jnp.where(sub == c, mine[i][chunk:, :], theirs[i][chunk:, :])
                rope = jnp.concatenate(
                    [packed[:, j * block : (j + 1) * block] for j in range(width // block)], axis=0
                )
                p = where_ref[k * CAP + c]
                hidden = (lane == 0) & ((p < 0) | (p * block + row >= length))
                put_tails(
                    base + c * block, rope.T, jnp.where(hidden, HIDE, 0.0).astype(jnp.bfloat16)
                )
        if fresh:
            plain = jnp.zeros((block, ROPE), jnp.bfloat16)
            lat[:block, :] = lat_a[...]
            lat[block:chunk, :] = lat_b[...]
            put_tails(0, rope_a[...].T, plain)
            put_tails(block, rope_b[:ROPE, :].T, plain)
            i = lax.broadcasted_iota(jnp.int32, (queries, queries), 0)
            j = lax.broadcasted_iota(jnp.int32, (queries, queries), 1)
            flip = sub * block
            seen = jnp.bitwise_xor(i, flip) <= jnp.bitwise_xor(j, flip)
            bias[...] = jnp.where(seen, 0.0, HIDE)

    def form_keys(role):
        for r in range(0, keys, chunk):
            rows = slice(r, r + chunk)
            k2 = jnp.dot(lat[rows, :], role[4][...], preferred_element_type=jnp.float32)
            for j in range(2):
                kc[j, rows, :NOPE] = k2[:, head(j)].astype(jnp.bfloat16)

    def form_values(role, slot):
        v2 = lax.dot_general(
            role[5][...], lat[...], (((0,), (1,)), ((), ())), preferred_element_type=jnp.float32
        )
        for j in range(2):
            vt[slot, j, :VDIM, :] = v2[j * VDIM : (j + 1) * VDIM].astype(jnp.bfloat16)

    def form_scores(role, slot, j):
        qn_a, qr_a, qn_b, qr_b = role[:4]
        lane = lax.broadcasted_iota(jnp.int32, (queries, LANES), 1)
        qn = jnp.concatenate([qn_a[:, head(j)], qn_b[:, head(j)]], axis=0)
        qr = jnp.concatenate([qr_a[...], qr_b[...]], axis=0)
        fill = jnp.where(lane == (1 - j) * ROPE, 1.0, 0.0).astype(jnp.bfloat16)
        own = (lane >= ROPE) if j else (lane < ROPE)
        qc = jnp.concatenate([qn, jnp.where(own, qr, fill)], axis=1)
        s = lax.dot_general(
            kc[j], qc, (((1,), (1,)), ((), ())), preferred_element_type=jnp.float32
        )
        if fresh:
            s = jnp.concatenate([s[:queries] + bias[...], s[queries:]], axis=0)
        score[slot, j] = s
        most = jnp.max(s, axis=0, keepdims=True)
        peak[slot, j] = jnp.broadcast_to(most, (8, queries))

    def before(slot, j):
        rows = slice((slot * 2 + j) * 8, (slot * 2 + j) * 8 + 1)
        return stat_ref[rows, :]

    def form_weights(slot, j):
        most = peak[slot, j, :1, :]
        if not fresh:
            most = jnp.maximum(most, before(slot, j))
        weight[slot, j] = jnp.exp2((score[slot, j] - most) * RATE).astype(jnp.bfloat16)

    def form_output(slot, j):
        o = jnp.dot(vt[slot, j], weight[slot, j], preferred_element_type=jnp.float32)
        o, norm = o[:VDIM], o[VDIM : VDIM + 1]
        index = slot * 2 + j
        if fresh:
            acc_ref[index * VDIM : (index + 1) * VDIM, :] = o
            row = lax.broadcasted_iota(jnp.int32, (8, queries), 0)
            stat_ref[index * 8 : (index + 1) * 8, :] = jnp.where(row == 0, peak[slot, j], norm)
        else:
            old = before(slot, j)
            most = jnp.maximum(peak[slot, j, :1, :], old)
            keep = jnp.exp2((old - most) * RATE)
            norm = norm + keep * stat_ref[index * 8 + 1 : index * 8 + 2, :]
            o = (o + keep * acc_ref[index * VDIM : (index + 1) * VDIM, :]) / norm
            o = o.T.astype(jnp.bfloat16)
            out_ref[:, head(index)] = o[:block]
            send_ref[:, head(index)] = o[block:]

    def both(slot, role):
        form_weights(slot, 0)
        form_weights(slot, 1)
        if role is not None:
            form_keys(role)
            form_values(role, 1 - slot)
        for j in range(2):
            form_output(slot, j)
            if role is not None:
                form_scores(role, 1 - slot, j)

    @pl.when(t == 0)
    def _():
        build()
        form_keys(lead)
        form_values(lead, 0)
        for j in range(2):
            form_scores(lead, 0, j)

    @pl.when(t < halves - 1)
    def _():
        both(0, odd)
        both(1, even)

    @pl.when(t == halves - 1)
    def _():
        both(0, odd)
        both(1, None)


def attend(steps, sub, where, mine, theirs, new_latent, rope_turned, q_nope, q_rope,
           other, w_uk, w_uv, state):
    fresh = state is None
    block, latent = new_latent.shape
    heads = w_uk.shape[1] // NOPE // 2
    pairs = heads // 2
    halves = pairs // 2
    keys = (len(steps) + (1 if fresh else 0)) * CAP * block
    whole = lambda a: pl.BlockSpec(a.shape, lambda t, *_: (0,) * a.ndim)
    nope_at = latent
    rope_at = nope_at + heads * NOPE
    tail_at = rope_at + heads * ROPE

    def at(width, first):
        return pl.BlockSpec((block, width), lambda t, *_: (0, first // width))

    def follow(width, first, pair):
        return pl.BlockSpec((block, width), lambda t, *_: (0, first // width + pair(t)))

    def ours(rows, width, pair):
        return pl.BlockSpec((rows, width), lambda t, s, *_: (0, s[0] * pairs + pair(t)))

    specs = [pl.BlockSpec(memory_space=pltpu.VMEM)] * (2 * len(steps))
    args = [*mine, *theirs]
    if fresh:
        specs += [whole(new_latent), whole(rope_turned), at(latent, 0), at(LANES, tail_at)]
        args += [new_latent, rope_turned, other, other]
    for pair in (
        lambda t: 0 * t,
        lambda t: 2 * t + 1,
        lambda t: jnp.minimum(2 * t + 2, pairs - 1),
    ):
        specs += [
            ours(block, 2 * NOPE, pair),
            ours(block, 2 * ROPE, pair),
            follow(2 * NOPE, nope_at, pair),
            follow(2 * ROPE, rope_at, pair),
            ours(latent, 2 * NOPE, pair),
            ours(latent, 2 * VDIM, pair),
        ]
        args += [q_nope, q_rope, other, other, w_uk, w_uv]
    tall = lambda rows: pl.BlockSpec((rows, 2 * block), lambda t, *_: (t, 0))
    state_specs = [tall(4 * VDIM), tall(32)]
    scratch = [
        pltpu.VMEM((keys, latent), jnp.bfloat16),
        pltpu.VMEM((2, keys, NOPE + LANES), jnp.bfloat16),
        pltpu.VMEM((2, 2, VDIM + 16, keys), jnp.bfloat16),
        pltpu.VMEM((2, 2, keys, 2 * block), jnp.float32),
        pltpu.VMEM((2, 2, keys, 2 * block), jnp.bfloat16),
        pltpu.VMEM((2, 2, 8, 2 * block), jnp.float32),
    ]
    if fresh:
        out_specs = state_specs
        out_shape = [
            jax.ShapeDtypeStruct((heads * VDIM, 2 * block), jnp.float32),
            jax.ShapeDtypeStruct((heads * 8, 2 * block), jnp.float32),
        ]
        scratch.append(pltpu.VMEM((2 * block, 2 * block), jnp.float32))
    else:
        specs += state_specs
        args += state
        out_specs = [
            pl.BlockSpec((block, 4 * VDIM), lambda t, s, *_: (0, s[0] * halves + t)),
            pl.BlockSpec((block, 4 * VDIM), lambda t, *_: (0, t)),
        ]
        out_shape = [
            jax.ShapeDtypeStruct((block, 2 * heads * VDIM), jnp.bfloat16),
            jax.ShapeDtypeStruct((block, heads * VDIM), jnp.bfloat16),
        ]
    return pl.pallas_call(
        functools.partial(attend_kernel, steps, fresh, halves),
        grid_spec=pltpu.PrefetchScalarGridSpec(
            num_scalar_prefetch=2,
            grid=(halves,),
            in_specs=specs,
            out_specs=out_specs,
            scratch_shapes=scratch,
        ),
        out_shape=out_shape,
        compiler_params=pltpu.CompilerParams(vmem_limit_bytes=(40 if len(steps) < 8 else 60) << 20),
        cost_estimate=pl.CostEstimate(
            flops=4 * keys * latent * heads * NOPE + 8 * block * keys * heads * 256,
            bytes_accessed=8 * 1024 * 1024,
            transcendentals=2 * block * keys * heads,
        ),
        name="attend_new" if fresh else "attend_prefix",
    )(sub, where, *args)


def join_kernel(kept_ref, back_ref, out_ref, sem):
    there = 1 - lax.axis_index("sub")
    half = back_ref.shape[1]
    copy = pltpu.make_async_copy(
        back_ref, out_ref.at[:, pl.ds(pl.multiple_of(there * half, LANES), half)], sem
    )
    copy.start()
    copy.wait()


def join(kept, back):
    return pl.pallas_call(
        join_kernel,
        out_shape=jax.ShapeDtypeStruct(kept.shape, kept.dtype),
        in_specs=[pl.BlockSpec(memory_space=pl.ANY)] * 2,
        out_specs=pl.BlockSpec(memory_space=pl.ANY),
        scratch_shapes=[pltpu.SemaphoreType.DMA(())],
        input_output_aliases={0: 0},
        compiler_params=pltpu.CompilerParams(vmem_limit_bytes=1 << 20),
        name="join",
    )(kept, back)


def shards(
    q_nope,
    q_rope,
    new_latent,
    new_rope,
    pool_latent,
    pool_rope,
    w_uk,
    w_uv,
    block_list,
    prefix_len,
    block_slot,
):
    n = lax.axis_size("req")
    sub = lax.axis_index("sub")
    swap = lambda a: lax.ppermute(a, "sub", [(0, 1), (1, 0)])
    cross = lambda a, k: lax.ppermute(a, "req", [(i, i ^ k) for i in range(n)])
    far = list(range(n - 1, 0, -1))
    keep = lambda a: pltpu.with_memory_space_constraint(a, pltpu.HBM)
    q_nope, q_rope, new_latent, w_uk, w_uv = map(keep, (q_nope, q_rope, new_latent, w_uk, w_uv))
    pool_latent = keep(pool_latent)
    slots = keep(block_slot)
    pool_turned = keep(pool_rope.swapaxes(1, 2))
    rope_turned = keep(new_rope.T)
    got = {}
    for k in far:
        got[k] = cross(block_list, k)
    lists = [keep(block_list)] + [got[k] for k in range(1, n)]
    other, length = prepare(prefix_len, new_latent, q_nope, q_rope, rope_turned)
    other = swap(other)
    sent, where = pack(n, lists, slots, length, pool_latent, pool_turned)
    local = swap(sent[0])
    mine = []
    for k in far:
        mine.append(cross(sent[k], k))
    theirs = []
    for k, a in zip(far, mine):
        theirs.append(swap(a))
    common = (new_latent, rope_turned, q_nope, q_rope, other, w_uk, w_uv)
    state = attend([0], sub.reshape(1), where, [sent[0]], [local], *common, None)
    kept, gone = attend(far, sub.reshape(1), where, mine, theirs, *common, state)
    back = swap(gone)
    return join(kept, back)


def solution(mesh):
    placed = (
        P(("groups", "req", "sub"), "head"),
        P(("groups", "req", "sub"), "head"),
        P(("groups", "req", "sub"), None),
        P(("groups", "req", "sub"), None),
        P(("groups", "req"), None, "sub"),
        P(("groups", "req"), None, None),
        P(None, "head"),
        P(None, "head"),
        P(("groups", "req"), None),
        P(("groups", "req")),
        P("groups"),
    )
    return jax.shard_map(
        shards,
        mesh=mesh,
        in_specs=placed,
        out_specs=P(("groups", "req", "sub"), "head"),
        check_vma=False,
    )
```

```python
import functools
import math

import jax
import jax.numpy as jnp
from jax import lax
from jax.experimental import pallas as pl
from jax.experimental.pallas import tpu as pltpu
from jax.sharding import PartitionSpec as P


NOPE = 128
ROPE = 64
VDIM = 128
CAP = 2
LANES = 128
HIDE = -1e30


def pack_kernel(n, blocks, pool_local, lists, slots_ref, len_ref, pool_ref, rope_ref, outs, where_ref,
                index_ref, count_ref, lat_sem, rope_sem):
    me = lax.axis_index("req")
    sub = lax.axis_index("sub")
    block = pool_ref.shape[1]
    width = pool_ref.shape[2]
    for i in range(n * CAP):
        index_ref[i] = 0
        where_ref[i] = -1
    where_ref[n * CAP] = len_ref[0]
    for i in range(n):
        count_ref[i] = 0
    for k in range(n):
        found = jnp.int32(0)
        for p in range(blocks):
            physical = slots_ref[lists[k][0, p]]
            owner = physical // pool_local
            mine = owner == me

            @pl.when(mine)
            def _():
                index_ref[k * CAP + found] = physical - owner * pool_local

            found = found + mine.astype(jnp.int32)
            if k == 0:
                step = jnp.bitwise_xor(me, owner)
                earlier = count_ref[step]
                where_ref[step * CAP + earlier] = p
                count_ref[step] = earlier + 1
    parts = width // block
    rows = ROPE // parts
    copies = []
    for k in range(n):
        for c in range(CAP):
            copies.append(pltpu.make_async_copy(
                pool_ref.at[index_ref[k * CAP + c]],
                outs[k].at[pl.ds(c * block, block)],
                lat_sem.at[k * CAP + c],
            ))
        for i in range(parts):
            copies.append(pltpu.make_async_copy(
                rope_ref.at[index_ref[k * CAP + sub], pl.ds(i * rows, rows)],
                outs[k].at[pl.ds(CAP * block, rows), pl.ds(i * block, block)],
                rope_sem.at[k * parts + i],
            ))
    for copy in copies:
        copy.start()
    for copy in copies:
        copy.wait()


def pack(n, lists, block_slot, prefix_len, pool_latent, rope_turned):
    pool_local, block, width = pool_latent.shape
    blocks = lists[0].shape[1]
    rows = CAP * block + block * ROPE // width
    vmem = pl.BlockSpec(memory_space=pltpu.VMEM)
    smem = pl.BlockSpec(memory_space=pltpu.SMEM)

    def body(*refs):
        pack_kernel(
            n, blocks, pool_local, refs[:n], *refs[n : n + 4],
            refs[n + 4 : 2 * n + 4], *refs[2 * n + 4 :],
        )

    out = pl.pallas_call(
        body,
        out_shape=[jax.ShapeDtypeStruct((rows, width), jnp.bfloat16)] * n
        + [jax.ShapeDtypeStruct((n * CAP + 1,), jnp.int32)],
        in_specs=[smem] * (n + 2) + [pl.BlockSpec(memory_space=pl.ANY)] * 2,
        out_specs=[vmem] * n + [smem],
        scratch_shapes=[
            pltpu.SMEM((n * CAP,), jnp.int32),
            pltpu.SMEM((n,), jnp.int32),
            pltpu.SemaphoreType.DMA((n * CAP,)),
            pltpu.SemaphoreType.DMA((n * width // block,)),
        ],
        compiler_params=pltpu.CompilerParams(vmem_limit_bytes=16 << 20),
        cost_estimate=pl.CostEstimate(flops=0, bytes_accessed=4 * n * rows * width, transcendentals=0),
        name="pack",
    )(*lists, block_slot, prefix_len, pool_latent, rope_turned)
    return out[:n], out[n]


def prepare_kernel(len_ref, lat_ref, qn_ref, qr_ref, rope_ref, wk_ref, wv_ref,
                   out_ref, qn_out, qr_out, wk_out, wv_out, kept_ref, sem):
    kept_ref[0] = len_ref[0]
    sub = lax.axis_index("sub")
    latent = lat_ref.shape[1]
    tail = out_ref.shape[1] - rope_ref.shape[1]

    def part(ref, which):
        half = ref.shape[1] // 2
        return ref.at[:, pl.ds(pl.multiple_of(which * half, LANES), half)]

    half = qn_out.shape[1]
    rope_half = qr_out.shape[1]
    moves = [
        (lat_ref, out_ref.at[:, pl.ds(0, latent)]),
        (part(qn_ref, 1 - sub), out_ref.at[:, pl.ds(latent, half)]),
        (part(qr_ref, 1 - sub), out_ref.at[:, pl.ds(latent + half, rope_half)]),
        (rope_ref, out_ref.at[pl.ds(0, ROPE), pl.ds(tail, rope_ref.shape[1])]),
        (part(qn_ref, sub), qn_out),
        (part(qr_ref, sub), qr_out),
        (part(wk_ref, sub), wk_out),
        (part(wv_ref, sub), wv_out),
    ]
    copies = [pltpu.make_async_copy(*move, sem.at[i]) for i, move in enumerate(moves)]
    for copy in copies:
        copy.start()
    for copy in copies:
        copy.wait()


def prepare(prefix_len, new_latent, q_nope, q_rope, rope_turned, w_uk, w_uv):
    rows, latent = new_latent.shape
    half = q_nope.shape[1] // 2
    rope_half = q_rope.shape[1] // 2
    shapes = [
        (rows, latent + half + rope_half + rows),
        (rows, half),
        (rows, rope_half),
        (latent, half),
        (latent, half),
    ]
    return pl.pallas_call(
        prepare_kernel,
        out_shape=[jax.ShapeDtypeStruct(shape, jnp.bfloat16) for shape in shapes]
        + [jax.ShapeDtypeStruct((1,), jnp.int32)],
        in_specs=[pl.BlockSpec(memory_space=pltpu.SMEM)] + [pl.BlockSpec(memory_space=pl.ANY)] * 6,
        out_specs=[pl.BlockSpec(memory_space=pltpu.VMEM)] * 5
        + [pl.BlockSpec(memory_space=pltpu.SMEM)],
        scratch_shapes=[pltpu.SemaphoreType.DMA((8,))],
        compiler_params=pltpu.CompilerParams(vmem_limit_bytes=16 << 20),
        cost_estimate=pl.CostEstimate(
            flops=0, bytes_accessed=4 * sum(math.prod(shape) for shape in shapes), transcendentals=0
        ),
        name="prepare",
    )(prefix_len, new_latent, q_nope, q_rope, rope_turned, w_uk, w_uv)


RATE = math.log2(math.e) / math.sqrt(NOPE + ROPE)


def attend_kernel(steps, fresh, *refs):
    count = len(steps)
    where_ref, lat_a, rope_a, other, qn_ref, qr_ref, wk_ref, wv_ref, *refs = refs
    mine = refs[:count]
    theirs = refs[count : 2 * count]
    refs = refs[2 * count :]
    if fresh:
        acc_ref, stat_ref, lat, kc, vt, score, weight, peak, bias = refs
    else:
        (acc_ref, stat_ref, out_ref, send_ref, lat, kc, vt, score, weight, peak, result,
         sem) = refs
    sub = lax.axis_index("sub")
    block, latent = lat_a.shape
    chunk = CAP * block
    first = chunk if fresh else 0
    queries = 2 * block
    keys = lat.shape[0]
    half = qn_ref.shape[1]
    halves = half // (4 * NOPE)
    nope_at = latent
    rope_at = nope_at + half
    tail_at = rope_at + qr_ref.shape[1]
    head = lambda j: slice(j * LANES, (j + 1) * LANES)
    at = lambda start, size: pl.ds(pl.multiple_of(start, size), size)

    def build():
        def put_tails(base, rope, mask):
            kc[0, base : base + block, NOPE:] = jnp.concatenate([rope, mask], axis=1)
            kc[1, base : base + block, NOPE:] = jnp.concatenate([mask, rope], axis=1)

        lane = lax.broadcasted_iota(jnp.int32, (block, ROPE), 1)
        row = lax.broadcasted_iota(jnp.int32, (block, ROPE), 0)
        length = where_ref[where_ref.shape[0] - 1]
        vt[:, :, VDIM:, :] = jnp.ones((2, 2, 16, keys), jnp.bfloat16)
        for i, k in enumerate(steps):
            width = mine[i].shape[1]
            here = pl.multiple_of(sub * width, width)
            there = pl.multiple_of((1 - sub) * width, width)
            base = first + i * chunk
            lat[base : base + chunk, pl.ds(here, width)] = mine[i][:chunk, :]
            lat[base : base + chunk, pl.ds(there, width)] = theirs[i][:chunk, :]
            for c in range(CAP):
                packed = jnp.where(sub == c, mine[i][chunk:, :], theirs[i][chunk:, :])
                rope = jnp.concatenate(
                    [packed[:, j * block : (j + 1) * block] for j in range(width // block)], axis=0
                )
                p = where_ref[k * CAP + c]
                hidden = (lane == 0) & ((p < 0) | (p * block + row >= length))
                put_tails(
                    base + c * block, rope.T, jnp.where(hidden, HIDE, 0.0).astype(jnp.bfloat16)
                )
        if fresh:
            plain = jnp.zeros((block, ROPE), jnp.bfloat16)
            lat[:block, :] = lat_a[...]
            lat[block:chunk, :] = other[:, :latent]
            put_tails(0, rope_a[...].T, plain)
            put_tails(block, other[:ROPE, tail_at:].T, plain)
            i = lax.broadcasted_iota(jnp.int32, (queries, queries), 0)
            j = lax.broadcasted_iota(jnp.int32, (queries, queries), 1)
            flip = sub * block
            seen = jnp.bitwise_xor(i, flip) <= jnp.bitwise_xor(j, flip)
            bias[...] = jnp.where(seen, 0.0, HIDE)

    def form_keys(pair):
        columns = at(pair * 2 * NOPE, 2 * NOPE)
        for r in range(0, keys, chunk):
            rows = slice(r, r + chunk)
            k2 = jnp.dot(lat[rows, :], wk_ref[:, columns], preferred_element_type=jnp.float32)
            for j in range(2):
                kc[j, rows, :NOPE] = k2[:, head(j)].astype(jnp.bfloat16)

    def form_values(pair, slot):
        v2 = lax.dot_general(
            wv_ref[:, at(pair * 2 * VDIM, 2 * VDIM)], lat[...], (((0,), (1,)), ((), ())),
            preferred_element_type=jnp.float32,
        )
        for j in range(2):
            vt[slot, j, :VDIM, :] = v2[j * VDIM : (j + 1) * VDIM].astype(jnp.bfloat16)

    def form_scores(pair, slot, j):
        lane = lax.broadcasted_iota(jnp.int32, (queries, LANES), 1)
        nope = pair * 2 * NOPE + j * NOPE
        qn = jnp.concatenate(
            [qn_ref[:, at(nope, NOPE)], other[:, at(nope_at + nope, NOPE)]], axis=0
        )
        rope = pair * LANES
        qr = jnp.concatenate(
            [qr_ref[:, at(rope, LANES)], other[:, at(rope_at + rope, LANES)]], axis=0
        )
        fill = jnp.where(lane == (1 - j) * ROPE, 1.0, 0.0).astype(jnp.bfloat16)
        own = (lane >= ROPE) if j else (lane < ROPE)
        qc = jnp.concatenate([qn, jnp.where(own, qr, fill)], axis=1)
        s = lax.dot_general(
            kc[j], qc, (((1,), (1,)), ((), ())), preferred_element_type=jnp.float32
        )
        if fresh:
            s = jnp.concatenate([s[:queries] + bias[...], s[queries:]], axis=0)
        score[slot, j] = s
        most = jnp.max(s, axis=0, keepdims=True)
        peak[slot, j] = jnp.broadcast_to(most, (8, queries))

    def form_weights(pair, slot, j):
        most = peak[slot, j, :1, :]
        if not fresh:
            most = jnp.maximum(most, stat_ref[at((2 * pair + j) * 8, 8), :][:1])
        weight[slot, j] = jnp.exp2((score[slot, j] - most) * RATE).astype(jnp.bfloat16)

    def form_output(pair, slot, j):
        o = jnp.dot(vt[slot, j], weight[slot, j], preferred_element_type=jnp.float32)
        o, norm = o[:VDIM], o[VDIM : VDIM + 1]
        rows = at((2 * pair + j) * VDIM, VDIM)
        stat_rows = at((2 * pair + j) * 8, 8)
        if fresh:
            acc_ref[rows, :] = o
            row = lax.broadcasted_iota(jnp.int32, (8, queries), 0)
            stat_ref[stat_rows, :] = jnp.where(row == 0, peak[slot, j], norm)
        else:
            stat = stat_ref[stat_rows, :]
            old = stat[:1]
            most = jnp.maximum(peak[slot, j, :1, :], old)
            keep = jnp.exp2((old - most) * RATE)
            norm = norm + keep * stat[1:2]
            o = (o + keep * acc_ref[rows, :]) / norm
            o = o.T.astype(jnp.bfloat16)
            columns = at((2 * pair + j) * VDIM, VDIM)
            result[:, columns] = o[:block]
            send_ref[:, columns] = o[block:]

    def both(pair, slot, more=True):
        form_weights(pair, slot, 0)
        form_weights(pair, slot, 1)
        if more:
            form_keys(pair + 1)
            form_values(pair + 1, 1 - slot)
        for j in range(2):
            form_output(pair, slot, j)
            if more:
                form_scores(pair + 1, 1 - slot, j)

    def deliver(t):
        width = 4 * VDIM
        return pltpu.make_async_copy(
            result.at[:, at(t * width, width)],
            out_ref.at[:, at(sub * half + t * width, width)],
            sem.at[t],
        )

    build()
    form_keys(0)
    form_values(0, 0)
    for j in range(2):
        form_scores(0, 0, j)

    def body(t, carry):
        both(2 * t, 0)
        both(2 * t + 1, 1)
        if not fresh:
            deliver(t).start()
        return carry

    if halves > 1:
        lax.fori_loop(0, halves - 1, body, 0)
    both(2 * halves - 2, 0)
    both(2 * halves - 1, 1, False)
    if not fresh:
        deliver(halves - 1).start()
        for t in range(halves):
            deliver(t).wait()


def attend(steps, where, mine, theirs, new_latent, rope_turned, other, qn, qr, wk, wv, state):
    fresh = state is None
    block, latent = new_latent.shape
    heads = wk.shape[1] // NOPE
    keys = (len(steps) + (1 if fresh else 0)) * CAP * block
    vmem = pl.BlockSpec(memory_space=pltpu.VMEM)
    args = [where, new_latent, rope_turned, other, qn, qr, wk, wv, *mine, *theirs]
    specs = [pl.BlockSpec(memory_space=pltpu.SMEM)] + [vmem] * (len(args) - 1)
    scratch = [
        pltpu.VMEM((keys, latent), jnp.bfloat16),
        pltpu.VMEM((2, keys, NOPE + LANES), jnp.bfloat16),
        pltpu.VMEM((2, 2, VDIM + 16, keys), jnp.bfloat16),
        pltpu.VMEM((2, 2, keys, 2 * block), jnp.float32),
        pltpu.VMEM((2, 2, keys, 2 * block), jnp.bfloat16),
        pltpu.VMEM((2, 2, 8, 2 * block), jnp.float32),
    ]
    if fresh:
        out_specs = [vmem, vmem]
        out_shape = [
            jax.ShapeDtypeStruct((heads * VDIM, 2 * block), jnp.float32),
            jax.ShapeDtypeStruct((heads * 8, 2 * block), jnp.float32),
        ]
        scratch.append(pltpu.VMEM((2 * block, 2 * block), jnp.float32))
    else:
        specs += [vmem, vmem]
        args += state
        out_specs = [pl.BlockSpec(memory_space=pl.ANY), vmem]
        out_shape = [
            jax.ShapeDtypeStruct((block, 2 * heads * VDIM), jnp.bfloat16),
            jax.ShapeDtypeStruct((block, heads * VDIM), jnp.bfloat16),
        ]
        scratch += [
            pltpu.VMEM((block, heads * VDIM), jnp.bfloat16),
            pltpu.SemaphoreType.DMA((heads // 4,)),
        ]
    return pl.pallas_call(
        functools.partial(attend_kernel, steps, fresh),
        in_specs=specs,
        out_specs=out_specs,
        scratch_shapes=scratch,
        out_shape=out_shape,
        compiler_params=pltpu.CompilerParams(vmem_limit_bytes=(36 if len(steps) < 8 else 48) << 20),
        cost_estimate=pl.CostEstimate(
            flops=4 * keys * latent * heads * NOPE + 8 * block * keys * heads * 256,
            bytes_accessed=8 * 1024 * 1024,
            transcendentals=2 * block * keys * heads,
        ),
        name="attend_new" if fresh else "attend_prefix",
    )(*args)


def join_kernel(kept_ref, back_ref, out_ref, sem):
    there = 1 - lax.axis_index("sub")
    half = back_ref.shape[1]
    copy = pltpu.make_async_copy(
        back_ref, out_ref.at[:, pl.ds(pl.multiple_of(there * half, LANES), half)], sem
    )
    copy.start()
    copy.wait()


def join(kept, back):
    return pl.pallas_call(
        join_kernel,
        out_shape=jax.ShapeDtypeStruct(kept.shape, kept.dtype),
        in_specs=[pl.BlockSpec(memory_space=pl.ANY)] * 2,
        out_specs=pl.BlockSpec(memory_space=pl.ANY),
        scratch_shapes=[pltpu.SemaphoreType.DMA(())],
        input_output_aliases={0: 0},
        compiler_params=pltpu.CompilerParams(vmem_limit_bytes=1 << 20),
        name="join",
    )(kept, back)


def shards(
    q_nope,
    q_rope,
    new_latent,
    new_rope,
    pool_latent,
    pool_rope,
    w_uk,
    w_uv,
    block_list,
    prefix_len,
    block_slot,
):
    n = lax.axis_size("req")
    swap = lambda a: lax.ppermute(a, "sub", [(0, 1), (1, 0)])
    cross = lambda a, k: lax.ppermute(a, "req", [(i, i ^ k) for i in range(n)])
    far = list(range(n - 1, 0, -1))
    keep = lambda a: pltpu.with_memory_space_constraint(a, pltpu.HBM)
    q_nope, q_rope, new_latent, w_uk, w_uv = map(keep, (q_nope, q_rope, new_latent, w_uk, w_uv))
    pool_latent = keep(pool_latent)
    slots = keep(block_slot)
    pool_turned = keep(pool_rope.swapaxes(1, 2))
    rope_turned = keep(new_rope.T)
    got = {}
    for k in far:
        got[k] = cross(block_list, k)
    lists = [keep(block_list)] + [got[k] for k in range(1, n)]
    other, qn, qr, wk, wv, length = prepare(
        prefix_len, new_latent, q_nope, q_rope, rope_turned, w_uk, w_uv
    )
    other = swap(other)
    sent, where = pack(n, lists, slots, length, pool_latent, pool_turned)
    local = swap(sent[0])
    mine = []
    for k in far:
        mine.append(cross(sent[k], k))
    theirs = []
    for k, a in zip(far, mine):
        theirs.append(swap(a))
    common = (new_latent, rope_turned, other, qn, qr, wk, wv)
    state = attend([0], where, [sent[0]], [local], *common, None)
    kept, gone = attend(far, where, mine, theirs, *common, state)
    back = swap(gone)
    return join(kept, back)


def solution(mesh):
    placed = (
        P(("groups", "req", "sub"), "head"),
        P(("groups", "req", "sub"), "head"),
        P(("groups", "req", "sub"), None),
        P(("groups", "req", "sub"), None),
        P(("groups", "req"), None, "sub"),
        P(("groups", "req"), None, None),
        P(None, "head"),
        P(None, "head"),
        P(("groups", "req"), None),
        P(("groups", "req")),
        P("groups"),
    )
    return jax.shard_map(
        shards,
        mesh=mesh,
        in_specs=placed,
        out_specs=P(("groups", "req", "sub"), "head"),
        check_vma=False,
    )
```

```python
import functools
import math

import jax
import jax.numpy as jnp
from jax import lax
from jax.experimental import pallas as pl
from jax.experimental.pallas import tpu as pltpu
from jax.sharding import PartitionSpec as P


NOPE = 128
ROPE = 64
VDIM = 128
CAP = 2
LANES = 128
HIDE = -1e30


def pack_kernel(n, blocks, pool_local, lists, slots_ref, pool_ref, rope_ref, outs, where_ref,
                index_ref, count_ref, lat_sem, rope_sem):
    me = lax.axis_index("req")
    sub = lax.axis_index("sub")
    block = pool_ref.shape[1]
    width = pool_ref.shape[2]
    for i in range(n * CAP):
        index_ref[i] = 0
        where_ref[i] = -1
    for i in range(n):
        count_ref[i] = 0
    for k in range(n):
        found = jnp.int32(0)
        for p in range(blocks):
            physical = slots_ref[lists[k][0, p]]
            owner = physical // pool_local
            mine = owner == me

            @pl.when(mine)
            def _():
                index_ref[k * CAP + found] = physical - owner * pool_local

            found = found + mine.astype(jnp.int32)
            if k == 0:
                step = jnp.bitwise_xor(me, owner)
                earlier = count_ref[step]
                where_ref[step * CAP + earlier] = p
                count_ref[step] = earlier + 1
    parts = width // block
    rows = ROPE // parts
    copies = []
    for k in range(n):
        for c in range(CAP):
            copies.append(pltpu.make_async_copy(
                pool_ref.at[index_ref[k * CAP + c]],
                outs[k].at[pl.ds(c * block, block)],
                lat_sem.at[k * CAP + c],
            ))
        for i in range(parts):
            copies.append(pltpu.make_async_copy(
                rope_ref.at[index_ref[k * CAP + sub], pl.ds(i * rows, rows)],
                outs[k].at[pl.ds(CAP * block, rows), pl.ds(i * block, block)],
                rope_sem.at[k * parts + i],
            ))
    for copy in copies:
        copy.start()
    for copy in copies:
        copy.wait()


def pack(n, lists, block_slot, pool_latent, rope_turned):
    pool_local, block, width = pool_latent.shape
    blocks = lists[0].shape[1]
    rows = CAP * block + block * ROPE // width
    vmem = pl.BlockSpec(memory_space=pltpu.VMEM)
    smem = pl.BlockSpec(memory_space=pltpu.SMEM)

    def body(*refs):
        pack_kernel(
            n, blocks, pool_local, refs[:n], *refs[n : n + 3],
            refs[n + 3 : 2 * n + 3], *refs[2 * n + 3 :],
        )

    out = pl.pallas_call(
        body,
        out_shape=[jax.ShapeDtypeStruct((rows, width), jnp.bfloat16)] * n
        + [jax.ShapeDtypeStruct((n * CAP,), jnp.int32)],
        in_specs=[smem] * (n + 1) + [pl.BlockSpec(memory_space=pl.ANY)] * 2,
        out_specs=[vmem] * n + [smem],
        scratch_shapes=[
            pltpu.SMEM((n * CAP,), jnp.int32),
            pltpu.SMEM((n,), jnp.int32),
            pltpu.SemaphoreType.DMA((n * CAP,)),
            pltpu.SemaphoreType.DMA((n * width // block,)),
        ],
        compiler_params=pltpu.CompilerParams(vmem_limit_bytes=16 << 20),
        cost_estimate=pl.CostEstimate(flops=0, bytes_accessed=4 * n * rows * width, transcendentals=0),
        name="pack",
    )(*lists, block_slot, pool_latent, rope_turned)
    return out[:n], out[n]


def half_of(ref, which):
    half = ref.shape[1] // 2
    return ref.at[:, pl.ds(pl.multiple_of(which * half, LANES), half)]


def move(moves, sem):
    copies = [pltpu.make_async_copy(*pair, sem.at[i]) for i, pair in enumerate(moves)]
    for copy in copies:
        copy.start()
    for copy in copies:
        copy.wait()


def prepare_kernel(lat_ref, qn_ref, qr_ref, rope_ref, out_ref, sem):
    there = 1 - lax.axis_index("sub")
    latent = lat_ref.shape[1]
    half = qn_ref.shape[1] // 2
    rope_half = qr_ref.shape[1] // 2
    tail = latent + half + rope_half
    move(
        [
            (lat_ref, out_ref.at[:, pl.ds(0, latent)]),
            (half_of(qn_ref, there), out_ref.at[:, pl.ds(latent, half)]),
            (half_of(qr_ref, there), out_ref.at[:, pl.ds(latent + half, rope_half)]),
            (rope_ref, out_ref.at[pl.ds(0, ROPE), pl.ds(tail, rope_ref.shape[1])]),
        ],
        sem,
    )


def load_kernel(*refs):
    sub = lax.axis_index("sub")
    *refs, sem = refs
    count = len(refs) // 2
    move([(half_of(a, sub), b) for a, b in zip(refs[:count], refs[count:])], sem)


def gather_call(kernel, args, shapes):
    return pl.pallas_call(
        kernel,
        out_shape=[jax.ShapeDtypeStruct(shape, jnp.bfloat16) for shape in shapes],
        in_specs=[pl.BlockSpec(memory_space=pl.ANY)] * len(args),
        out_specs=[pl.BlockSpec(memory_space=pltpu.VMEM)] * len(shapes),
        scratch_shapes=[pltpu.SemaphoreType.DMA((len(args),))],
        compiler_params=pltpu.CompilerParams(vmem_limit_bytes=16 << 20),
        cost_estimate=pl.CostEstimate(
            flops=0, bytes_accessed=4 * sum(math.prod(shape) for shape in shapes), transcendentals=0
        ),
    )(*args)


def prepare(new_latent, q_nope, q_rope, rope_turned):
    rows, latent = new_latent.shape
    width = latent + q_nope.shape[1] // 2 + q_rope.shape[1] // 2 + rows
    args = (new_latent, q_nope, q_rope, rope_turned)
    return gather_call(prepare_kernel, args, [(rows, width)])[0]


def load(*args):
    return gather_call(load_kernel, args, [(a.shape[0], a.shape[1] // 2) for a in args])


RATE = math.log2(math.e) / math.sqrt(NOPE + ROPE)


def attend_kernel(steps, fresh, *refs):
    count = len(steps)
    where_ref, len_ref, lat_a, rope_a, other, qn_ref, qr_ref, wk_ref, wv_ref, *refs = refs
    mine = refs[:count]
    theirs = refs[count : 2 * count]
    refs = refs[2 * count :]
    if fresh:
        acc_ref, stat_ref, lat, kc, vt, score, weight, peak, bias = refs
    else:
        (acc_ref, stat_ref, out_ref, send_ref, lat, kc, vt, score, weight, peak, result,
         sem) = refs
    sub = lax.axis_index("sub")
    block, latent = lat_a.shape
    chunk = CAP * block
    first = chunk if fresh else 0
    queries = 2 * block
    keys = lat.shape[0]
    half = qn_ref.shape[1]
    halves = half // (4 * NOPE)
    nope_at = latent
    rope_at = nope_at + half
    tail_at = rope_at + qr_ref.shape[1]
    head = lambda j: slice(j * LANES, (j + 1) * LANES)
    at = lambda start, size: pl.ds(pl.multiple_of(start, size), size)

    def build():
        def put_tails(base, rope, mask):
            kc[0, base : base + block, NOPE:] = jnp.concatenate([rope, mask], axis=1)
            kc[1, base : base + block, NOPE:] = jnp.concatenate([mask, rope], axis=1)

        lane = lax.broadcasted_iota(jnp.int32, (block, ROPE), 1)
        row = lax.broadcasted_iota(jnp.int32, (block, ROPE), 0)
        length = jnp.broadcast_to(len_ref[:1, :ROPE], (block, ROPE)) + lane
        vt[:, :, VDIM:, :] = jnp.ones((2, 2, 16, keys), jnp.bfloat16)
        for i, k in enumerate(steps):
            width = mine[i].shape[1]
            here = pl.multiple_of(sub * width, width)
            there = pl.multiple_of((1 - sub) * width, width)
            base = first + i * chunk
            lat[base : base + chunk, pl.ds(here, width)] = mine[i][:chunk, :]
            lat[base : base + chunk, pl.ds(there, width)] = theirs[i][:chunk, :]
            for c in range(CAP):
                packed = jnp.where(sub == c, mine[i][chunk:, :], theirs[i][chunk:, :])
                rope = jnp.concatenate(
                    [packed[:, j * block : (j + 1) * block] for j in range(width // block)], axis=0
                )
                p = where_ref[k * CAP + c]
                hidden = (lane == 0) & ((p < 0) | (p * block + row >= length))
                put_tails(
                    base + c * block, rope.T, jnp.where(hidden, HIDE, 0.0).astype(jnp.bfloat16)
                )
        if fresh:
            plain = jnp.zeros((block, ROPE), jnp.bfloat16)
            lat[:block, :] = lat_a[...]
            lat[block:chunk, :] = other[:, :latent]
            put_tails(0, rope_a[...].T, plain)
            put_tails(block, other[:ROPE, tail_at:].T, plain)
            i = lax.broadcasted_iota(jnp.int32, (queries, queries), 0)
            j = lax.broadcasted_iota(jnp.int32, (queries, queries), 1)
            flip = sub * block
            seen = jnp.bitwise_xor(i, flip) <= jnp.bitwise_xor(j, flip)
            bias[...] = jnp.where(seen, 0.0, HIDE)

    def form_keys(pair):
        columns = at(pair * 2 * NOPE, 2 * NOPE)
        for r in range(0, keys, chunk):
            rows = slice(r, r + chunk)
            k2 = jnp.dot(lat[rows, :], wk_ref[:, columns], preferred_element_type=jnp.float32)
            for j in range(2):
                kc[j, rows, :NOPE] = k2[:, head(j)].astype(jnp.bfloat16)

    def form_values(pair, slot):
        v2 = lax.dot_general(
            wv_ref[:, at(pair * 2 * VDIM, 2 * VDIM)], lat[...], (((0,), (1,)), ((), ())),
            preferred_element_type=jnp.float32,
        )
        for j in range(2):
            vt[slot, j, :VDIM, :] = v2[j * VDIM : (j + 1) * VDIM].astype(jnp.bfloat16)

    def form_scores(pair, slot, j):
        lane = lax.broadcasted_iota(jnp.int32, (queries, LANES), 1)
        nope = pair * 2 * NOPE + j * NOPE
        qn = jnp.concatenate(
            [qn_ref[:, at(nope, NOPE)], other[:, at(nope_at + nope, NOPE)]], axis=0
        )
        rope = pair * LANES
        qr = jnp.concatenate(
            [qr_ref[:, at(rope, LANES)], other[:, at(rope_at + rope, LANES)]], axis=0
        )
        fill = jnp.where(lane == (1 - j) * ROPE, 1.0, 0.0).astype(jnp.bfloat16)
        own = (lane >= ROPE) if j else (lane < ROPE)
        qc = jnp.concatenate([qn, jnp.where(own, qr, fill)], axis=1)
        s = lax.dot_general(
            kc[j], qc, (((1,), (1,)), ((), ())), preferred_element_type=jnp.float32
        )
        if fresh:
            s = jnp.concatenate([s[:queries] + bias[...], s[queries:]], axis=0)
        score[slot, j] = s
        most = jnp.max(s, axis=0, keepdims=True)
        peak[slot, j] = jnp.broadcast_to(most, (8, queries))

    def form_weights(pair, slot, j):
        most = peak[slot, j, :1, :]
        if not fresh:
            most = jnp.maximum(most, stat_ref[at((2 * pair + j) * 8, 8), :][:1])
        weight[slot, j] = jnp.exp2((score[slot, j] - most) * RATE).astype(jnp.bfloat16)

    def form_output(pair, slot, j):
        o = jnp.dot(vt[slot, j], weight[slot, j], preferred_element_type=jnp.float32)
        o, norm = o[:VDIM], o[VDIM : VDIM + 1]
        rows = at((2 * pair + j) * VDIM, VDIM)
        stat_rows = at((2 * pair + j) * 8, 8)
        if fresh:
            acc_ref[rows, :] = o
            row = lax.broadcasted_iota(jnp.int32, (8, queries), 0)
            stat_ref[stat_rows, :] = jnp.where(row == 0, peak[slot, j], norm)
        else:
            stat = stat_ref[stat_rows, :]
            old = stat[:1]
            most = jnp.maximum(peak[slot, j, :1, :], old)
            keep = jnp.exp2((old - most) * RATE)
            norm = norm + keep * stat[1:2]
            o = (o + keep * acc_ref[rows, :]) / norm
            o = o.T.astype(jnp.bfloat16)
            columns = at((2 * pair + j) * VDIM, VDIM)
            result[:, columns] = o[:block]
            send_ref[:, columns] = o[block:]

    def both(pair, slot, more=True):
        form_weights(pair, slot, 0)
        form_weights(pair, slot, 1)
        if more:
            form_keys(pair + 1)
            form_values(pair + 1, 1 - slot)
        for j in range(2):
            form_output(pair, slot, j)
            if more:
                form_scores(pair + 1, 1 - slot, j)

    def deliver(t):
        width = 4 * VDIM
        return pltpu.make_async_copy(
            result.at[:, at(t * width, width)],
            out_ref.at[:, at(sub * half + t * width, width)],
            sem.at[t],
        )

    build()
    form_keys(0)
    form_values(0, 0)
    for j in range(2):
        form_scores(0, 0, j)

    def body(t, carry):
        both(2 * t, 0)
        both(2 * t + 1, 1)
        if not fresh:
            deliver(t).start()
        return carry

    if halves > 1:
        lax.fori_loop(0, halves - 1, body, 0)
    both(2 * halves - 2, 0)
    both(2 * halves - 1, 1, False)
    if not fresh:
        deliver(halves - 1).start()
        for t in range(halves):
            deliver(t).wait()


def attend(steps, where, length, mine, theirs, new_latent, rope_turned, other, qn, qr, wk, wv, state):
    fresh = state is None
    block, latent = new_latent.shape
    heads = wk.shape[1] // NOPE
    keys = (len(steps) + (1 if fresh else 0)) * CAP * block
    vmem = pl.BlockSpec(memory_space=pltpu.VMEM)
    args = [where, length, new_latent, rope_turned, other, qn, qr, wk, wv, *mine, *theirs]
    specs = [pl.BlockSpec(memory_space=pltpu.SMEM)] + [vmem] * (len(args) - 1)
    scratch = [
        pltpu.VMEM((keys, latent), jnp.bfloat16),
        pltpu.VMEM((2, keys, NOPE + LANES), jnp.bfloat16),
        pltpu.VMEM((2, 2, VDIM + 16, keys), jnp.bfloat16),
        pltpu.VMEM((2, 2, keys, 2 * block), jnp.float32),
        pltpu.VMEM((2, 2, keys, 2 * block), jnp.bfloat16),
        pltpu.VMEM((2, 2, 8, 2 * block), jnp.float32),
    ]
    if fresh:
        out_specs = [vmem, vmem]
        out_shape = [
            jax.ShapeDtypeStruct((heads * VDIM, 2 * block), jnp.float32),
            jax.ShapeDtypeStruct((heads * 8, 2 * block), jnp.float32),
        ]
        scratch.append(pltpu.VMEM((2 * block, 2 * block), jnp.float32))
    else:
        specs += [vmem, vmem]
        args += state
        out_specs = [pl.BlockSpec(memory_space=pl.ANY), vmem]
        out_shape = [
            jax.ShapeDtypeStruct((block, 2 * heads * VDIM), jnp.bfloat16),
            jax.ShapeDtypeStruct((block, heads * VDIM), jnp.bfloat16),
        ]
        scratch += [
            pltpu.VMEM((block, heads * VDIM), jnp.bfloat16),
            pltpu.SemaphoreType.DMA((heads // 4,)),
        ]
    return pl.pallas_call(
        functools.partial(attend_kernel, steps, fresh),
        in_specs=specs,
        out_specs=out_specs,
        scratch_shapes=scratch,
        out_shape=out_shape,
        compiler_params=pltpu.CompilerParams(vmem_limit_bytes=(36 if len(steps) < 8 else 48) << 20),
        cost_estimate=pl.CostEstimate(
            flops=4 * keys * latent * heads * NOPE + 8 * block * keys * heads * 256,
            bytes_accessed=8 * 1024 * 1024,
            transcendentals=2 * block * keys * heads,
        ),
        name="attend_new" if fresh else "attend_prefix",
    )(*args)


def join_kernel(kept_ref, back_ref, out_ref, sem):
    there = 1 - lax.axis_index("sub")
    half = back_ref.shape[1]
    copy = pltpu.make_async_copy(
        back_ref, out_ref.at[:, pl.ds(pl.multiple_of(there * half, LANES), half)], sem
    )
    copy.start()
    copy.wait()


def join(kept, back):
    return pl.pallas_call(
        join_kernel,
        out_shape=jax.ShapeDtypeStruct(kept.shape, kept.dtype),
        in_specs=[pl.BlockSpec(memory_space=pl.ANY)] * 2,
        out_specs=pl.BlockSpec(memory_space=pl.ANY),
        scratch_shapes=[pltpu.SemaphoreType.DMA(())],
        input_output_aliases={0: 0},
        compiler_params=pltpu.CompilerParams(vmem_limit_bytes=1 << 20),
        name="join",
    )(kept, back)


def shards(
    q_nope,
    q_rope,
    new_latent,
    new_rope,
    pool_latent,
    pool_rope,
    w_uk,
    w_uv,
    block_list,
    prefix_len,
    block_slot,
):
    n = lax.axis_size("req")
    swap = lambda a: lax.ppermute(a, "sub", [(0, 1), (1, 0)])
    cross = lambda a, k: lax.ppermute(a, "req", [(i, i ^ k) for i in range(n)])
    far = list(range(n - 1, 0, -1))
    keep = lambda a: pltpu.with_memory_space_constraint(a, pltpu.HBM)
    q_nope, q_rope, new_latent, w_uk, w_uv = map(keep, (q_nope, q_rope, new_latent, w_uk, w_uv))
    pool_latent = keep(pool_latent)
    slots = keep(block_slot)
    pool_turned = keep(pool_rope.swapaxes(1, 2))
    rope_turned = keep(new_rope.T)
    got = {}
    for k in far:
        got[k] = cross(block_list, k)
    lists = [keep(block_list)] + [got[k] for k in range(1, n)]
    other = prepare(new_latent, q_nope, q_rope, rope_turned)
    other = swap(other)
    sent, where = pack(n, lists, slots, pool_latent, pool_turned)
    local = swap(sent[0])
    length = prefix_len - lax.broadcasted_iota(jnp.int32, (8, LANES), 1)
    mine = []
    for k in far:
        mine.append(cross(sent[k], k))
    theirs = []
    for k, a in zip(far, mine):
        theirs.append(swap(a))
    loaded = load(q_nope, q_rope, w_uk, w_uv)
    common = (new_latent, rope_turned, other, *loaded)
    state = attend([0], where, length, [sent[0]], [local], *common, None)
    kept, gone = attend(far, where, length, mine, theirs, *common, state)
    back = swap(gone)
    return join(kept, back)


def solution(mesh):
    placed = (
        P(("groups", "req", "sub"), "head"),
        P(("groups", "req", "sub"), "head"),
        P(("groups", "req", "sub"), None),
        P(("groups", "req", "sub"), None),
        P(("groups", "req"), None, "sub"),
        P(("groups", "req"), None, None),
        P(None, "head"),
        P(None, "head"),
        P(("groups", "req"), None),
        P(("groups", "req")),
        P("groups"),
    )
    return jax.shard_map(
        shards,
        mesh=mesh,
        in_specs=placed,
        out_specs=P(("groups", "req", "sub"), "head"),
        check_vma=False,
    )
```

```python
import functools
import math

import jax
import jax.numpy as jnp
from jax import lax
from jax.experimental import pallas as pl
from jax.experimental.pallas import tpu as pltpu
from jax.sharding import PartitionSpec as P


NOPE = 128
ROPE = 64
VDIM = 128
CAP = 2
LANES = 128
HIDE = -1e30


def pack_kernel(n, blocks, pool_local, lists, slots_ref, pool_ref, rope_ref, outs, where_ref,
                index_ref, count_ref, lat_sem, rope_sem):
    me = lax.axis_index("req")
    sub = lax.axis_index("sub")
    block = pool_ref.shape[1]
    width = pool_ref.shape[2]
    for i in range(n * CAP):
        index_ref[i] = 0
        where_ref[i] = -1
    for i in range(n):
        count_ref[i] = 0
    for k in range(n):
        found = jnp.int32(0)
        for p in range(blocks):
            physical = slots_ref[lists[k][0, p]]
            owner = physical // pool_local
            mine = owner == me

            @pl.when(mine)
            def _():
                index_ref[k * CAP + found] = physical - owner * pool_local

            found = found + mine.astype(jnp.int32)
            if k == 0:
                step = jnp.bitwise_xor(me, owner)
                earlier = count_ref[step]
                where_ref[step * CAP + earlier] = p
                count_ref[step] = earlier + 1
    parts = width // block
    rows = ROPE // parts
    copies = []
    for k in range(n):
        for c in range(CAP):
            copies.append(pltpu.make_async_copy(
                pool_ref.at[index_ref[k * CAP + c]],
                outs[k].at[pl.ds(c * block, block)],
                lat_sem.at[k * CAP + c],
            ))
        for i in range(parts):
            copies.append(pltpu.make_async_copy(
                rope_ref.at[index_ref[k * CAP + sub], pl.ds(i * rows, rows)],
                outs[k].at[pl.ds(CAP * block, rows), pl.ds(i * block, block)],
                rope_sem.at[k * parts + i],
            ))
    for copy in copies:
        copy.start()
    for copy in copies:
        copy.wait()


def pack(n, lists, block_slot, pool_latent, rope_turned):
    pool_local, block, width = pool_latent.shape
    blocks = lists[0].shape[1]
    rows = CAP * block + block * ROPE // width
    vmem = pl.BlockSpec(memory_space=pltpu.VMEM)
    smem = pl.BlockSpec(memory_space=pltpu.SMEM)

    def body(*refs):
        pack_kernel(
            n, blocks, pool_local, refs[:n], *refs[n : n + 3],
            refs[n + 3 : 2 * n + 3], *refs[2 * n + 3 :],
        )

    out = pl.pallas_call(
        body,
        out_shape=[jax.ShapeDtypeStruct((rows, width), jnp.bfloat16)] * n
        + [jax.ShapeDtypeStruct((n * CAP,), jnp.int32)],
        in_specs=[smem] * (n + 1) + [pl.BlockSpec(memory_space=pl.ANY)] * 2,
        out_specs=[vmem] * n + [smem],
        scratch_shapes=[
            pltpu.SMEM((n * CAP,), jnp.int32),
            pltpu.SMEM((n,), jnp.int32),
            pltpu.SemaphoreType.DMA((n * CAP,)),
            pltpu.SemaphoreType.DMA((n * width // block,)),
        ],
        compiler_params=pltpu.CompilerParams(vmem_limit_bytes=16 << 20),
        cost_estimate=pl.CostEstimate(flops=0, bytes_accessed=4 * n * rows * width, transcendentals=0),
        name="pack",
    )(*lists, block_slot, pool_latent, rope_turned)
    return out[:n], out[n]


def half_of(ref, which):
    half = ref.shape[1] // 2
    return ref.at[:, pl.ds(pl.multiple_of(which * half, LANES), half)]


def move(moves, sem):
    copies = [pltpu.make_async_copy(*pair, sem.at[i]) for i, pair in enumerate(moves)]
    for copy in copies:
        copy.start()
    for copy in copies:
        copy.wait()


def prepare_kernel(lat_ref, qn_ref, qr_ref, rope_ref, pool_ref, pool_rope_ref,
                   out_ref, pool_out, pool_rope_out, sem):
    there = 1 - lax.axis_index("sub")
    latent = lat_ref.shape[1]
    half = qn_ref.shape[1] // 2
    rope_half = qr_ref.shape[1] // 2
    tail = latent + half + rope_half
    move(
        [
            (lat_ref, out_ref.at[:, pl.ds(0, latent)]),
            (half_of(qn_ref, there), out_ref.at[:, pl.ds(latent, half)]),
            (half_of(qr_ref, there), out_ref.at[:, pl.ds(latent + half, rope_half)]),
            (rope_ref, out_ref.at[pl.ds(0, ROPE), pl.ds(tail, rope_ref.shape[1])]),
            (pool_ref, pool_out),
            (pool_rope_ref, pool_rope_out),
        ],
        sem,
    )


def load_kernel(*refs):
    sub = lax.axis_index("sub")
    *refs, sem = refs
    count = len(refs) // 2
    move([(half_of(a, sub), b) for a, b in zip(refs[:count], refs[count:])], sem)


def gather_call(kernel, args, shapes):
    return pl.pallas_call(
        kernel,
        out_shape=[jax.ShapeDtypeStruct(shape, jnp.bfloat16) for shape in shapes],
        in_specs=[pl.BlockSpec(memory_space=pl.ANY)] * len(args),
        out_specs=[pl.BlockSpec(memory_space=pltpu.VMEM)] * len(shapes),
        scratch_shapes=[pltpu.SemaphoreType.DMA((len(args),))],
        compiler_params=pltpu.CompilerParams(vmem_limit_bytes=16 << 20),
        cost_estimate=pl.CostEstimate(
            flops=0, bytes_accessed=4 * sum(math.prod(shape) for shape in shapes), transcendentals=0
        ),
    )(*args)


def prepare(new_latent, q_nope, q_rope, rope_turned, pool_latent, pool_turned):
    rows, latent = new_latent.shape
    width = latent + q_nope.shape[1] // 2 + q_rope.shape[1] // 2 + rows
    args = (new_latent, q_nope, q_rope, rope_turned, pool_latent, pool_turned)
    shapes = [(rows, width), pool_latent.shape, pool_turned.shape]
    return gather_call(prepare_kernel, args, shapes)


def load(*args):
    return gather_call(load_kernel, args, [(a.shape[0], a.shape[1] // 2) for a in args])


RATE = math.log2(math.e) / math.sqrt(NOPE + ROPE)


def attend_kernel(steps, fresh, *refs):
    count = len(steps)
    where_ref, len_ref, lat_a, rope_a, other, qn_ref, qr_ref, wk_ref, wv_ref, *refs = refs
    mine = refs[:count]
    theirs = refs[count : 2 * count]
    refs = refs[2 * count :]
    if fresh:
        acc_ref, stat_ref, lat, kc, vt, score, weight, peak, norms, bias = refs
    else:
        (acc_ref, stat_ref, out_ref, send_ref, lat, kc, vt, score, weight, peak, norms, result,
         sem) = refs
    sub = lax.axis_index("sub")
    block, latent = lat_a.shape
    chunk = CAP * block
    first = chunk if fresh else 0
    queries = 2 * block
    keys = lat.shape[0]
    half = qn_ref.shape[1]
    halves = half // (4 * NOPE)
    nope_at = latent
    rope_at = nope_at + half
    tail_at = rope_at + qr_ref.shape[1]
    head = lambda j: slice(j * LANES, (j + 1) * LANES)
    at = lambda start, size: pl.ds(pl.multiple_of(start, size), size)

    def build():
        def put_tails(base, rope, mask):
            kc[0, base : base + block, NOPE:] = jnp.concatenate([rope, mask], axis=1)
            kc[1, base : base + block, NOPE:] = jnp.concatenate([mask, rope], axis=1)

        lane = lax.broadcasted_iota(jnp.int32, (block, ROPE), 1)
        row = lax.broadcasted_iota(jnp.int32, (block, ROPE), 0)
        length = jnp.broadcast_to(len_ref[:1, :ROPE], (block, ROPE)) + lane
        for i, k in enumerate(steps):
            width = mine[i].shape[1]
            here = pl.multiple_of(sub * width, width)
            there = pl.multiple_of((1 - sub) * width, width)
            base = first + i * chunk
            lat[base : base + chunk, pl.ds(here, width)] = mine[i][:chunk, :]
            lat[base : base + chunk, pl.ds(there, width)] = theirs[i][:chunk, :]
            for c in range(CAP):
                packed = jnp.where(sub == c, mine[i][chunk:, :], theirs[i][chunk:, :])
                rope = jnp.concatenate(
                    [packed[:, j * block : (j + 1) * block] for j in range(width // block)], axis=0
                )
                p = where_ref[k * CAP + c]
                hidden = (lane == 0) & ((p < 0) | (p * block + row >= length))
                put_tails(
                    base + c * block, rope.T, jnp.where(hidden, HIDE, 0.0).astype(jnp.bfloat16)
                )
        if fresh:
            plain = jnp.zeros((block, ROPE), jnp.bfloat16)
            lat[:block, :] = lat_a[...]
            lat[block:chunk, :] = other[:, :latent]
            put_tails(0, rope_a[...].T, plain)
            put_tails(block, other[:ROPE, tail_at:].T, plain)
            i = lax.broadcasted_iota(jnp.int32, (queries, queries), 0)
            j = lax.broadcasted_iota(jnp.int32, (queries, queries), 1)
            flip = sub * block
            seen = jnp.bitwise_xor(i, flip) <= jnp.bitwise_xor(j, flip)
            bias[...] = jnp.where(seen, 0.0, HIDE)

    def form_keys(pair):
        columns = at(pair * 2 * NOPE, 2 * NOPE)
        for r in range(0, keys, chunk):
            rows = slice(r, r + chunk)
            k2 = jnp.dot(lat[rows, :], wk_ref[:, columns], preferred_element_type=jnp.float32)
            for j in range(2):
                kc[j, rows, :NOPE] = k2[:, head(j)].astype(jnp.bfloat16)

    def form_values(pair, slot):
        v2 = lax.dot_general(
            wv_ref[:, at(pair * 2 * VDIM, 2 * VDIM)], lat[...], (((0,), (1,)), ((), ())),
            preferred_element_type=jnp.float32,
        )
        for j in range(2):
            vt[slot, j] = v2[j * VDIM : (j + 1) * VDIM].astype(jnp.bfloat16)

    def form_scores(pair, slot, j):
        lane = lax.broadcasted_iota(jnp.int32, (queries, LANES), 1)
        nope = pair * 2 * NOPE + j * NOPE
        qn = jnp.concatenate(
            [qn_ref[:, at(nope, NOPE)], other[:, at(nope_at + nope, NOPE)]], axis=0
        )
        rope = pair * LANES
        qr = jnp.concatenate(
            [qr_ref[:, at(rope, LANES)], other[:, at(rope_at + rope, LANES)]], axis=0
        )
        fill = jnp.where(lane == (1 - j) * ROPE, 1.0, 0.0).astype(jnp.bfloat16)
        own = (lane >= ROPE) if j else (lane < ROPE)
        qc = jnp.concatenate([qn, jnp.where(own, qr, fill)], axis=1)
        s = lax.dot_general(
            kc[j], qc, (((1,), (1,)), ((), ())), preferred_element_type=jnp.float32
        )
        if fresh:
            s = jnp.concatenate([s[:queries] + bias[...], s[queries:]], axis=0)
        score[slot, j] = s
        most = jnp.max(s, axis=0, keepdims=True)
        peak[slot, j] = jnp.broadcast_to(most, (8, queries))

    def form_weights(pair, slot, j):
        most = peak[slot, j, :1, :]
        if not fresh:
            most = jnp.maximum(most, stat_ref[at((2 * pair + j) * 8, 8), :][:1])
        e = jnp.exp2((score[slot, j] - most) * RATE)
        norms[slot, j] = jnp.broadcast_to(jnp.sum(e, axis=0, keepdims=True), (8, queries))
        weight[slot, j] = e.astype(jnp.bfloat16)

    def form_output(pair, slot, j):
        o = jnp.dot(vt[slot, j], weight[slot, j], preferred_element_type=jnp.float32)
        norm = norms[slot, j, :1, :]
        rows = at((2 * pair + j) * VDIM, VDIM)
        stat_rows = at((2 * pair + j) * 8, 8)
        if fresh:
            acc_ref[rows, :] = o
            row = lax.broadcasted_iota(jnp.int32, (8, queries), 0)
            stat_ref[stat_rows, :] = jnp.where(row == 0, peak[slot, j], norm)
        else:
            stat = stat_ref[stat_rows, :]
            old = stat[:1]
            most = jnp.maximum(peak[slot, j, :1, :], old)
            keep = jnp.exp2((old - most) * RATE)
            norm = norm + keep * stat[1:2]
            o = (o + keep * acc_ref[rows, :]) / norm
            o = o.T.astype(jnp.bfloat16)
            columns = at((2 * pair + j) * VDIM, VDIM)
            result[:, columns] = o[:block]
            send_ref[:, columns] = o[block:]

    def both(pair, slot, more=True):
        form_weights(pair, slot, 0)
        form_weights(pair, slot, 1)
        if more:
            form_keys(pair + 1)
            form_values(pair + 1, 1 - slot)
        for j in range(2):
            if not fresh:
                form_output(pair, slot, j)
            if more:
                form_scores(pair + 1, 1 - slot, j)
            if fresh:
                form_output(pair, slot, j)

    def deliver(t):
        width = 4 * VDIM
        return pltpu.make_async_copy(
            result.at[:, at(t * width, width)],
            out_ref.at[:, at(sub * half + t * width, width)],
            sem.at[t],
        )

    build()
    form_keys(0)
    form_values(0, 0)
    for j in range(2):
        form_scores(0, 0, j)

    def body(t, carry):
        both(2 * t, 0)
        both(2 * t + 1, 1)
        if not fresh:
            deliver(t).start()
        return carry

    if halves > 1:
        lax.fori_loop(0, halves - 1, body, 0)
    both(2 * halves - 2, 0)
    both(2 * halves - 1, 1, False)
    if not fresh:
        deliver(halves - 1).start()
        for t in range(halves):
            deliver(t).wait()


def attend(steps, where, length, mine, theirs, new_latent, rope_turned, other, qn, qr, wk, wv, state):
    fresh = state is None
    block, latent = new_latent.shape
    heads = wk.shape[1] // NOPE
    keys = (len(steps) + (1 if fresh else 0)) * CAP * block
    vmem = pl.BlockSpec(memory_space=pltpu.VMEM)
    args = [where, length, new_latent, rope_turned, other, qn, qr, wk, wv, *mine, *theirs]
    specs = [pl.BlockSpec(memory_space=pltpu.SMEM)] + [vmem] * (len(args) - 1)
    scratch = [
        pltpu.VMEM((keys, latent), jnp.bfloat16),
        pltpu.VMEM((2, keys, NOPE + LANES), jnp.bfloat16),
        pltpu.VMEM((2, 2, VDIM, keys), jnp.bfloat16),
        pltpu.VMEM((2, 2, keys, 2 * block), jnp.float32),
        pltpu.VMEM((2, 2, keys, 2 * block), jnp.bfloat16),
        pltpu.VMEM((2, 2, 8, 2 * block), jnp.float32),
        pltpu.VMEM((2, 2, 8, 2 * block), jnp.float32),
    ]
    if fresh:
        out_specs = [vmem, vmem]
        out_shape = [
            jax.ShapeDtypeStruct((heads * VDIM, 2 * block), jnp.float32),
            jax.ShapeDtypeStruct((heads * 8, 2 * block), jnp.float32),
        ]
        scratch.append(pltpu.VMEM((2 * block, 2 * block), jnp.float32))
    else:
        specs += [vmem, vmem]
        args += state
        out_specs = [pl.BlockSpec(memory_space=pl.ANY), vmem]
        out_shape = [
            jax.ShapeDtypeStruct((block, 2 * heads * VDIM), jnp.bfloat16),
            jax.ShapeDtypeStruct((block, heads * VDIM), jnp.bfloat16),
        ]
        scratch += [
            pltpu.VMEM((block, heads * VDIM), jnp.bfloat16),
            pltpu.SemaphoreType.DMA((heads // 4,)),
        ]
    return pl.pallas_call(
        functools.partial(attend_kernel, steps, fresh),
        in_specs=specs,
        out_specs=out_specs,
        scratch_shapes=scratch,
        out_shape=out_shape,
        compiler_params=pltpu.CompilerParams(vmem_limit_bytes=(36 if len(steps) < 8 else 48) << 20),
        cost_estimate=pl.CostEstimate(
            flops=4 * keys * latent * heads * NOPE + 8 * block * keys * heads * 256,
            bytes_accessed=8 * 1024 * 1024,
            transcendentals=2 * block * keys * heads,
        ),
        name="attend_new" if fresh else "attend_prefix",
    )(*args)


def join_kernel(kept_ref, back_ref, out_ref, sem):
    there = 1 - lax.axis_index("sub")
    half = back_ref.shape[1]
    copy = pltpu.make_async_copy(
        back_ref, out_ref.at[:, pl.ds(pl.multiple_of(there * half, LANES), half)], sem
    )
    copy.start()
    copy.wait()


def join(kept, back):
    return pl.pallas_call(
        join_kernel,
        out_shape=jax.ShapeDtypeStruct(kept.shape, kept.dtype),
        in_specs=[pl.BlockSpec(memory_space=pl.ANY)] * 2,
        out_specs=pl.BlockSpec(memory_space=pl.ANY),
        scratch_shapes=[pltpu.SemaphoreType.DMA(())],
        input_output_aliases={0: 0},
        compiler_params=pltpu.CompilerParams(vmem_limit_bytes=1 << 20),
        name="join",
    )(kept, back)


def shards(
    q_nope,
    q_rope,
    new_latent,
    new_rope,
    pool_latent,
    pool_rope,
    w_uk,
    w_uv,
    block_list,
    prefix_len,
    block_slot,
):
    n = lax.axis_size("req")
    swap = lambda a: lax.ppermute(a, "sub", [(0, 1), (1, 0)])
    cross = lambda a, k: lax.ppermute(a, "req", [(i, i ^ k) for i in range(n)])
    far = list(range(n - 1, 0, -1))
    keep = lambda a: pltpu.with_memory_space_constraint(a, pltpu.HBM)
    q_nope, q_rope, new_latent, w_uk, w_uv = map(keep, (q_nope, q_rope, new_latent, w_uk, w_uv))
    pool_latent = keep(pool_latent)
    slots = keep(block_slot)
    pool_turned = keep(pool_rope.swapaxes(1, 2))
    rope_turned = keep(new_rope.T)
    got = {}
    for k in far:
        got[k] = cross(block_list, k)
    lists = [keep(block_list)] + [got[k] for k in range(1, n)]
    other, pool_latent, pool_turned = prepare(
        new_latent, q_nope, q_rope, rope_turned, pool_latent, pool_turned
    )
    other = swap(other)
    sent, where = pack(n, lists, slots, pool_latent, pool_turned)
    local = swap(sent[0])
    length = prefix_len - lax.broadcasted_iota(jnp.int32, (8, LANES), 1)
    mine = []
    for k in far:
        mine.append(cross(sent[k], k))
    theirs = []
    for k, a in zip(far, mine):
        theirs.append(swap(a))
    loaded = load(q_nope, q_rope, w_uk, w_uv)
    common = (new_latent, rope_turned, other, *loaded)
    state = attend([0], where, length, [sent[0]], [local], *common, None)
    kept, gone = attend(far, where, length, mine, theirs, *common, state)
    back = swap(gone)
    return join(kept, back)


def solution(mesh):
    placed = (
        P(("groups", "req", "sub"), "head"),
        P(("groups", "req", "sub"), "head"),
        P(("groups", "req", "sub"), None),
        P(("groups", "req", "sub"), None),
        P(("groups", "req"), None, "sub"),
        P(("groups", "req"), None, None),
        P(None, "head"),
        P(None, "head"),
        P(("groups", "req"), None),
        P(("groups", "req")),
        P("groups"),
    )
    return jax.shard_map(
        shards,
        mesh=mesh,
        in_specs=placed,
        out_specs=P(("groups", "req", "sub"), "head"),
        check_vma=False,
    )
```

```python
import functools
import math

import jax
import jax.numpy as jnp
from jax import lax
from jax.experimental import pallas as pl
from jax.experimental.pallas import tpu as pltpu
from jax.sharding import PartitionSpec as P


NOPE = 128
ROPE = 64
VDIM = 128
CAP = 2
LANES = 128
HIDE = -1e30


def pack_kernel(kinds, own, blocks, pool_local, lists, slots_ref, pool_ref, rope_ref, outs,
                where_ref, index_ref, count_ref, lat_sem, rope_sem):
    me = lax.axis_index("req")
    sub = lax.axis_index("sub")
    block = pool_ref.shape[1]
    width = pool_ref.shape[2]
    for i in range(len(kinds) * CAP):
        index_ref[i] = 0
    if own:
        for i in range(where_ref.shape[0]):
            where_ref[i] = -1
        for i in range(count_ref.shape[0]):
            count_ref[i] = 0
    for i, k in enumerate(kinds):
        found = jnp.int32(0)
        for p in range(blocks):
            physical = slots_ref[lists[i][0, p]]
            owner = physical // pool_local
            mine = owner == me

            @pl.when(mine)
            def _():
                index_ref[i * CAP + found] = physical - owner * pool_local

            found = found + mine.astype(jnp.int32)
            if k == 0:
                step = jnp.bitwise_xor(me, owner)
                earlier = count_ref[step]
                where_ref[step * CAP + earlier] = p
                count_ref[step] = earlier + 1
    parts = width // block
    rows = ROPE // parts
    copies = []
    for i in range(len(kinds)):
        for c in range(CAP):
            copies.append(pltpu.make_async_copy(
                pool_ref.at[index_ref[i * CAP + c]],
                outs[i].at[pl.ds(c * block, block)],
                lat_sem.at[i * CAP + c],
            ))
        for j in range(parts):
            copies.append(pltpu.make_async_copy(
                rope_ref.at[index_ref[i * CAP + sub], pl.ds(j * rows, rows)],
                outs[i].at[pl.ds(CAP * block, rows), pl.ds(j * block, block)],
                rope_sem.at[i * parts + j],
            ))
    for copy in copies:
        copy.start()
    for copy in copies:
        copy.wait()


def pack(n, kinds, lists, block_slot, pool_latent, rope_turned):
    pool_local, block, width = pool_latent.shape
    blocks = lists[0].shape[1]
    rows = CAP * block + block * ROPE // width
    count = len(kinds)
    own = 0 in kinds
    vmem = pl.BlockSpec(memory_space=pltpu.VMEM)
    smem = pl.BlockSpec(memory_space=pltpu.SMEM)

    def body(*refs):
        ins, refs = refs[: count + 3], refs[count + 3 :]
        outs, refs = refs[:count], refs[count:]
        where_ref, refs = (refs[0], refs[1:]) if own else (None, refs)
        pack_kernel(kinds, own, blocks, pool_local, ins[:count], *ins[count:], outs, where_ref, *refs)

    return pl.pallas_call(
        body,
        out_shape=[jax.ShapeDtypeStruct((rows, width), jnp.bfloat16)] * count
        + [jax.ShapeDtypeStruct((n * CAP,), jnp.int32)] * own,
        in_specs=[smem] * (count + 1) + [pl.BlockSpec(memory_space=pl.ANY)] * 2,
        out_specs=[vmem] * count + [smem] * own,
        scratch_shapes=[
            pltpu.SMEM((count * CAP,), jnp.int32),
            pltpu.SMEM((n,), jnp.int32),
            pltpu.SemaphoreType.DMA((count * CAP,)),
            pltpu.SemaphoreType.DMA((count * width // block,)),
        ],
        compiler_params=pltpu.CompilerParams(vmem_limit_bytes=16 << 20),
        cost_estimate=pl.CostEstimate(
            flops=0, bytes_accessed=4 * count * rows * width, transcendentals=0
        ),
        name="pack",
    )(*lists, block_slot, pool_latent, rope_turned)


def half_of(ref, which):
    half = ref.shape[1] // 2
    return ref.at[:, pl.ds(pl.multiple_of(which * half, LANES), half)]


def move(moves, sem):
    copies = [pltpu.make_async_copy(*pair, sem.at[i]) for i, pair in enumerate(moves)]
    for copy in copies:
        copy.start()
    for copy in copies:
        copy.wait()


def prepare_kernel(lat_ref, qn_ref, qr_ref, rope_ref, pool_ref, pool_rope_ref,
                   out_ref, pool_out, pool_rope_out, sem):
    there = 1 - lax.axis_index("sub")
    latent = lat_ref.shape[1]
    half = qn_ref.shape[1] // 2
    rope_half = qr_ref.shape[1] // 2
    tail = latent + half + rope_half
    move(
        [
            (lat_ref, out_ref.at[:, pl.ds(0, latent)]),
            (half_of(qn_ref, there), out_ref.at[:, pl.ds(latent, half)]),
            (half_of(qr_ref, there), out_ref.at[:, pl.ds(latent + half, rope_half)]),
            (rope_ref, out_ref.at[pl.ds(0, ROPE), pl.ds(tail, rope_ref.shape[1])]),
            (pool_ref, pool_out),
            (pool_rope_ref, pool_rope_out),
        ],
        sem,
    )


def load_kernel(*refs):
    sub = lax.axis_index("sub")
    *refs, sem = refs
    count = len(refs) // 2
    move([(half_of(a, sub), b) for a, b in zip(refs[:count], refs[count:])], sem)


def gather_call(kernel, args, shapes):
    return pl.pallas_call(
        kernel,
        out_shape=[jax.ShapeDtypeStruct(shape, jnp.bfloat16) for shape in shapes],
        in_specs=[pl.BlockSpec(memory_space=pl.ANY)] * len(args),
        out_specs=[pl.BlockSpec(memory_space=pltpu.VMEM)] * len(shapes),
        scratch_shapes=[pltpu.SemaphoreType.DMA((len(args),))],
        compiler_params=pltpu.CompilerParams(vmem_limit_bytes=16 << 20),
        cost_estimate=pl.CostEstimate(
            flops=0, bytes_accessed=4 * sum(math.prod(shape) for shape in shapes), transcendentals=0
        ),
    )(*args)


def prepare(new_latent, q_nope, q_rope, rope_turned, pool_latent, pool_turned):
    rows, latent = new_latent.shape
    width = latent + q_nope.shape[1] // 2 + q_rope.shape[1] // 2 + rows
    args = (new_latent, q_nope, q_rope, rope_turned, pool_latent, pool_turned)
    shapes = [(rows, width), pool_latent.shape, pool_turned.shape]
    return gather_call(prepare_kernel, args, shapes)


def load(*args):
    return gather_call(load_kernel, args, [(a.shape[0], a.shape[1] // 2) for a in args])


RATE = math.log2(math.e) / math.sqrt(NOPE + ROPE)


def attend_kernel(steps, fresh, *refs):
    count = len(steps)
    where_ref, len_ref, lat_a, rope_a, other, qn_ref, qr_ref, wk_ref, wv_ref, *refs = refs
    mine = refs[:count]
    theirs = refs[count : 2 * count]
    refs = refs[2 * count :]
    if fresh:
        acc_ref, stat_ref, lat, kc, vt, score, weight, peak, norms, bias = refs
    else:
        (acc_ref, stat_ref, out_ref, send_ref, lat, kc, vt, score, weight, peak, norms, result,
         sem) = refs
    sub = lax.axis_index("sub")
    block, latent = lat_a.shape
    chunk = CAP * block
    first = chunk if fresh else 0
    queries = 2 * block
    keys = lat.shape[0]
    half = qn_ref.shape[1]
    halves = half // (4 * NOPE)
    nope_at = latent
    rope_at = nope_at + half
    tail_at = rope_at + qr_ref.shape[1]
    head = lambda j: slice(j * LANES, (j + 1) * LANES)
    at = lambda start, size: pl.ds(pl.multiple_of(start, size), size)

    def build():
        def put_tails(base, rope, mask):
            kc[0, base : base + block, NOPE:] = jnp.concatenate([rope, mask], axis=1)
            kc[1, base : base + block, NOPE:] = jnp.concatenate([mask, rope], axis=1)

        lane = lax.broadcasted_iota(jnp.int32, (block, ROPE), 1)
        row = lax.broadcasted_iota(jnp.int32, (block, ROPE), 0)
        length = jnp.broadcast_to(len_ref[:1, :ROPE], (block, ROPE)) + lane
        for i, k in enumerate(steps):
            width = mine[i].shape[1]
            here = pl.multiple_of(sub * width, width)
            there = pl.multiple_of((1 - sub) * width, width)
            base = first + i * chunk
            lat[base : base + chunk, pl.ds(here, width)] = mine[i][:chunk, :]
            lat[base : base + chunk, pl.ds(there, width)] = theirs[i][:chunk, :]
            for c in range(CAP):
                packed = jnp.where(sub == c, mine[i][chunk:, :], theirs[i][chunk:, :])
                rope = jnp.concatenate(
                    [packed[:, j * block : (j + 1) * block] for j in range(width // block)], axis=0
                )
                p = where_ref[k * CAP + c]
                hidden = (lane == 0) & ((p < 0) | (p * block + row >= length))
                put_tails(
                    base + c * block, rope.T, jnp.where(hidden, HIDE, 0.0).astype(jnp.bfloat16)
                )
        if fresh:
            plain = jnp.zeros((block, ROPE), jnp.bfloat16)
            lat[:block, :] = lat_a[...]
            lat[block:chunk, :] = other[:, :latent]
            put_tails(0, rope_a[...].T, plain)
            put_tails(block, other[:ROPE, tail_at:].T, plain)
            i = lax.broadcasted_iota(jnp.int32, (queries, queries), 0)
            j = lax.broadcasted_iota(jnp.int32, (queries, queries), 1)
            flip = sub * block
            seen = jnp.bitwise_xor(i, flip) <= jnp.bitwise_xor(j, flip)
            bias[...] = jnp.where(seen, 0.0, HIDE)

    def form_keys(pair):
        columns = at(pair * 2 * NOPE, 2 * NOPE)
        for r in range(0, keys, chunk):
            rows = slice(r, r + chunk)
            k2 = jnp.dot(lat[rows, :], wk_ref[:, columns], preferred_element_type=jnp.float32)
            for j in range(2):
                kc[j, rows, :NOPE] = k2[:, head(j)].astype(jnp.bfloat16)

    def form_values(pair, slot):
        v2 = lax.dot_general(
            wv_ref[:, at(pair * 2 * VDIM, 2 * VDIM)], lat[...], (((0,), (1,)), ((), ())),
            preferred_element_type=jnp.float32,
        )
        for j in range(2):
            vt[slot, j] = v2[j * VDIM : (j + 1) * VDIM].astype(jnp.bfloat16)

    def form_scores(pair, slot, j):
        lane = lax.broadcasted_iota(jnp.int32, (queries, LANES), 1)
        nope = pair * 2 * NOPE + j * NOPE
        qn = jnp.concatenate(
            [qn_ref[:, at(nope, NOPE)], other[:, at(nope_at + nope, NOPE)]], axis=0
        )
        rope = pair * LANES
        qr = jnp.concatenate(
            [qr_ref[:, at(rope, LANES)], other[:, at(rope_at + rope, LANES)]], axis=0
        )
        fill = jnp.where(lane == (1 - j) * ROPE, 1.0, 0.0).astype(jnp.bfloat16)
        own = (lane >= ROPE) if j else (lane < ROPE)
        qc = jnp.concatenate([qn, jnp.where(own, qr, fill)], axis=1)
        s = lax.dot_general(
            kc[j], qc, (((1,), (1,)), ((), ())), preferred_element_type=jnp.float32
        )
        if fresh:
            s = jnp.concatenate([s[:queries] + bias[...], s[queries:]], axis=0)
        score[slot, j] = s
        most = jnp.max(s, axis=0, keepdims=True)
        peak[slot, j] = jnp.broadcast_to(most, (8, queries))

    def form_weights(pair, slot, j):
        most = peak[slot, j, :1, :]
        if not fresh:
            most = jnp.maximum(most, stat_ref[at((2 * pair + j) * 8, 8), :][:1])
        e = jnp.exp2((score[slot, j] - most) * RATE)
        norms[slot, j] = jnp.broadcast_to(jnp.sum(e, axis=0, keepdims=True), (8, queries))
        weight[slot, j] = e.astype(jnp.bfloat16)

    def form_output(pair, slot, j):
        o = jnp.dot(vt[slot, j], weight[slot, j], preferred_element_type=jnp.float32)
        norm = norms[slot, j, :1, :]
        rows = at((2 * pair + j) * VDIM, VDIM)
        stat_rows = at((2 * pair + j) * 8, 8)
        if fresh:
            acc_ref[rows, :] = o
            row = lax.broadcasted_iota(jnp.int32, (8, queries), 0)
            stat_ref[stat_rows, :] = jnp.where(row == 0, peak[slot, j], norm)
        else:
            stat = stat_ref[stat_rows, :]
            old = stat[:1]
            most = jnp.maximum(peak[slot, j, :1, :], old)
            keep = jnp.exp2((old - most) * RATE)
            norm = norm + keep * stat[1:2]
            o = (o + keep * acc_ref[rows, :]) / norm
            o = o.T.astype(jnp.bfloat16)
            columns = at((2 * pair + j) * VDIM, VDIM)
            result[:, columns] = o[:block]
            send_ref[:, columns] = o[block:]

    def both(pair, slot, more=True):
        form_weights(pair, slot, 0)
        form_weights(pair, slot, 1)
        if more:
            form_keys(pair + 1)
            form_values(pair + 1, 1 - slot)
        for j in range(2):
            if not fresh:
                form_output(pair, slot, j)
            if more:
                form_scores(pair + 1, 1 - slot, j)
            if fresh:
                form_output(pair, slot, j)

    def deliver(t):
        width = 4 * VDIM
        return pltpu.make_async_copy(
            result.at[:, at(t * width, width)],
            out_ref.at[:, at(sub * half + t * width, width)],
            sem.at[t],
        )

    build()
    form_keys(0)
    form_values(0, 0)
    for j in range(2):
        form_scores(0, 0, j)

    def body(t, carry):
        both(2 * t, 0)
        both(2 * t + 1, 1)
        if not fresh:
            deliver(t).start()
        return carry

    if halves > 1:
        lax.fori_loop(0, halves - 1, body, 0)
    both(2 * halves - 2, 0)
    both(2 * halves - 1, 1, False)
    if not fresh:
        deliver(halves - 1).start()
        for t in range(halves):
            deliver(t).wait()


def attend(steps, where, length, mine, theirs, new_latent, rope_turned, other, qn, qr, wk, wv, state):
    fresh = state is None
    block, latent = new_latent.shape
    heads = wk.shape[1] // NOPE
    keys = (len(steps) + (1 if fresh else 0)) * CAP * block
    vmem = pl.BlockSpec(memory_space=pltpu.VMEM)
    args = [where, length, new_latent, rope_turned, other, qn, qr, wk, wv, *mine, *theirs]
    specs = [pl.BlockSpec(memory_space=pltpu.SMEM)] + [vmem] * (len(args) - 1)
    scratch = [
        pltpu.VMEM((keys, latent), jnp.bfloat16),
        pltpu.VMEM((2, keys, NOPE + LANES), jnp.bfloat16),
        pltpu.VMEM((2, 2, VDIM, keys), jnp.bfloat16),
        pltpu.VMEM((2, 2, keys, 2 * block), jnp.float32),
        pltpu.VMEM((2, 2, keys, 2 * block), jnp.bfloat16),
        pltpu.VMEM((2, 2, 8, 2 * block), jnp.float32),
        pltpu.VMEM((2, 2, 8, 2 * block), jnp.float32),
    ]
    if fresh:
        out_specs = [vmem, vmem]
        out_shape = [
            jax.ShapeDtypeStruct((heads * VDIM, 2 * block), jnp.float32),
            jax.ShapeDtypeStruct((heads * 8, 2 * block), jnp.float32),
        ]
        scratch.append(pltpu.VMEM((2 * block, 2 * block), jnp.float32))
    else:
        specs += [vmem, vmem]
        args += state
        out_specs = [pl.BlockSpec(memory_space=pl.ANY), vmem]
        out_shape = [
            jax.ShapeDtypeStruct((block, 2 * heads * VDIM), jnp.bfloat16),
            jax.ShapeDtypeStruct((block, heads * VDIM), jnp.bfloat16),
        ]
        scratch += [
            pltpu.VMEM((block, heads * VDIM), jnp.bfloat16),
            pltpu.SemaphoreType.DMA((heads // 4,)),
        ]
    return pl.pallas_call(
        functools.partial(attend_kernel, steps, fresh),
        in_specs=specs,
        out_specs=out_specs,
        scratch_shapes=scratch,
        out_shape=out_shape,
        compiler_params=pltpu.CompilerParams(vmem_limit_bytes=(36 if len(steps) < 8 else 48) << 20),
        cost_estimate=pl.CostEstimate(
            flops=4 * keys * latent * heads * NOPE + 8 * block * keys * heads * 256,
            bytes_accessed=8 * 1024 * 1024,
            transcendentals=2 * block * keys * heads,
        ),
        name="attend_new" if fresh else "attend_prefix",
    )(*args)


def join_kernel(kept_ref, back_ref, out_ref, sem):
    there = 1 - lax.axis_index("sub")
    half = back_ref.shape[1]
    copy = pltpu.make_async_copy(
        back_ref, out_ref.at[:, pl.ds(pl.multiple_of(there * half, LANES), half)], sem
    )
    copy.start()
    copy.wait()


def join(kept, back):
    return pl.pallas_call(
        join_kernel,
        out_shape=jax.ShapeDtypeStruct(kept.shape, kept.dtype),
        in_specs=[pl.BlockSpec(memory_space=pl.ANY)] * 2,
        out_specs=pl.BlockSpec(memory_space=pl.ANY),
        scratch_shapes=[pltpu.SemaphoreType.DMA(())],
        input_output_aliases={0: 0},
        compiler_params=pltpu.CompilerParams(vmem_limit_bytes=1 << 20),
        name="join",
    )(kept, back)


def shards(
    q_nope,
    q_rope,
    new_latent,
    new_rope,
    pool_latent,
    pool_rope,
    w_uk,
    w_uv,
    block_list,
    prefix_len,
    block_slot,
):
    n = lax.axis_size("req")
    swap = lambda a: lax.ppermute(a, "sub", [(0, 1), (1, 0)])
    cross = lambda a, k: lax.ppermute(a, "req", [(i, i ^ k) for i in range(n)])
    far = list(range(n - 1, 0, -1))
    keep = lambda a: pltpu.with_memory_space_constraint(a, pltpu.HBM)
    q_nope, q_rope, new_latent, w_uk, w_uv = map(keep, (q_nope, q_rope, new_latent, w_uk, w_uv))
    pool_latent = keep(pool_latent)
    slots = keep(block_slot)
    pool_turned = keep(pool_rope.swapaxes(1, 2))
    rope_turned = keep(new_rope.T)
    got = {}
    for k in far:
        got[k] = cross(block_list, k)
    lists = [keep(block_list)] + [got[k] for k in range(1, n)]
    other, pool_latent, pool_turned = prepare(
        new_latent, q_nope, q_rope, rope_turned, pool_latent, pool_turned
    )
    other = swap(other)
    early = n // 2
    sent = {early: pack(n, [early], [lists[early]], slots, pool_latent, pool_turned)[0]}
    kinds = [k for k in range(n) if k != early]
    *rest, where = pack(n, kinds, [lists[k] for k in kinds], slots, pool_latent, pool_turned)
    sent.update(zip(kinds, rest))
    local = swap(sent[0])
    length = prefix_len - lax.broadcasted_iota(jnp.int32, (8, LANES), 1)
    mine = []
    for k in far:
        mine.append(cross(sent[k], k))
    theirs = []
    for k, a in zip(far, mine):
        theirs.append(swap(a))
    loaded = load(q_nope, q_rope, w_uk, w_uv)
    common = (new_latent, rope_turned, other, *loaded)
    state = attend([0], where, length, [sent[0]], [local], *common, None)
    kept, gone = attend(far, where, length, mine, theirs, *common, state)
    back = swap(gone)
    return join(kept, back)


def solution(mesh):
    placed = (
        P(("groups", "req", "sub"), "head"),
        P(("groups", "req", "sub"), "head"),
        P(("groups", "req", "sub"), None),
        P(("groups", "req", "sub"), None),
        P(("groups", "req"), None, "sub"),
        P(("groups", "req"), None, None),
        P(None, "head"),
        P(None, "head"),
        P(("groups", "req"), None),
        P(("groups", "req")),
        P("groups"),
    )
    return jax.shard_map(
        shards,
        mesh=mesh,
        in_specs=placed,
        out_specs=P(("groups", "req", "sub"), "head"),
        check_vma=False,
    )
```

```python
import functools
import math

import jax
import jax.numpy as jnp
from jax import lax
from jax.experimental import pallas as pl
from jax.experimental.pallas import tpu as pltpu
from jax.sharding import PartitionSpec as P


NOPE = 128
ROPE = 64
VDIM = 128
CAP = 2
LANES = 128
HIDE = -1e30


def pack_kernel(kinds, own, blocks, pool_local, lists, slots_ref, pool_ref, rope_ref, outs,
                where_ref, index_ref, count_ref, lat_sem, rope_sem):
    me = lax.axis_index("req")
    sub = lax.axis_index("sub")
    block = pool_ref.shape[1]
    width = pool_ref.shape[2]
    for i in range(len(kinds) * CAP):
        index_ref[i] = 0
    if own:
        for i in range(where_ref.shape[0]):
            where_ref[i] = -1
        for i in range(count_ref.shape[0]):
            count_ref[i] = 0
    for i, k in enumerate(kinds):
        found = jnp.int32(0)
        for p in range(blocks):
            physical = slots_ref[lists[i][0, p]]
            owner = physical // pool_local
            mine = owner == me

            @pl.when(mine)
            def _():
                index_ref[i * CAP + found] = physical - owner * pool_local

            found = found + mine.astype(jnp.int32)
            if k == 0:
                step = jnp.bitwise_xor(me, owner)
                earlier = count_ref[step]
                where_ref[step * CAP + earlier] = p
                count_ref[step] = earlier + 1
    parts = width // block
    rows = ROPE // parts
    copies = []
    for i in range(len(kinds)):
        for c in range(CAP):
            copies.append(pltpu.make_async_copy(
                pool_ref.at[index_ref[i * CAP + c]],
                outs[i].at[pl.ds(c * block, block)],
                lat_sem.at[i * CAP + c],
            ))
        for j in range(parts):
            copies.append(pltpu.make_async_copy(
                rope_ref.at[index_ref[i * CAP + sub], pl.ds(j * rows, rows)],
                outs[i].at[pl.ds(CAP * block, rows), pl.ds(j * block, block)],
                rope_sem.at[i * parts + j],
            ))
    for copy in copies:
        copy.start()
    for copy in copies:
        copy.wait()


def pack(n, kinds, lists, block_slot, pool_latent, rope_turned):
    pool_local, block, width = pool_latent.shape
    blocks = lists[0].shape[1]
    rows = CAP * block + block * ROPE // width
    count = len(kinds)
    own = 0 in kinds
    vmem = pl.BlockSpec(memory_space=pltpu.VMEM)
    smem = pl.BlockSpec(memory_space=pltpu.SMEM)

    def body(*refs):
        ins, refs = refs[: count + 3], refs[count + 3 :]
        outs, refs = refs[:count], refs[count:]
        where_ref, refs = (refs[0], refs[1:]) if own else (None, refs)
        pack_kernel(kinds, own, blocks, pool_local, ins[:count], *ins[count:], outs, where_ref, *refs)

    return pl.pallas_call(
        body,
        out_shape=[jax.ShapeDtypeStruct((rows, width), jnp.bfloat16)] * count
        + [jax.ShapeDtypeStruct((n * CAP,), jnp.int32)] * own,
        in_specs=[smem] * (count + 1) + [pl.BlockSpec(memory_space=pl.ANY)] * 2,
        out_specs=[vmem] * count + [smem] * own,
        scratch_shapes=[
            pltpu.SMEM((count * CAP,), jnp.int32),
            pltpu.SMEM((n,), jnp.int32),
            pltpu.SemaphoreType.DMA((count * CAP,)),
            pltpu.SemaphoreType.DMA((count * width // block,)),
        ],
        compiler_params=pltpu.CompilerParams(vmem_limit_bytes=16 << 20),
        cost_estimate=pl.CostEstimate(
            flops=0, bytes_accessed=4 * count * rows * width, transcendentals=0
        ),
        name="pack",
    )(*lists, block_slot, pool_latent, rope_turned)


def half_of(ref, which):
    half = ref.shape[1] // 2
    return ref.at[:, pl.ds(pl.multiple_of(which * half, LANES), half)]


def move(moves, sem):
    copies = [pltpu.make_async_copy(*pair, sem.at[i]) for i, pair in enumerate(moves)]
    for copy in copies:
        copy.start()
    for copy in copies:
        copy.wait()


def prepare_kernel(lat_ref, qn_ref, qr_ref, rope_ref, pool_ref, pool_rope_ref,
                   out_ref, pool_out, pool_rope_out, sem):
    there = 1 - lax.axis_index("sub")
    latent = lat_ref.shape[1]
    half = qn_ref.shape[1] // 2
    rope_half = qr_ref.shape[1] // 2
    tail = latent + half + rope_half
    move(
        [
            (lat_ref, out_ref.at[:, pl.ds(0, latent)]),
            (half_of(qn_ref, there), out_ref.at[:, pl.ds(latent, half)]),
            (half_of(qr_ref, there), out_ref.at[:, pl.ds(latent + half, rope_half)]),
            (rope_ref, out_ref.at[pl.ds(0, ROPE), pl.ds(tail, rope_ref.shape[1])]),
            (pool_ref, pool_out),
            (pool_rope_ref, pool_rope_out),
        ],
        sem,
    )


def gather_call(kernel, args, shapes):
    return pl.pallas_call(
        kernel,
        out_shape=[jax.ShapeDtypeStruct(shape, jnp.bfloat16) for shape in shapes],
        in_specs=[pl.BlockSpec(memory_space=pl.ANY)] * len(args),
        out_specs=[pl.BlockSpec(memory_space=pltpu.VMEM)] * len(shapes),
        scratch_shapes=[pltpu.SemaphoreType.DMA((len(args),))],
        compiler_params=pltpu.CompilerParams(vmem_limit_bytes=16 << 20),
        cost_estimate=pl.CostEstimate(
            flops=0, bytes_accessed=4 * sum(math.prod(shape) for shape in shapes), transcendentals=0
        ),
    )(*args)


def prepare(new_latent, q_nope, q_rope, rope_turned, pool_latent, pool_turned):
    rows, latent = new_latent.shape
    width = latent + q_nope.shape[1] // 2 + q_rope.shape[1] // 2 + rows
    args = (new_latent, q_nope, q_rope, rope_turned, pool_latent, pool_turned)
    shapes = [(rows, width), pool_latent.shape, pool_turned.shape]
    return gather_call(prepare_kernel, args, shapes)


RATE = math.log2(math.e) / math.sqrt(NOPE + ROPE)


def attend_kernel(steps, fresh, *refs):
    count = len(steps)
    where_ref, len_ref, lat_a, rope_a, other, qn_ref, qr_ref, wk_ref, wv_ref, *refs = refs
    mine = refs[:count]
    theirs = refs[count : 2 * count]
    refs = refs[2 * count :]
    if fresh:
        wide = (qn_ref, qr_ref, wk_ref, wv_ref)
        (acc_ref, stat_ref, qn_ref, qr_ref, wk_ref, wv_ref,
         lat, kc, vt, score, weight, peak, norms, bias, sem) = refs
    else:
        (acc_ref, stat_ref, out_ref, send_ref, lat, kc, vt, score, weight, peak, norms, result,
         sem) = refs
    sub = lax.axis_index("sub")
    block, latent = lat_a.shape
    chunk = CAP * block
    first = chunk if fresh else 0
    queries = 2 * block
    keys = lat.shape[0]
    half = qn_ref.shape[1]
    halves = half // (4 * NOPE)
    nope_at = latent
    rope_at = nope_at + half
    tail_at = rope_at + qr_ref.shape[1]
    head = lambda j: slice(j * LANES, (j + 1) * LANES)
    at = lambda start, size: pl.ds(pl.multiple_of(start, size), size)

    def fetch(pair):
        copies = []
        for i, (ref, out) in enumerate(zip(wide, (qn_ref, qr_ref, wk_ref, wv_ref))):
            span = out.shape[1]
            size = span * 2 * NOPE // half
            copies.append(pltpu.make_async_copy(
                ref.at[:, at(sub * span + pair * size, size)],
                out.at[:, at(pair * size, size)],
                sem.at[i, pair],
            ))
        return copies

    def arrive(pair):
        if fresh:
            for copy in fetch(pair):
                copy.wait()

    def build():
        def put_tails(base, rope, mask):
            kc[0, base : base + block, NOPE:] = jnp.concatenate([rope, mask], axis=1)
            kc[1, base : base + block, NOPE:] = jnp.concatenate([mask, rope], axis=1)

        lane = lax.broadcasted_iota(jnp.int32, (block, ROPE), 1)
        row = lax.broadcasted_iota(jnp.int32, (block, ROPE), 0)
        length = jnp.broadcast_to(len_ref[:1, :ROPE], (block, ROPE)) + lane
        for i, k in enumerate(steps):
            width = mine[i].shape[1]
            here = pl.multiple_of(sub * width, width)
            there = pl.multiple_of((1 - sub) * width, width)
            base = first + i * chunk
            lat[base : base + chunk, pl.ds(here, width)] = mine[i][:chunk, :]
            lat[base : base + chunk, pl.ds(there, width)] = theirs[i][:chunk, :]
            for c in range(CAP):
                packed = jnp.where(sub == c, mine[i][chunk:, :], theirs[i][chunk:, :])
                rope = jnp.concatenate(
                    [packed[:, j * block : (j + 1) * block] for j in range(width // block)], axis=0
                )
                p = where_ref[k * CAP + c]
                hidden = (lane == 0) & ((p < 0) | (p * block + row >= length))
                put_tails(
                    base + c * block, rope.T, jnp.where(hidden, HIDE, 0.0).astype(jnp.bfloat16)
                )
        if fresh:
            plain = jnp.zeros((block, ROPE), jnp.bfloat16)
            lat[:block, :] = lat_a[...]
            lat[block:chunk, :] = other[:, :latent]
            put_tails(0, rope_a[...].T, plain)
            put_tails(block, other[:ROPE, tail_at:].T, plain)
            i = lax.broadcasted_iota(jnp.int32, (queries, queries), 0)
            j = lax.broadcasted_iota(jnp.int32, (queries, queries), 1)
            flip = sub * block
            seen = jnp.bitwise_xor(i, flip) <= jnp.bitwise_xor(j, flip)
            bias[...] = jnp.where(seen, 0.0, HIDE)

    def form_keys(pair):
        columns = at(pair * 2 * NOPE, 2 * NOPE)
        for r in range(0, keys, chunk):
            rows = slice(r, r + chunk)
            k2 = jnp.dot(lat[rows, :], wk_ref[:, columns], preferred_element_type=jnp.float32)
            for j in range(2):
                kc[j, rows, :NOPE] = k2[:, head(j)].astype(jnp.bfloat16)

    def form_values(pair, slot):
        v2 = lax.dot_general(
            wv_ref[:, at(pair * 2 * VDIM, 2 * VDIM)], lat[...], (((0,), (1,)), ((), ())),
            preferred_element_type=jnp.float32,
        )
        for j in range(2):
            vt[slot, j] = v2[j * VDIM : (j + 1) * VDIM].astype(jnp.bfloat16)

    def form_scores(pair, slot, j):
        lane = lax.broadcasted_iota(jnp.int32, (queries, LANES), 1)
        nope = pair * 2 * NOPE + j * NOPE
        qn = jnp.concatenate(
            [qn_ref[:, at(nope, NOPE)], other[:, at(nope_at + nope, NOPE)]], axis=0
        )
        rope = pair * LANES
        qr = jnp.concatenate(
            [qr_ref[:, at(rope, LANES)], other[:, at(rope_at + rope, LANES)]], axis=0
        )
        fill = jnp.where(lane == (1 - j) * ROPE, 1.0, 0.0).astype(jnp.bfloat16)
        own = (lane >= ROPE) if j else (lane < ROPE)
        qc = jnp.concatenate([qn, jnp.where(own, qr, fill)], axis=1)
        s = lax.dot_general(
            kc[j], qc, (((1,), (1,)), ((), ())), preferred_element_type=jnp.float32
        )
        if fresh:
            s = jnp.concatenate([s[:queries] + bias[...], s[queries:]], axis=0)
        score[slot, j] = s
        most = jnp.max(s, axis=0, keepdims=True)
        peak[slot, j] = jnp.broadcast_to(most, (8, queries))

    def form_weights(pair, slot, j):
        most = peak[slot, j, :1, :]
        if not fresh:
            most = jnp.maximum(most, stat_ref[at((2 * pair + j) * 8, 8), :][:1])
        e = jnp.exp2((score[slot, j] - most) * RATE)
        norms[slot, j] = jnp.broadcast_to(jnp.sum(e, axis=0, keepdims=True), (8, queries))
        weight[slot, j] = e.astype(jnp.bfloat16)

    def form_output(pair, slot, j):
        o = jnp.dot(vt[slot, j], weight[slot, j], preferred_element_type=jnp.float32)
        norm = norms[slot, j, :1, :]
        rows = at((2 * pair + j) * VDIM, VDIM)
        stat_rows = at((2 * pair + j) * 8, 8)
        if fresh:
            acc_ref[rows, :] = o
            row = lax.broadcasted_iota(jnp.int32, (8, queries), 0)
            stat_ref[stat_rows, :] = jnp.where(row == 0, peak[slot, j], norm)
        else:
            stat = stat_ref[stat_rows, :]
            old = stat[:1]
            most = jnp.maximum(peak[slot, j, :1, :], old)
            keep = jnp.exp2((old - most) * RATE)
            norm = norm + keep * stat[1:2]
            o = (o + keep * acc_ref[rows, :]) / norm
            o = o.T.astype(jnp.bfloat16)
            columns = at((2 * pair + j) * VDIM, VDIM)
            result[:, columns] = o[:block]
            send_ref[:, columns] = o[block:]

    def both(pair, slot, more=True):
        form_weights(pair, slot, 0)
        form_weights(pair, slot, 1)
        if more:
            arrive(pair + 1)
            form_keys(pair + 1)
            form_values(pair + 1, 1 - slot)
        for j in range(2):
            if not fresh:
                form_output(pair, slot, j)
            if more:
                form_scores(pair + 1, 1 - slot, j)
            if fresh:
                form_output(pair, slot, j)

    def deliver(t):
        width = 4 * VDIM
        return pltpu.make_async_copy(
            result.at[:, at(t * width, width)],
            out_ref.at[:, at(sub * half + t * width, width)],
            sem.at[t],
        )

    if fresh:
        for pair in range(2 * halves):
            for copy in fetch(pair):
                copy.start()
    build()
    arrive(0)
    form_keys(0)
    form_values(0, 0)
    for j in range(2):
        form_scores(0, 0, j)

    def body(t, carry):
        both(2 * t, 0)
        both(2 * t + 1, 1)
        if not fresh:
            deliver(t).start()
        return carry

    if halves > 1:
        lax.fori_loop(0, halves - 1, body, 0)
    both(2 * halves - 2, 0)
    both(2 * halves - 1, 1, False)
    if not fresh:
        deliver(halves - 1).start()
        for t in range(halves):
            deliver(t).wait()


def attend(steps, where, length, mine, theirs, new_latent, rope_turned, other, qn, qr, wk, wv, state):
    fresh = state is None
    block, latent = new_latent.shape
    heads = wk.shape[1] // NOPE // (2 if fresh else 1)
    keys = (len(steps) + (1 if fresh else 0)) * CAP * block
    vmem = pl.BlockSpec(memory_space=pltpu.VMEM)
    args = [where, length, new_latent, rope_turned, other, qn, qr, wk, wv, *mine, *theirs]
    place = pl.BlockSpec(memory_space=pl.ANY) if fresh else vmem
    specs = [pl.BlockSpec(memory_space=pltpu.SMEM)] + [vmem] * 4 + [place] * 4
    specs += [vmem] * (2 * len(steps))
    scratch = [
        pltpu.VMEM((keys, latent), jnp.bfloat16),
        pltpu.VMEM((2, keys, NOPE + LANES), jnp.bfloat16),
        pltpu.VMEM((2, 2, VDIM, keys), jnp.bfloat16),
        pltpu.VMEM((2, 2, keys, 2 * block), jnp.float32),
        pltpu.VMEM((2, 2, keys, 2 * block), jnp.bfloat16),
        pltpu.VMEM((2, 2, 8, 2 * block), jnp.float32),
        pltpu.VMEM((2, 2, 8, 2 * block), jnp.float32),
    ]
    if fresh:
        out_specs = [vmem] * 6
        out_shape = [
            jax.ShapeDtypeStruct((heads * VDIM, 2 * block), jnp.float32),
            jax.ShapeDtypeStruct((heads * 8, 2 * block), jnp.float32),
        ] + [
            jax.ShapeDtypeStruct((a.shape[0], a.shape[1] // 2), jnp.bfloat16)
            for a in (qn, qr, wk, wv)
        ]
        scratch += [
            pltpu.VMEM((2 * block, 2 * block), jnp.float32),
            pltpu.SemaphoreType.DMA((4, heads // 2)),
        ]
    else:
        specs += [vmem, vmem]
        args += state
        out_specs = [pl.BlockSpec(memory_space=pl.ANY), vmem]
        out_shape = [
            jax.ShapeDtypeStruct((block, 2 * heads * VDIM), jnp.bfloat16),
            jax.ShapeDtypeStruct((block, heads * VDIM), jnp.bfloat16),
        ]
        scratch += [
            pltpu.VMEM((block, heads * VDIM), jnp.bfloat16),
            pltpu.SemaphoreType.DMA((heads // 4,)),
        ]
    return pl.pallas_call(
        functools.partial(attend_kernel, steps, fresh),
        in_specs=specs,
        out_specs=out_specs,
        scratch_shapes=scratch,
        out_shape=out_shape,
        compiler_params=pltpu.CompilerParams(vmem_limit_bytes=(36 if len(steps) < 8 else 48) << 20),
        cost_estimate=pl.CostEstimate(
            flops=4 * keys * latent * heads * NOPE + 8 * block * keys * heads * 256,
            bytes_accessed=8 * 1024 * 1024,
            transcendentals=2 * block * keys * heads,
        ),
        name="attend_new" if fresh else "attend_prefix",
    )(*args)


def join_kernel(kept_ref, back_ref, out_ref, sem):
    there = 1 - lax.axis_index("sub")
    half = back_ref.shape[1]
    copy = pltpu.make_async_copy(
        back_ref, out_ref.at[:, pl.ds(pl.multiple_of(there * half, LANES), half)], sem
    )
    copy.start()
    copy.wait()


def join(kept, back):
    return pl.pallas_call(
        join_kernel,
        out_shape=jax.ShapeDtypeStruct(kept.shape, kept.dtype),
        in_specs=[pl.BlockSpec(memory_space=pl.ANY)] * 2,
        out_specs=pl.BlockSpec(memory_space=pl.ANY),
        scratch_shapes=[pltpu.SemaphoreType.DMA(())],
        input_output_aliases={0: 0},
        compiler_params=pltpu.CompilerParams(vmem_limit_bytes=1 << 20),
        name="join",
    )(kept, back)


def shards(
    q_nope,
    q_rope,
    new_latent,
    new_rope,
    pool_latent,
    pool_rope,
    w_uk,
    w_uv,
    block_list,
    prefix_len,
    block_slot,
):
    n = lax.axis_size("req")
    swap = lambda a: lax.ppermute(a, "sub", [(0, 1), (1, 0)])
    cross = lambda a, k: lax.ppermute(a, "req", [(i, i ^ k) for i in range(n)])
    far = list(range(n - 1, 0, -1))
    keep = lambda a: pltpu.with_memory_space_constraint(a, pltpu.HBM)
    q_nope, q_rope, new_latent, w_uk, w_uv = map(keep, (q_nope, q_rope, new_latent, w_uk, w_uv))
    pool_latent = keep(pool_latent)
    slots = keep(block_slot)
    pool_turned = keep(pool_rope.swapaxes(1, 2))
    rope_turned = keep(new_rope.T)
    got = {}
    for k in far:
        got[k] = cross(block_list, k)
    lists = [keep(block_list)] + [got[k] for k in range(1, n)]
    other, pool_latent, pool_turned = prepare(
        new_latent, q_nope, q_rope, rope_turned, pool_latent, pool_turned
    )
    other = swap(other)
    early = n // 2
    sent = {early: pack(n, [early], [lists[early]], slots, pool_latent, pool_turned)[0]}
    kinds = [k for k in range(n) if k != early]
    *rest, where = pack(n, kinds, [lists[k] for k in kinds], slots, pool_latent, pool_turned)
    sent.update(zip(kinds, rest))
    local = swap(sent[0])
    length = prefix_len - lax.broadcasted_iota(jnp.int32, (8, LANES), 1)
    mine = []
    for k in far:
        mine.append(cross(sent[k], k))
    theirs = []
    for k, a in zip(far, mine):
        theirs.append(swap(a))
    common = (new_latent, rope_turned, other)
    wide = (q_nope, q_rope, w_uk, w_uv)
    *state, qn, qr, wk, wv = attend([0], where, length, [sent[0]], [local], *common, *wide, None)
    kept, gone = attend(
        far, where, length, mine, theirs, *common, qn, qr, wk, wv, state
    )
    back = swap(gone)
    return join(kept, back)


def solution(mesh):
    placed = (
        P(("groups", "req", "sub"), "head"),
        P(("groups", "req", "sub"), "head"),
        P(("groups", "req", "sub"), None),
        P(("groups", "req", "sub"), None),
        P(("groups", "req"), None, "sub"),
        P(("groups", "req"), None, None),
        P(None, "head"),
        P(None, "head"),
        P(("groups", "req"), None),
        P(("groups", "req")),
        P("groups"),
    )
    return jax.shard_map(
        shards,
        mesh=mesh,
        in_specs=placed,
        out_specs=P(("groups", "req", "sub"), "head"),
        check_vma=False,
    )
```

```python
import functools
import math

import jax
import jax.numpy as jnp
from jax import lax
from jax.experimental import pallas as pl
from jax.experimental.pallas import tpu as pltpu
from jax.sharding import PartitionSpec as P


NOPE = 128
ROPE = 64
VDIM = 128
CAP = 2
LANES = 128
HIDE = -1e30


def pack_kernel(kinds, own, blocks, pool_local, lists, slots_ref, pool_ref, rope_ref, outs,
                where_ref, index_ref, count_ref, lat_sem, rope_sem):
    me = lax.axis_index("req")
    sub = lax.axis_index("sub")
    block = pool_ref.shape[1]
    width = pool_ref.shape[2]
    for i in range(len(kinds) * CAP):
        index_ref[i] = 0
    if own:
        for i in range(where_ref.shape[0]):
            where_ref[i] = -1
        for i in range(count_ref.shape[0]):
            count_ref[i] = 0
    for i, k in enumerate(kinds):
        found = jnp.int32(0)
        for p in range(blocks):
            physical = slots_ref[lists[i][0, p]]
            owner = physical // pool_local
            mine = owner == me

            @pl.when(mine)
            def _():
                index_ref[i * CAP + found] = physical - owner * pool_local

            found = found + mine.astype(jnp.int32)
            if k == 0:
                step = jnp.bitwise_xor(me, owner)
                earlier = count_ref[step]
                where_ref[step * CAP + earlier] = p
                count_ref[step] = earlier + 1
    parts = width // block
    rows = ROPE // parts
    copies = []
    for i in range(len(kinds)):
        for c in range(CAP):
            copies.append(pltpu.make_async_copy(
                pool_ref.at[index_ref[i * CAP + c]],
                outs[i].at[pl.ds(c * block, block)],
                lat_sem.at[i * CAP + c],
            ))
        for j in range(parts):
            copies.append(pltpu.make_async_copy(
                rope_ref.at[index_ref[i * CAP + sub], pl.ds(j * rows, rows)],
                outs[i].at[pl.ds(CAP * block, rows), pl.ds(j * block, block)],
                rope_sem.at[i * parts + j],
            ))
    for copy in copies:
        copy.start()
    for copy in copies:
        copy.wait()


def pack(n, kinds, lists, block_slot, pool_latent, rope_turned):
    pool_local, block, width = pool_latent.shape
    blocks = lists[0].shape[1]
    rows = CAP * block + block * ROPE // width
    count = len(kinds)
    own = 0 in kinds
    vmem = pl.BlockSpec(memory_space=pltpu.VMEM)
    smem = pl.BlockSpec(memory_space=pltpu.SMEM)

    def body(*refs):
        ins, refs = refs[: count + 3], refs[count + 3 :]
        outs, refs = refs[:count], refs[count:]
        where_ref, refs = (refs[0], refs[1:]) if own else (None, refs)
        pack_kernel(kinds, own, blocks, pool_local, ins[:count], *ins[count:], outs, where_ref, *refs)

    return pl.pallas_call(
        body,
        out_shape=[jax.ShapeDtypeStruct((rows, width), jnp.bfloat16)] * count
        + [jax.ShapeDtypeStruct((n * CAP,), jnp.int32)] * own,
        in_specs=[smem] * (count + 1) + [pl.BlockSpec(memory_space=pl.ANY)] * 2,
        out_specs=[vmem] * count + [smem] * own,
        scratch_shapes=[
            pltpu.SMEM((count * CAP,), jnp.int32),
            pltpu.SMEM((n,), jnp.int32),
            pltpu.SemaphoreType.DMA((count * CAP,)),
            pltpu.SemaphoreType.DMA((count * width // block,)),
        ],
        compiler_params=pltpu.CompilerParams(vmem_limit_bytes=16 << 20),
        cost_estimate=pl.CostEstimate(
            flops=0, bytes_accessed=4 * count * rows * width, transcendentals=0
        ),
        name="pack",
    )(*lists, block_slot, pool_latent, rope_turned)


def half_of(ref, which):
    half = ref.shape[1] // 2
    return ref.at[:, pl.ds(pl.multiple_of(which * half, LANES), half)]


def move(moves, sem):
    copies = [pltpu.make_async_copy(*pair, sem.at[i]) for i, pair in enumerate(moves)]
    for copy in copies:
        copy.start()
    for copy in copies:
        copy.wait()


def prepare_kernel(lat_ref, qn_ref, qr_ref, rope_ref, pool_ref, pool_rope_ref,
                   out_ref, pool_out, pool_rope_out, sem):
    there = 1 - lax.axis_index("sub")
    latent = lat_ref.shape[1]
    half = qn_ref.shape[1] // 2
    rope_half = qr_ref.shape[1] // 2
    tail = latent + half + rope_half
    move(
        [
            (lat_ref, out_ref.at[:, pl.ds(0, latent)]),
            (half_of(qn_ref, there), out_ref.at[:, pl.ds(latent, half)]),
            (half_of(qr_ref, there), out_ref.at[:, pl.ds(latent + half, rope_half)]),
            (rope_ref, out_ref.at[pl.ds(0, ROPE), pl.ds(tail, rope_ref.shape[1])]),
            (pool_ref, pool_out),
            (pool_rope_ref, pool_rope_out),
        ],
        sem,
    )


def gather_call(kernel, args, shapes):
    return pl.pallas_call(
        kernel,
        out_shape=[jax.ShapeDtypeStruct(shape, jnp.bfloat16) for shape in shapes],
        in_specs=[pl.BlockSpec(memory_space=pl.ANY)] * len(args),
        out_specs=[pl.BlockSpec(memory_space=pltpu.VMEM)] * len(shapes),
        scratch_shapes=[pltpu.SemaphoreType.DMA((len(args),))],
        compiler_params=pltpu.CompilerParams(vmem_limit_bytes=16 << 20),
        cost_estimate=pl.CostEstimate(
            flops=0, bytes_accessed=4 * sum(math.prod(shape) for shape in shapes), transcendentals=0
        ),
    )(*args)


def prepare(new_latent, q_nope, q_rope, rope_turned, pool_latent, pool_turned):
    rows, latent = new_latent.shape
    width = latent + q_nope.shape[1] // 2 + q_rope.shape[1] // 2 + rows
    args = (new_latent, q_nope, q_rope, rope_turned, pool_latent, pool_turned)
    shapes = [(rows, width), pool_latent.shape, pool_turned.shape]
    return gather_call(prepare_kernel, args, shapes)


RATE = math.log2(math.e) / math.sqrt(NOPE + ROPE)


def attend_kernel(steps, fresh, *refs):
    count = len(steps)
    where_ref, len_ref, lat_a, rope_a, other, qn_ref, qr_ref, wk_ref, wv_ref, *refs = refs
    mine = refs[:count]
    theirs = refs[count : 2 * count]
    refs = refs[2 * count :]
    if fresh:
        wide = (qn_ref, qr_ref, wk_ref, wv_ref)
        (acc_ref, stat_ref, qn_ref, qr_ref, wk_ref, wv_ref,
         lat, kc, vt, score, weight, peak, norms, bias, sem) = refs
    else:
        (acc_ref, stat_ref, out_ref, send_ref, lat, kc, vt, score, weight, peak, norms, result,
         sem) = refs
    sub = lax.axis_index("sub")
    block, latent = lat_a.shape
    chunk = CAP * block
    first = chunk if fresh else 0
    queries = 2 * block
    keys = lat.shape[0]
    half = qn_ref.shape[1]
    halves = half // (4 * NOPE)
    nope_at = latent
    rope_at = nope_at + half
    tail_at = rope_at + qr_ref.shape[1]
    head = lambda j: slice(j * LANES, (j + 1) * LANES)
    at = lambda start, size: pl.ds(pl.multiple_of(start, size), size)

    def fetch(pair):
        copies = []
        for i, (ref, out) in enumerate(zip(wide, (qn_ref, qr_ref, wk_ref, wv_ref))):
            span = out.shape[1]
            size = span * 2 * NOPE // half
            copies.append(pltpu.make_async_copy(
                ref.at[:, at(sub * span + pair * size, size)],
                out.at[:, at(pair * size, size)],
                sem.at[i, pair],
            ))
        return copies

    def send_for(pair):
        if fresh:
            for copy in fetch(pair):
                copy.start()

    def arrive(pair):
        if fresh:
            for copy in fetch(pair):
                copy.wait()

    def build():
        def put_tails(base, rope, mask):
            kc[0, base : base + block, NOPE:] = jnp.concatenate([rope, mask], axis=1)
            kc[1, base : base + block, NOPE:] = jnp.concatenate([mask, rope], axis=1)

        lane = lax.broadcasted_iota(jnp.int32, (block, ROPE), 1)
        row = lax.broadcasted_iota(jnp.int32, (block, ROPE), 0)
        length = jnp.broadcast_to(len_ref[:1, :ROPE], (block, ROPE)) + lane
        for i, k in enumerate(steps):
            width = mine[i].shape[1]
            here = pl.multiple_of(sub * width, width)
            there = pl.multiple_of((1 - sub) * width, width)
            base = first + i * chunk
            lat[base : base + chunk, pl.ds(here, width)] = mine[i][:chunk, :]
            lat[base : base + chunk, pl.ds(there, width)] = theirs[i][:chunk, :]
            for c in range(CAP):
                packed = jnp.where(sub == c, mine[i][chunk:, :], theirs[i][chunk:, :])
                rope = jnp.concatenate(
                    [packed[:, j * block : (j + 1) * block] for j in range(width // block)], axis=0
                )
                p = where_ref[k * CAP + c]
                hidden = (lane == 0) & ((p < 0) | (p * block + row >= length))
                put_tails(
                    base + c * block, rope.T, jnp.where(hidden, HIDE, 0.0).astype(jnp.bfloat16)
                )
        if fresh:
            plain = jnp.zeros((block, ROPE), jnp.bfloat16)
            lat[:block, :] = lat_a[...]
            lat[block:chunk, :] = other[:, :latent]
            put_tails(0, rope_a[...].T, plain)
            put_tails(block, other[:ROPE, tail_at:].T, plain)
            i = lax.broadcasted_iota(jnp.int32, (queries, queries), 0)
            j = lax.broadcasted_iota(jnp.int32, (queries, queries), 1)
            flip = sub * block
            seen = jnp.bitwise_xor(i, flip) <= jnp.bitwise_xor(j, flip)
            bias[...] = jnp.where(seen, 0.0, HIDE)

    def form_keys(pair):
        columns = at(pair * 2 * NOPE, 2 * NOPE)
        for r in range(0, keys, chunk):
            rows = slice(r, r + chunk)
            k2 = jnp.dot(lat[rows, :], wk_ref[:, columns], preferred_element_type=jnp.float32)
            for j in range(2):
                kc[j, rows, :NOPE] = k2[:, head(j)].astype(jnp.bfloat16)

    def form_values(pair, slot):
        v2 = lax.dot_general(
            wv_ref[:, at(pair * 2 * VDIM, 2 * VDIM)], lat[...], (((0,), (1,)), ((), ())),
            preferred_element_type=jnp.float32,
        )
        for j in range(2):
            vt[slot, j] = v2[j * VDIM : (j + 1) * VDIM].astype(jnp.bfloat16)

    def form_scores(pair, slot, j):
        lane = lax.broadcasted_iota(jnp.int32, (queries, LANES), 1)
        nope = pair * 2 * NOPE + j * NOPE
        qn = jnp.concatenate(
            [qn_ref[:, at(nope, NOPE)], other[:, at(nope_at + nope, NOPE)]], axis=0
        )
        rope = pair * LANES
        qr = jnp.concatenate(
            [qr_ref[:, at(rope, LANES)], other[:, at(rope_at + rope, LANES)]], axis=0
        )
        fill = jnp.where(lane == (1 - j) * ROPE, 1.0, 0.0).astype(jnp.bfloat16)
        own = (lane >= ROPE) if j else (lane < ROPE)
        qc = jnp.concatenate([qn, jnp.where(own, qr, fill)], axis=1)
        s = lax.dot_general(
            kc[j], qc, (((1,), (1,)), ((), ())), preferred_element_type=jnp.float32
        )
        if fresh:
            s = jnp.concatenate([s[:queries] + bias[...], s[queries:]], axis=0)
        score[slot, j] = s
        most = jnp.max(s, axis=0, keepdims=True)
        peak[slot, j] = jnp.broadcast_to(most, (8, queries))

    def form_weights(pair, slot, j):
        most = peak[slot, j, :1, :]
        if not fresh:
            most = jnp.maximum(most, stat_ref[at((2 * pair + j) * 8, 8), :][:1])
        e = jnp.exp2((score[slot, j] - most) * RATE)
        norms[slot, j] = jnp.broadcast_to(jnp.sum(e, axis=0, keepdims=True), (8, queries))
        weight[slot, j] = e.astype(jnp.bfloat16)

    def form_output(pair, slot, j):
        o = jnp.dot(vt[slot, j], weight[slot, j], preferred_element_type=jnp.float32)
        norm = norms[slot, j, :1, :]
        rows = at((2 * pair + j) * VDIM, VDIM)
        stat_rows = at((2 * pair + j) * 8, 8)
        if fresh:
            acc_ref[rows, :] = o
            row = lax.broadcasted_iota(jnp.int32, (8, queries), 0)
            stat_ref[stat_rows, :] = jnp.where(row == 0, peak[slot, j], norm)
        else:
            stat = stat_ref[stat_rows, :]
            old = stat[:1]
            most = jnp.maximum(peak[slot, j, :1, :], old)
            keep = jnp.exp2((old - most) * RATE)
            norm = norm + keep * stat[1:2]
            o = (o + keep * acc_ref[rows, :]) / norm
            o = o.T.astype(jnp.bfloat16)
            columns = at((2 * pair + j) * VDIM, VDIM)
            result[:, columns] = o[:block]
            send_ref[:, columns] = o[block:]

    def both(pair, slot, more=True, ahead=True):
        if ahead:
            send_for(pair + 2)
        form_weights(pair, slot, 0)
        form_weights(pair, slot, 1)
        if more:
            arrive(pair + 1)
            form_keys(pair + 1)
            form_values(pair + 1, 1 - slot)
        for j in range(2):
            if not fresh:
                form_output(pair, slot, j)
            if more:
                form_scores(pair + 1, 1 - slot, j)
            if fresh:
                form_output(pair, slot, j)

    def deliver(t):
        width = 4 * VDIM
        return pltpu.make_async_copy(
            result.at[:, at(t * width, width)],
            out_ref.at[:, at(sub * half + t * width, width)],
            sem.at[t],
        )

    send_for(0)
    send_for(1)
    build()
    arrive(0)
    form_keys(0)
    form_values(0, 0)
    for j in range(2):
        form_scores(0, 0, j)

    def body(t, carry):
        both(2 * t, 0)
        both(2 * t + 1, 1)
        if not fresh:
            deliver(t).start()
        return carry

    if halves > 1:
        lax.fori_loop(0, halves - 1, body, 0)
    both(2 * halves - 2, 0, ahead=False)
    both(2 * halves - 1, 1, more=False, ahead=False)
    if not fresh:
        deliver(halves - 1).start()
        for t in range(halves):
            deliver(t).wait()


def attend(steps, where, length, mine, theirs, new_latent, rope_turned, other, qn, qr, wk, wv, state):
    fresh = state is None
    block, latent = new_latent.shape
    heads = wk.shape[1] // NOPE // (2 if fresh else 1)
    keys = (len(steps) + (1 if fresh else 0)) * CAP * block
    vmem = pl.BlockSpec(memory_space=pltpu.VMEM)
    args = [where, length, new_latent, rope_turned, other, qn, qr, wk, wv, *mine, *theirs]
    place = pl.BlockSpec(memory_space=pl.ANY) if fresh else vmem
    specs = [pl.BlockSpec(memory_space=pltpu.SMEM)] + [vmem] * 4 + [place] * 4
    specs += [vmem] * (2 * len(steps))
    scratch = [
        pltpu.VMEM((keys, latent), jnp.bfloat16),
        pltpu.VMEM((2, keys, NOPE + LANES), jnp.bfloat16),
        pltpu.VMEM((2, 2, VDIM, keys), jnp.bfloat16),
        pltpu.VMEM((2, 2, keys, 2 * block), jnp.float32),
        pltpu.VMEM((2, 2, keys, 2 * block), jnp.bfloat16),
        pltpu.VMEM((2, 2, 8, 2 * block), jnp.float32),
        pltpu.VMEM((2, 2, 8, 2 * block), jnp.float32),
    ]
    if fresh:
        out_specs = [vmem] * 6
        out_shape = [
            jax.ShapeDtypeStruct((heads * VDIM, 2 * block), jnp.float32),
            jax.ShapeDtypeStruct((heads * 8, 2 * block), jnp.float32),
        ] + [
            jax.ShapeDtypeStruct((a.shape[0], a.shape[1] // 2), jnp.bfloat16)
            for a in (qn, qr, wk, wv)
        ]
        scratch += [
            pltpu.VMEM((2 * block, 2 * block), jnp.float32),
            pltpu.SemaphoreType.DMA((4, heads // 2)),
        ]
    else:
        specs += [vmem, vmem]
        args += state
        out_specs = [pl.BlockSpec(memory_space=pl.ANY), vmem]
        out_shape = [
            jax.ShapeDtypeStruct((block, 2 * heads * VDIM), jnp.bfloat16),
            jax.ShapeDtypeStruct((block, heads * VDIM), jnp.bfloat16),
        ]
        scratch += [
            pltpu.VMEM((block, heads * VDIM), jnp.bfloat16),
            pltpu.SemaphoreType.DMA((heads // 4,)),
        ]
    return pl.pallas_call(
        functools.partial(attend_kernel, steps, fresh),
        in_specs=specs,
        out_specs=out_specs,
        scratch_shapes=scratch,
        out_shape=out_shape,
        compiler_params=pltpu.CompilerParams(vmem_limit_bytes=(36 if len(steps) < 8 else 48) << 20),
        cost_estimate=pl.CostEstimate(
            flops=4 * keys * latent * heads * NOPE + 8 * block * keys * heads * 256,
            bytes_accessed=8 * 1024 * 1024,
            transcendentals=2 * block * keys * heads,
        ),
        name="attend_new" if fresh else "attend_prefix",
    )(*args)


def join_kernel(kept_ref, back_ref, out_ref, sem):
    there = 1 - lax.axis_index("sub")
    half = back_ref.shape[1]
    copy = pltpu.make_async_copy(
        back_ref, out_ref.at[:, pl.ds(pl.multiple_of(there * half, LANES), half)], sem
    )
    copy.start()
    copy.wait()


def join(kept, back):
    return pl.pallas_call(
        join_kernel,
        out_shape=jax.ShapeDtypeStruct(kept.shape, kept.dtype),
        in_specs=[pl.BlockSpec(memory_space=pl.ANY)] * 2,
        out_specs=pl.BlockSpec(memory_space=pl.ANY),
        scratch_shapes=[pltpu.SemaphoreType.DMA(())],
        input_output_aliases={0: 0},
        compiler_params=pltpu.CompilerParams(vmem_limit_bytes=1 << 20),
        name="join",
    )(kept, back)


def shards(
    q_nope,
    q_rope,
    new_latent,
    new_rope,
    pool_latent,
    pool_rope,
    w_uk,
    w_uv,
    block_list,
    prefix_len,
    block_slot,
):
    n = lax.axis_size("req")
    swap = lambda a: lax.ppermute(a, "sub", [(0, 1), (1, 0)])
    cross = lambda a, k: lax.ppermute(a, "req", [(i, i ^ k) for i in range(n)])
    far = list(range(n - 1, 0, -1))
    keep = lambda a: pltpu.with_memory_space_constraint(a, pltpu.HBM)
    q_nope, q_rope, new_latent, w_uk, w_uv = map(keep, (q_nope, q_rope, new_latent, w_uk, w_uv))
    pool_latent = keep(pool_latent)
    slots = keep(block_slot)
    pool_turned = keep(pool_rope.swapaxes(1, 2))
    rope_turned = keep(new_rope.T)
    got = {}
    for k in far:
        got[k] = cross(block_list, k)
    lists = [keep(block_list)] + [got[k] for k in range(1, n)]
    other, pool_latent, pool_turned = prepare(
        new_latent, q_nope, q_rope, rope_turned, pool_latent, pool_turned
    )
    other = swap(other)
    early = n // 2
    sent = {early: pack(n, [early], [lists[early]], slots, pool_latent, pool_turned)[0]}
    kinds = [k for k in range(n) if k != early]
    *rest, where = pack(n, kinds, [lists[k] for k in kinds], slots, pool_latent, pool_turned)
    sent.update(zip(kinds, rest))
    local = swap(sent[0])
    length = prefix_len - lax.broadcasted_iota(jnp.int32, (8, LANES), 1)
    mine = []
    for k in far:
        mine.append(cross(sent[k], k))
    theirs = []
    for k, a in zip(far, mine):
        theirs.append(swap(a))
    common = (new_latent, rope_turned, other)
    wide = (q_nope, q_rope, w_uk, w_uv)
    *state, qn, qr, wk, wv = attend([0], where, length, [sent[0]], [local], *common, *wide, None)
    kept, gone = attend(
        far, where, length, mine, theirs, *common, qn, qr, wk, wv, state
    )
    back = swap(gone)
    return join(kept, back)


def solution(mesh):
    placed = (
        P(("groups", "req", "sub"), "head"),
        P(("groups", "req", "sub"), "head"),
        P(("groups", "req", "sub"), None),
        P(("groups", "req", "sub"), None),
        P(("groups", "req"), None, "sub"),
        P(("groups", "req"), None, None),
        P(None, "head"),
        P(None, "head"),
        P(("groups", "req"), None),
        P(("groups", "req")),
        P("groups"),
    )
    return jax.shard_map(
        shards,
        mesh=mesh,
        in_specs=placed,
        out_specs=P(("groups", "req", "sub"), "head"),
        check_vma=False,
    )
```
